128 devices in a mesh: ctx: 32 (over z, x, core), exp: 4 (over y).
Axes of the slice: x: 4, y: 4, z: 4, core: 2. Of those that a mesh axis runs over, the one named last changes fastest.
Arguments:
- queries: bfloat16 [8192, 4096], P('ctx', 'exp'), may hold values from -6 to 6
- key_rows: bfloat16 [8192, 4096], P('ctx', 'exp'), may hold values from -6 to 6
- value_rows: bfloat16 [8192, 4096], P('ctx', 'exp'), may hold values from -6 to 6
- gate_rows: bfloat16 [8192, 4096], P('ctx', 'exp'), may hold values from -6 to 6
- decay_exp: int32 [32], P('exp'), may hold values from 5 to 16
- attn_gain: float32 [4096], P('exp'), may hold values from 0.1 to 1.9
- out_proj: bfloat16 [4096, 6144], P('exp'), may hold values from -0.09375 to 0.09375
- residual: bfloat16 [8192, 6144], P(('ctx', 'exp')), may hold values from -6 to 6
- norm_gain: float32 [6144], replicated, may hold values from 0.1 to 1.9
- routes: int32 [8192, 2], P('ctx'), may hold values from 0 to 31, as said below
- route_weights: float32 [8192, 2], P('ctx'), may hold values from 0.1 to 1
- w_gate: bfloat16 [4, 9216, 6144], P('exp', 'ctx'), may hold values from -0.078125 to 0.078125
- w_up: bfloat16 [4, 9216, 6144], P('exp', 'ctx'), may hold values from -0.078125 to 0.078125
- w_down: bfloat16 [4, 9216, 6144], P('exp', 'ctx'), may hold values from -0.0625 to 0.0625
Outputs:
- layer_out: bfloat16 [8192, 6144], P(('ctx', 'exp'))
The draws below stay inside these ranges and needn't reach their ends.
Inputs may be any that keep to these rules, and one draw needn't show every extreme that they name: `routes`: A row's two entries differ. An expert e below 4 is named only in column e % 2. In every aligned block of 64 rows each expert below 4 is named at most 8 times, and some expert below 4 exactly 8 times.
All inputs are finite; a program needn't handle non-finite values.
Results may differ from the reference program's by a relative error of at most 0.018.
Values may be sent and summed in bfloat16 or wider, within the bound.
A program may use at most 128 MiB of HBM per device.

```python
import jax
import jax.numpy as jnp
from jax import lax

D = 6144
HEADS = 32
HEAD = 128
FF = 9216
EXPERTS = 32
C = 256
L = 8192
RESIDENT = 4
CAPQ = 8
CAPE = 32
SLOTS = 1024
FFD = 288
N_CTX = 32
N_EXP = 4


def draw_routes(key, part):
    total_rows = C * N_CTX
    block_rows = C // N_EXP
    block_count = total_rows // block_rows
    resident = N_EXP
    key_list = jax.random.split(key, 8)
    owners = jnp.arange(resident, dtype=jnp.int32)
    favored = jax.random.randint(key_list[0], (), 0, resident)
    heavy = jax.random.randint(key_list[1], (block_count, resident), CAPQ // 2, CAPQ + 1)
    light = jax.random.randint(key_list[2], (block_count, resident), 0, CAPQ // 4 + 1)
    counts = jnp.where(owners[None, :] == favored, heavy, light)
    forced = jax.random.randint(key_list[3], (block_count,), 0, resident)
    counts = jnp.where(owners[None, :] == forced[:, None], CAPQ, counts)
    parity = owners % 2
    earlier = ((owners[:, None] < owners[None, :]) & (parity[:, None] == parity[None, :])).astype(jnp.int32)
    starts = jnp.sum(counts[:, :, None] * earlier[None], axis=1)
    chosen_list = []
    present_list = []
    for column_id in range(2):
        perm_keys = jax.random.split(key_list[4 + column_id], block_count)
        places = jax.vmap(lambda single: jax.random.permutation(single, block_rows))(perm_keys)
        inside = (places[:, :, None] >= starts[:, None, :]) & (places[:, :, None] < starts[:, None, :] + counts[:, None, :]) & (parity[None, None, :] == column_id)
        hits = inside.astype(jnp.int32)
        chosen_list.append(jnp.sum(hits * owners[None, None, :], axis=2))
        present_list.append(jnp.sum(hits, axis=2) > 0)
    spread = EXPERTS - resident
    first_free = jax.random.randint(key_list[6], (block_count, block_rows), 0, spread)
    step_free = jax.random.randint(key_list[7], (block_count, block_rows), 1, spread)
    free_zero = resident + first_free
    free_one = resident + (first_free + step_free) % spread
    pick_zero = jnp.where(present_list[0], chosen_list[0], free_zero)
    pick_one = jnp.where(present_list[1], chosen_list[1], free_one)
    return jnp.stack([pick_zero, pick_one], axis=-1).reshape(total_rows, 2).astype(jnp.int32)


def plant(array, key, least, high):
    dims = array.shape
    spot = [jax.random.randint(jax.random.fold_in(key, axis), (), 0, dims[axis]) for axis in range(len(dims))]
    array = array.at[tuple(spot)].set(least)
    longest = dims.index(max(dims))
    spot[longest] = (spot[longest] + 1) % dims[longest]
    return array.at[tuple(spot)].set(high)


def level_of(own_key, extent, shards, smallest, top_value):
    loudness, own = 1.0, jax.random.fold_in(own_key, 6)
    for dim, parts in shards:
        draws = jnp.exp(jax.random.uniform(jax.random.fold_in(own, dim), (parts,), jnp.float32, smallest / len(shards), top_value / len(shards)))
        loudness = loudness * jnp.repeat(draws, extent[dim] // parts).reshape([-1 if axis == dim else 1 for axis in range(len(extent))])
    return loudness


def gaussian(rng, extent, width, limit, cuts=(), kind=jnp.bfloat16):
    entries = width * jax.random.normal(rng, extent, jnp.float32)
    if cuts:
        entries = entries * level_of(rng, extent, cuts, -0.22, 0.18)
    return jnp.clip(entries, -limit, limit).astype(kind)


def setup_inputs(seed: int = 0) -> dict:
    arg_keys = jax.random.split(jax.random.key(seed), 15)
    return {
        "queries": gaussian(arg_keys[0], (L, HEADS * HEAD), 1.0, 6.0, ((0, 32), (1, 4))),
        "key_rows": gaussian(arg_keys[1], (L, HEADS * HEAD), 1.0, 6.0, ((0, 32), (1, 4))),
        "value_rows": gaussian(arg_keys[2], (L, HEADS * HEAD), 1.0, 6.0, ((0, 32), (1, 4))),
        "gate_rows": gaussian(arg_keys[3], (L, HEADS * HEAD), 1.0, 6.0, ((0, 32), (1, 4))),
        "decay_exp": plant(jax.random.randint(arg_keys[4], (HEADS,), 5, 17), jax.random.fold_in(arg_keys[4], 1), 5, 16).astype(jnp.int32),
        "attn_gain": jnp.clip(1.0 + 0.18 * jax.random.normal(arg_keys[5], (HEADS * HEAD,), jnp.float32), 0.1, 1.9),
        "out_proj": gaussian(arg_keys[6], (HEADS * HEAD, D), (HEADS * HEAD) ** -0.5, 0.09375, ((0, 4),)),
        "residual": gaussian(arg_keys[7], (L, D), 1.0, 6.0, ((0, 128),)),
        "norm_gain": jnp.clip(1.0 + 0.18 * jax.random.normal(arg_keys[8], (D,), jnp.float32), 0.1, 1.9),
        "routes": draw_routes(jax.random.fold_in(arg_keys[14], 71), 0),
        "route_weights": jnp.clip(0.1 + 0.9 * jax.random.uniform(arg_keys[10], (L, 2), jnp.float32) ** level_of(arg_keys[10], (L, 2), ((0, 32),), -0.2, 0.2), 0.1, 1.0),
        "w_gate": gaussian(arg_keys[11], (RESIDENT, FF, D), D ** -0.5, 0.078125, ((0, 4), (1, 32))),
        "w_up": gaussian(arg_keys[12], (RESIDENT, FF, D), D ** -0.5, 0.078125, ((0, 4), (1, 32))),
        "w_down": gaussian(arg_keys[13], (RESIDENT, FF, D), FF ** -0.5, 0.0625, ((0, 4), (1, 32))),
    }


EPSILON = 1e-06

def expert_part(slot_rows, gate_cols, up_cols, down_rows):
    contract_dims = (((1,), (1,)), ((), ()))
    first_half = lax.dot_general(slot_rows, gate_cols, contract_dims, preferred_element_type=jnp.float32)
    second_half = lax.dot_general(slot_rows, up_cols, contract_dims, preferred_element_type=jnp.float32)
    activated = (jax.nn.silu(first_half) * second_half).astype(jnp.bfloat16)
    return jnp.dot(activated, down_rows, preferred_element_type=jnp.float32)

def reference(queries, key_rows, value_rows, gate_rows, decay_exp, attn_gain, out_proj, residual, norm_gain, routes, route_weights, w_gate, w_up, w_down):
    decay_rates = jnp.exp2(-decay_exp.astype(jnp.float32))
    positions = jnp.arange(C, dtype=jnp.float32)
    offsets = positions[:, None] - positions[None, :]
    damping = jnp.where(offsets[None] >= 0.0, jnp.exp(-decay_rates[:, None, None] * jnp.maximum(offsets, 0.0)[None]), 0.0)
    tail_decay = jnp.exp(-decay_rates[None, :] * (C - 1.0 - positions)[:, None])
    lead_decay = jnp.exp(-decay_rates[None, :] * (positions + 1.0)[:, None])
    carry_decay = jnp.exp(-decay_rates * C)
    gain_heads = attn_gain.reshape(HEADS, HEAD)

    def span_step(carried_state, inputs):
        query_block, key_block, value_block, gate_block = inputs
        query_full = query_block.reshape(C, HEADS, HEAD).astype(jnp.float32)
        key_full = key_block.reshape(C, HEADS, HEAD).astype(jnp.float32)
        value_full = value_block.reshape(C, HEADS, HEAD).astype(jnp.float32)
        scores = jnp.einsum('thd,shd->hts', query_full, key_full)
        mixing = lax.optimization_barrier((scores * damping).astype(jnp.bfloat16))
        inner_part = jnp.einsum('hts,shd->thd', mixing.astype(jnp.float32), value_full)
        outer_part = jnp.einsum('thd,hde->the', query_full * lead_decay[:, :, None], carried_state, precision=lax.Precision.HIGHEST)
        keyed_rows = lax.optimization_barrier((key_full * tail_decay[:, :, None]).astype(jnp.bfloat16))
        update = jnp.einsum('shd,she->hde', keyed_rows.astype(jnp.float32), value_full)
        mixed_heads = inner_part + outer_part
        mean_square = lax.optimization_barrier(jnp.mean(mixed_heads * mixed_heads, axis=2, keepdims=True))
        normed_heads = mixed_heads * lax.rsqrt(mean_square + EPSILON)
        gate_full = gate_block.reshape(C, HEADS, HEAD).astype(jnp.float32)
        settled = (normed_heads * gain_heads * jax.nn.sigmoid(gate_full)).astype(jnp.bfloat16)
        return (carry_decay[:, None, None] * carried_state + update, settled.reshape(C, HEADS * HEAD))
    block_inputs = (queries.reshape(N_CTX, C, HEADS * HEAD), key_rows.reshape(N_CTX, C, HEADS * HEAD), value_rows.reshape(N_CTX, C, HEADS * HEAD), gate_rows.reshape(N_CTX, C, HEADS * HEAD))
    initial_state = jnp.zeros((HEADS, HEAD, HEAD), jnp.float32)
    final_state, settled_blocks = lax.scan(span_step, initial_state, block_inputs)
    settled_all = settled_blocks.reshape(L, HEADS * HEAD)
    hidden = residual.astype(jnp.float32) + jnp.dot(settled_all, out_proj, preferred_element_type=jnp.float32)
    mean_square = lax.optimization_barrier(jnp.mean(hidden * hidden, axis=1, keepdims=True))
    normed = (hidden * lax.rsqrt(mean_square + EPSILON) * norm_gain).astype(jnp.bfloat16)
    block_of = jnp.arange(L, dtype=jnp.int32) // C
    mixture = jnp.zeros((L, D), jnp.float32)
    for expert_id in range(N_EXP):
        column = expert_id % 2
        picked = routes[:, column] == expert_id
        slot_rank = (jnp.cumsum(picked.reshape(N_CTX, C).astype(jnp.int32), axis=1) - 1).reshape(L).astype(jnp.int32)
        target = jnp.where(picked, block_of * CAPE + slot_rank, SLOTS).astype(jnp.int32)
        buffer_rows = jnp.zeros((SLOTS, D), jnp.bfloat16).at[target].set(normed, mode='drop')
        gate_all = w_gate[expert_id]
        up_all = w_up[expert_id]
        down_all = w_down[expert_id]

        def slice_step(slice_id, running_sum):
            first_unit = (slice_id * FFD).astype(jnp.int32)
            part_term = expert_part(buffer_rows, lax.dynamic_slice_in_dim(gate_all, first_unit, FFD, 0), lax.dynamic_slice_in_dim(up_all, first_unit, FFD, 0), lax.dynamic_slice_in_dim(down_all, first_unit, FFD, 0))
            rounded = lax.optimization_barrier(part_term.astype(jnp.bfloat16))
            return running_sum + rounded.astype(jnp.float32)
        produced = lax.fori_loop(0, N_CTX, slice_step, jnp.zeros((SLOTS, D), jnp.float32))
        fetched = produced[jnp.minimum(target, SLOTS - 1)]
        mixture = mixture + jnp.where(picked[:, None], route_weights[:, column][:, None] * fetched, 0.0)
    return (hidden + mixture).astype(jnp.bfloat16)
```

```python
import jax
import jax.numpy as jnp
from jax import lax
from jax.sharding import PartitionSpec as P

EPSILON = 1e-06


def earlier_states(update, decay_rates, row_count):
    size, index = (lax.axis_size("ctx"), lax.axis_index("ctx"))
    everything = lax.all_gather(update.astype(jnp.bfloat16), "ctx").astype(jnp.float32)
    distance = (index - 1 - jnp.arange(size)).astype(jnp.float32)
    factors = jnp.where(
        distance[:, None] >= 0.0,
        jnp.exp(-decay_rates[None, :] * row_count * jnp.maximum(distance, 0.0)[:, None]),
        0.0,
    )
    return jnp.sum(everything * factors[:, :, None, None], axis=0)


def span_local(queries, key_rows, value_rows, decay_exp):
    row_count = queries.shape[0]
    head_count = decay_exp.shape[0]
    head_width = queries.shape[1] // head_count
    query_heads = queries.reshape(row_count, head_count, head_width)
    key_heads = key_rows.reshape(row_count, head_count, head_width)
    value_heads = value_rows.reshape(row_count, head_count, head_width)
    decay_rates = jnp.exp2(-decay_exp.astype(jnp.float32))
    positions = jnp.arange(row_count, dtype=jnp.float32)
    offsets = positions[:, None] - positions[None, :]
    damping = jnp.where(
        offsets[None] >= 0.0,
        jnp.exp(-decay_rates[:, None, None] * jnp.maximum(offsets, 0.0)[None]),
        0.0,
    )
    scores = jnp.einsum("thd,shd->hts", query_heads, key_heads, preferred_element_type=jnp.float32)
    mixing = (scores * damping).astype(jnp.bfloat16)
    inner_part = jnp.einsum("hts,shd->thd", mixing, value_heads, preferred_element_type=jnp.float32)
    tail_decay = jnp.exp(-decay_rates[None, :] * (row_count - 1.0 - positions)[:, None])
    keyed_rows = (key_heads.astype(jnp.float32) * tail_decay[:, :, None]).astype(jnp.bfloat16)
    update = jnp.einsum("shd,she->hde", keyed_rows, value_heads, preferred_element_type=jnp.float32)
    lead_decay = jnp.exp(-decay_rates[None, :] * (positions + 1.0)[:, None])
    leading = query_heads.astype(jnp.float32) * lead_decay[:, :, None]
    return (inner_part, leading, update, decay_rates)


def settle(inner_part, leading, prior_state, gate_rows, attn_gain):
    outer_part = jnp.einsum("thd,hde->the", leading, prior_state, precision=lax.Precision.HIGHEST)
    mixed_heads = inner_part + outer_part
    row_count, head_count, head_width = mixed_heads.shape
    mean_square = jnp.mean(mixed_heads * mixed_heads, axis=2, keepdims=True)
    normed_heads = mixed_heads * lax.rsqrt(mean_square + EPSILON)
    gain_heads = attn_gain.reshape(head_count, head_width)
    gate_heads = gate_rows.reshape(row_count, head_count, head_width).astype(jnp.float32)
    settled = (normed_heads * gain_heads * jax.nn.sigmoid(gate_heads)).astype(jnp.bfloat16)
    return settled.reshape(row_count, head_count * head_width)


def token_norm(hidden, norm_gain):
    mean_square = jnp.mean(hidden * hidden, axis=1, keepdims=True)
    return (hidden * lax.rsqrt(mean_square + EPSILON) * norm_gain).astype(jnp.bfloat16)


def slot_table(chosen_ids, expert_count, capacity):
    owners = jnp.arange(expert_count, dtype=jnp.int32)
    chosen = jnp.where(owners[:, None] % 2 == 0, chosen_ids[None, :, 0], chosen_ids[None, :, 1])
    picked = chosen == owners[:, None]
    row_count = chosen_ids.shape[0]
    upto = jnp.arange(row_count)[:, None] <= jnp.arange(row_count)[None, :]
    slot_rank = jnp.dot(picked.astype(jnp.float32), upto.astype(jnp.float32)) - 1.0
    slot_ids = jnp.arange(capacity, dtype=jnp.float32)
    return picked[:, None, :] & (slot_rank[:, None, :] == slot_ids[None, :, None])


def expert_part(slot_rows, gate_cols, up_cols, down_rows):
    contract_dims = (((1,), (1,)), ((), ()))
    first_half = lax.dot_general(
        slot_rows, gate_cols, contract_dims, preferred_element_type=jnp.float32
    )
    second_half = lax.dot_general(
        slot_rows, up_cols, contract_dims, preferred_element_type=jnp.float32
    )
    activated = (jax.nn.silu(first_half) * second_half).astype(jnp.bfloat16)
    return jnp.dot(activated, down_rows, preferred_element_type=jnp.float32)


def body(
    queries,
    key_rows,
    value_rows,
    gate_rows,
    decay_exp,
    attn_gain,
    out_proj,
    residual,
    norm_gain,
    routes,
    route_weights,
    w_gate,
    w_up,
    w_down,
):
    inner_part, leading, update, decay_rates = span_local(
        queries, key_rows, value_rows, decay_exp
    )
    span_rows = queries.shape[0]
    prior_state = earlier_states(update, decay_rates, span_rows)
    settled = settle(inner_part, leading, prior_state, gate_rows, attn_gain)
    group_count = lax.axis_size("exp")
    group_rows = span_rows // group_count
    first_mine = lax.axis_index("exp") * group_rows
    capacity = group_rows // 8
    projected = jnp.dot(settled, out_proj, preferred_element_type=jnp.float32)
    summed = lax.psum_scatter(
        projected.astype(jnp.bfloat16), "exp", scatter_dimension=0, tiled=True
    ).astype(jnp.float32)
    hidden = summed + residual.astype(jnp.float32)
    normed = token_norm(hidden, norm_gain)
    my_routes = lax.dynamic_slice_in_dim(routes, first_mine, group_rows, 0)
    my_weights = lax.dynamic_slice_in_dim(route_weights, first_mine, group_rows, 0)
    table = slot_table(my_routes, group_count, capacity)
    outgoing = jnp.einsum(
        "ecn,nd->ecd", table.astype(jnp.bfloat16), normed, preferred_element_type=jnp.float32
    ).astype(jnp.bfloat16)
    mine = lax.all_to_all(outgoing, "exp", 0, 0, tiled=True)
    mine = mine.reshape(group_count * capacity, -1)
    gathered = lax.all_gather(mine, "ctx", axis=0, tiled=True)
    produced = lax.psum_scatter(
        expert_part(gathered, w_gate[0], w_up[0], w_down[0]).astype(jnp.bfloat16),
        "ctx",
        scatter_dimension=0,
        tiled=True,
    )
    produced = produced.reshape(group_count, capacity, -1)
    returned = lax.all_to_all(produced, "exp", 0, 0, tiled=True)
    for column in range(2):
        fetched = jnp.einsum(
            "ecn,ecd->nd",
            table[column::2].astype(jnp.bfloat16),
            returned[column::2],
            preferred_element_type=jnp.float32,
        )
        hidden = hidden + my_weights[:, column][:, None] * fetched
    return hidden.astype(jnp.bfloat16)


def solution(mesh):
    in_specs = (
        P("ctx", "exp"),
        P("ctx", "exp"),
        P("ctx", "exp"),
        P("ctx", "exp"),
        P("exp"),
        P("exp"),
        P("exp", None),
        P(("ctx", "exp"), None),
        P(),
        P("ctx", None),
        P("ctx", None),
        P("exp", "ctx", None),
        P("exp", "ctx", None),
        P("exp", "ctx", None),
    )
    out_specs = P(("ctx", "exp"), None)
    return jax.shard_map(body, mesh=mesh, in_specs=in_specs, out_specs=out_specs, check_vma=False)
```

```python
import functools

import jax
import jax.numpy as jnp
from jax import lax
from jax.experimental import pallas as pl
from jax.experimental.pallas import tpu as pltpu
from jax.sharding import PartitionSpec as P

EPSILON = 1e-06


def earlier_states(update, decay_rates, row_count):
    size, index = (lax.axis_size("ctx"), lax.axis_index("ctx"))
    everything = lax.all_gather(update.astype(jnp.bfloat16), "ctx").astype(jnp.float32)
    distance = (index - 1 - jnp.arange(size)).astype(jnp.float32)
    factors = jnp.where(
        distance[:, None] >= 0.0,
        jnp.exp(-decay_rates[None, :] * row_count * jnp.maximum(distance, 0.0)[:, None]),
        0.0,
    )
    return jnp.sum(everything * factors[:, :, None, None], axis=0)


def span_local(queries, key_rows, value_rows, decay_exp):
    row_count = queries.shape[0]
    head_count = decay_exp.shape[0]
    head_width = queries.shape[1] // head_count
    query_heads = queries.reshape(row_count, head_count, head_width)
    key_heads = key_rows.reshape(row_count, head_count, head_width)
    value_heads = value_rows.reshape(row_count, head_count, head_width)
    decay_rates = jnp.exp2(-decay_exp.astype(jnp.float32))
    positions = jnp.arange(row_count, dtype=jnp.float32)
    offsets = positions[:, None] - positions[None, :]
    damping = jnp.where(
        offsets[None] >= 0.0,
        jnp.exp(-decay_rates[:, None, None] * jnp.maximum(offsets, 0.0)[None]),
        0.0,
    )
    scores = jnp.einsum("thd,shd->hts", query_heads, key_heads, preferred_element_type=jnp.float32)
    mixing = (scores * damping).astype(jnp.bfloat16)
    inner_part = jnp.einsum("hts,shd->thd", mixing, value_heads, preferred_element_type=jnp.float32)
    tail_decay = jnp.exp(-decay_rates[None, :] * (row_count - 1.0 - positions)[:, None])
    keyed_rows = (key_heads.astype(jnp.float32) * tail_decay[:, :, None]).astype(jnp.bfloat16)
    update = jnp.einsum("shd,she->hde", keyed_rows, value_heads, preferred_element_type=jnp.float32)
    lead_decay = jnp.exp(-decay_rates[None, :] * (positions + 1.0)[:, None])
    leading = query_heads.astype(jnp.float32) * lead_decay[:, :, None]
    return (inner_part, leading, update, decay_rates)


def settle(inner_part, leading, prior_state, gate_rows, attn_gain):
    outer_part = jnp.einsum("thd,hde->the", leading, prior_state, precision=lax.Precision.HIGHEST)
    mixed_heads = inner_part + outer_part
    row_count, head_count, head_width = mixed_heads.shape
    mean_square = jnp.mean(mixed_heads * mixed_heads, axis=2, keepdims=True)
    normed_heads = mixed_heads * lax.rsqrt(mean_square + EPSILON)
    gain_heads = attn_gain.reshape(head_count, head_width)
    gate_heads = gate_rows.reshape(row_count, head_count, head_width).astype(jnp.float32)
    settled = (normed_heads * gain_heads * jax.nn.sigmoid(gate_heads)).astype(jnp.bfloat16)
    return settled.reshape(row_count, head_count * head_width)


def token_norm(hidden, norm_gain):
    mean_square = jnp.mean(hidden * hidden, axis=1, keepdims=True)
    return (hidden * lax.rsqrt(mean_square + EPSILON) * norm_gain).astype(jnp.bfloat16)


def slot_table(chosen_ids, expert_count, capacity):
    owners = jnp.arange(expert_count, dtype=jnp.int32)
    chosen = jnp.where(owners[:, None] % 2 == 0, chosen_ids[None, :, 0], chosen_ids[None, :, 1])
    picked = chosen == owners[:, None]
    row_count = chosen_ids.shape[0]
    upto = jnp.arange(row_count)[:, None] <= jnp.arange(row_count)[None, :]
    slot_rank = jnp.dot(picked.astype(jnp.float32), upto.astype(jnp.float32)) - 1.0
    slot_ids = jnp.arange(capacity, dtype=jnp.float32)
    return picked[:, None, :] & (slot_rank[:, None, :] == slot_ids[None, :, None])


MESH = pl.DeviceIdType.MESH
BF16 = jnp.bfloat16
F32 = jnp.float32
RING = 4
CHUNKS = 3
WIDTH = 512
SLOTS = 32


def place(index):
    return index // 8, (index // 2) % 4, index % 2


class Copies:
    def __init__(self, send_sems, recv_sems, owner):
        self.send_sems, self.recv_sems, self.owner = send_sems, recv_sems, owner
        self.count, self.started = 0, []

    def start(self, source, target, ctx):
        copy = pltpu.make_async_remote_copy(
            src_ref=source,
            dst_ref=target,
            send_sem=self.send_sems.at[self.count],
            recv_sem=self.recv_sems.at[self.count],
            device_id=(ctx, self.owner),
            device_id_type=MESH,
        )
        copy.start()
        self.count += 1
        self.started.append(copy)
        return copy

    def finish(self):
        for copy in self.started:
            copy.wait_send()


def experts_kernel(
    slots, w_gate, w_up, w_down, out,
    rows, w_in, w_out, pre, act, part, in1, comb1, mid, in2, comb2,
    send_sems, recv_sems, local_sems,
):
    index, owner = lax.axis_index("ctx"), lax.axis_index("exp")
    z, x, core = place(index)

    def device(zz, xx):
        return zz * 8 + xx * 2 + core

    x_right, x_left = lax.rem(x + 1, RING), lax.rem(x + 3, RING)
    z_right, z_left = lax.rem(z + 1, RING), lax.rem(z + 3, RING)
    partner = index + 1 - 2 * core
    near = {
        "x": (x, x_left, x_right, device(z, x_left), device(z, x_right), lax.rem(x + 2, RING)),
        "z": (z, z_left, z_right, device(z_left, x), device(z_right, x), lax.rem(z + 2, RING)),
    }
    barrier = pltpu.get_barrier_semaphore()
    for other in (partner, near["x"][3], near["x"][4], near["z"][3], near["z"][4]):
        pl.semaphore_signal(barrier, inc=1, device_id=(other, owner), device_id_type=MESH)
    pl.semaphore_wait(barrier, 5)
    copies = Copies(send_sems, recv_sems, owner)
    units = w_gate.shape[0]

    first, second = ("x", "z"), ("z", "x")
    pairs = [(c, h) for c in range(CHUNKS) for h in range(2)]
    gather1, relay1, gather2, relay2, own = {}, {}, {}, {}, {}

    def line(c, h, stage, sub, at):
        axis = (first if stage == 1 else second)[h]
        if stage == 1:
            return rows.at[c, h, sub, at, x] if axis == "z" else rows.at[c, h, sub, z, at]
        return rows.at[c, h, sub, at] if axis == "z" else rows.at[c, h, sub, :, at]

    both = slice(None)
    for n, (c, h) in enumerate(pairs):
        me, left, right, to_left, to_right, far = near[first[h]]
        mine = line(c, h, 1, both, me)
        gather1[c, h] = (
            copies.start(slots.at[c, h], mine, to_right),
            copies.start(slots.at[c, h], mine, to_left),
        )
        own[c, h] = pltpu.make_async_copy(slots.at[c, h], mine, local_sems.at[n])
        own[c, h].start()

    weight_copies, weight_shares = [], []
    for n, (source, target, base) in enumerate(
        ((w_gate, w_in, 0), (w_up, w_in, 2 * units), (w_down, w_out, 0))
    ):
        copy = pltpu.make_async_copy(
            source, target.at[pl.ds(base, units)], local_sems.at[len(pairs) + n]
        )
        copy.start()
        weight_copies.append(copy)
        weight_shares.append(copies.start(source, target.at[pl.ds(base + units, units)], partner))

    def pass_on1(c, h):
        me, left, right, to_left, to_right, far = near[first[h]]
        from_left, from_right = gather1[c, h]
        from_left.wait_recv()
        source = line(c, h, 1, 0, left)
        one = copies.start(source, source, to_right)
        from_right.wait_recv()
        source = line(c, h, 1, 1, right)
        relay1[c, h] = (one, copies.start(source, source, to_left))

    def start2(c, h):
        for copy in relay1[c, h]:
            copy.wait_recv()
        own[c, h].wait()
        me, left, right, to_left, to_right, far = near[second[h]]
        mine = line(c, h, 2, both, me)
        gather2[c, h] = (copies.start(mine, mine, to_right), copies.start(mine, mine, to_left))

    def pass_on2(c, h):
        me, left, right, to_left, to_right, far = near[second[h]]
        from_left, from_right = gather2[c, h]
        from_left.wait_recv()
        source = line(c, h, 2, 0, left)
        one = copies.start(source, source, to_right)
        from_right.wait_recv()
        source = line(c, h, 2, 1, right)
        relay2[c, h] = (one, copies.start(source, source, to_left))

    def multiply_in(c):
        for h in range(2):
            for copy in relay2[c, h]:
                copy.wait_recv()
        if c == 0:
            for n in range(2):
                weight_copies[n].wait()
                weight_shares[n].wait_recv()

        def tile(t, carry):
            total = None
            for h in range(2):
                for sub in range(2):
                    block = rows[c, h, sub, pl.ds(2 * t, 2)].reshape(256, WIDTH)
                    column = ((c * 2 + h) * 2 + sub) * WIDTH
                    term = lax.dot_general(
                        w_in[:, column : column + WIDTH],
                        block,
                        (((1,), (1,)), ((), ())),
                        preferred_element_type=F32,
                    )
                    total = term if total is None else total + term
            if c == 0:
                pre[t] = total
            else:
                pre[t] = pre[t] + total
            return carry

        lax.fori_loop(0, 2, tile, 0)

    for c, h in pairs:
        pass_on1(c, h)
    for h in range(2):
        start2(0, h)
    for h in range(2):
        start2(1, h)
    for h in range(2):
        start2(2, h)
    for h in range(2):
        pass_on2(0, h)
    for h in range(2):
        pass_on2(1, h)
    multiply_in(0)
    for h in range(2):
        pass_on2(2, h)
    multiply_in(1)
    multiply_in(2)

    def activate(t, carry):
        gate = pre[t, : 2 * units]
        up = pre[t, 2 * units :]
        value = gate / (1.0 + jnp.exp(-gate)) * up
        act[pl.ds(pl.multiple_of(t * 256, 256), 256), :] = value.T.astype(BF16)
        return carry

    lax.fori_loop(0, 2, activate, 0)
    weight_copies[2].wait()
    weight_shares[2].wait_recv()

    def multiply_out(c):
        def block(n, carry):
            column = pl.multiple_of((c * 4 + n) * WIDTH, WIDTH)
            value = jnp.dot(
                act[...], w_out[:, pl.ds(column, WIDTH)], preferred_element_type=F32
            )
            part[c, n // 2, n % 2] = value.astype(BF16).reshape(RING, RING, SLOTS, WIDTH)
            return carry

        lax.fori_loop(0, 4, block, 0)

    def piece(c, h, sub, at):
        return part.at[c, h, sub, at] if second[h] == "z" else part.at[c, h, sub, :, at]

    def scatter(c, h, axis, view, landing):
        me, left, right, to_left, to_right, far = near[axis]
        return (
            copies.start(view(0, far), landing.at[c, h, 0], to_left),
            copies.start(view(1, far), landing.at[c, h, 1], to_right),
            copies.start(view(0, right), landing.at[c, h, 2], to_right),
            copies.start(view(1, left), landing.at[c, h, 3], to_left),
        )

    def join(c, h, axis, view, landing, staging, sent):
        me, left, right, to_left, to_right, far = near[axis]
        joined = []
        for sub, at, to in ((0, left, to_left), (1, right, to_right)):
            sent[sub].wait_recv()
            staging[c, h, sub] = (
                landing[c, h, sub].astype(F32) + view(sub, at)[...].astype(F32)
            ).astype(BF16)
            joined.append(copies.start(staging.at[c, h, sub], landing.at[c, h, 4 + sub], to))
        return joined

    def total(c, h, axis, view, landing, sent, joined, sub):
        me = near[axis][0]
        sent[2 + sub].wait_recv()
        joined[sub].wait_recv()
        return (
            view(sub, me)[...].astype(F32)
            + landing[c, h, 2 + sub].astype(F32)
            + landing[c, h, 4 + sub].astype(F32)
        ).astype(BF16)

    sent1, joined1, sent2, joined2 = {}, {}, {}, {}

    def send_part(c):
        for h in range(2):
            sent1[c, h] = scatter(c, h, second[h], functools.partial(piece, c, h), in1)

    def join_part(c):
        for h in range(2):
            view = functools.partial(piece, c, h)
            joined1[c, h] = join(c, h, second[h], view, in1, comb1, sent1[c, h])

    def middle(c, h, sub, at):
        return mid.at[c, h, sub, at]

    def send_mid(c):
        for h in range(2):
            view = functools.partial(piece, c, h)
            for sub in range(2):
                mid[c, h, sub] = total(
                    c, h, second[h], view, in1, sent1[c, h], joined1[c, h], sub
                )
            view = functools.partial(middle, c, h)
            sent2[c, h] = scatter(c, h, first[h], view, in2)

    def join_mid(c):
        for h in range(2):
            view = functools.partial(middle, c, h)
            joined2[c, h] = join(c, h, first[h], view, in2, comb2, sent2[c, h])

    def settle_out(c):
        for h in range(2):
            view = functools.partial(middle, c, h)
            for sub in range(2):
                out[c, h, sub] = total(
                    c, h, first[h], view, in2, sent2[c, h], joined2[c, h], sub
                )

    multiply_out(0)
    send_part(0)
    multiply_out(1)
    send_part(1)
    multiply_out(2)
    send_part(2)
    join_part(0)
    join_part(1)
    send_mid(0)
    join_part(2)
    join_mid(0)
    send_mid(1)
    settle_out(0)
    join_mid(1)
    send_mid(2)
    settle_out(1)
    join_mid(2)
    settle_out(2)
    copies.finish()


def experts(slots, w_gate, w_up, w_down):
    units, width = w_gate.shape
    blocked = slots.reshape(SLOTS, CHUNKS, 2, 2, WIDTH).transpose(1, 2, 3, 0, 4)
    count = CHUNKS * 2 * (8 + 12) + 3
    whole = (CHUNKS, 2, 2, RING, RING, SLOTS, WIDTH)
    produced = pl.pallas_call(
        experts_kernel,
        out_shape=jax.ShapeDtypeStruct(blocked.shape, BF16),
        in_specs=[pl.BlockSpec(memory_space=pltpu.VMEM)] + [pl.BlockSpec(memory_space=pl.ANY)] * 3,
        out_specs=pl.BlockSpec(memory_space=pltpu.VMEM),
        scratch_shapes=[
            pltpu.VMEM(whole, BF16),
            pltpu.VMEM((4 * units, width), BF16),
            pltpu.VMEM((2 * units, width), BF16),
            pltpu.VMEM((2, 4 * units, 256), F32),
            pltpu.VMEM((RING * RING * SLOTS, 2 * units), BF16),
            pltpu.VMEM(whole, BF16),
            pltpu.VMEM((CHUNKS, 2, 6, RING, SLOTS, WIDTH), BF16),
            pltpu.VMEM((CHUNKS, 2, 2, RING, SLOTS, WIDTH), BF16),
            pltpu.VMEM((CHUNKS, 2, 2, RING, SLOTS, WIDTH), BF16),
            pltpu.VMEM((CHUNKS, 2, 6, SLOTS, WIDTH), BF16),
            pltpu.VMEM((CHUNKS, 2, 2, SLOTS, WIDTH), BF16),
            pltpu.SemaphoreType.DMA((count,)),
            pltpu.SemaphoreType.DMA((count,)),
            pltpu.SemaphoreType.DMA((2 * CHUNKS + 3,)),
        ],
        compiler_params=pltpu.CompilerParams(
            collective_id=3, has_side_effects=True, vmem_limit_bytes=64000 * 1024
        ),
        name="experts",
    )(blocked, w_gate, w_up, w_down)
    return produced.transpose(3, 0, 1, 2, 4).reshape(SLOTS, width)


def body(
    queries,
    key_rows,
    value_rows,
    gate_rows,
    decay_exp,
    attn_gain,
    out_proj,
    residual,
    norm_gain,
    routes,
    route_weights,
    w_gate,
    w_up,
    w_down,
):
    inner_part, leading, update, decay_rates = span_local(
        queries, key_rows, value_rows, decay_exp
    )
    span_rows = queries.shape[0]
    prior_state = earlier_states(update, decay_rates, span_rows)
    settled = settle(inner_part, leading, prior_state, gate_rows, attn_gain)
    group_count = lax.axis_size("exp")
    group_rows = span_rows // group_count
    first_mine = lax.axis_index("exp") * group_rows
    capacity = group_rows // 8
    projected = jnp.dot(settled, out_proj, preferred_element_type=jnp.float32)
    summed = lax.psum_scatter(
        projected.astype(jnp.bfloat16), "exp", scatter_dimension=0, tiled=True
    ).astype(jnp.float32)
    hidden = summed + residual.astype(jnp.float32)
    normed = token_norm(hidden, norm_gain)
    my_routes = lax.dynamic_slice_in_dim(routes, first_mine, group_rows, 0)
    my_weights = lax.dynamic_slice_in_dim(route_weights, first_mine, group_rows, 0)
    table = slot_table(my_routes, group_count, capacity)
    outgoing = jnp.einsum(
        "ecn,nd->ecd", table.astype(jnp.bfloat16), normed, preferred_element_type=jnp.float32
    ).astype(jnp.bfloat16)
    mine = lax.all_to_all(outgoing, "exp", 0, 0, tiled=True)
    mine = mine.reshape(group_count * capacity, -1)
    produced = experts(mine, w_gate[0], w_up[0], w_down[0])
    produced = produced.reshape(group_count, capacity, -1)
    returned = lax.all_to_all(produced, "exp", 0, 0, tiled=True)
    for column in range(2):
        fetched = jnp.einsum(
            "ecn,ecd->nd",
            table[column::2].astype(jnp.bfloat16),
            returned[column::2],
            preferred_element_type=jnp.float32,
        )
        hidden = hidden + my_weights[:, column][:, None] * fetched
    return hidden.astype(jnp.bfloat16)


def solution(mesh):
    in_specs = (
        P("ctx", "exp"),
        P("ctx", "exp"),
        P("ctx", "exp"),
        P("ctx", "exp"),
        P("exp"),
        P("exp"),
        P("exp", None),
        P(("ctx", "exp"), None),
        P(),
        P("ctx", None),
        P("ctx", None),
        P("exp", "ctx", None),
        P("exp", "ctx", None),
        P("exp", "ctx", None),
    )
    out_specs = P(("ctx", "exp"), None)
    return jax.shard_map(body, mesh=mesh, in_specs=in_specs, out_specs=out_specs, check_vma=False)
```

```python
import functools

import jax
import jax.numpy as jnp
from jax import lax
from jax.experimental import pallas as pl
from jax.experimental.pallas import tpu as pltpu
from jax.sharding import PartitionSpec as P

EPSILON = 1e-06
MESH = pl.DeviceIdType.MESH
BF16 = jnp.bfloat16
F32 = jnp.float32
RING = 4
CHUNKS = 3
WIDTH = 512
SLOTS = 32


def attention_kernel(
    decay_exp, queries_hbm, keys_hbm, values_hbm, gates_hbm, attn_gain, settled,
    queries, key_rows, value_rows, gate_rows, update, gathered, prior, state, inner,
    send_sems, recv_sems, send_sems2, recv_sems2, local_sems,
):
    index, owner = lax.axis_index("ctx"), lax.axis_index("exp")
    size = gathered.shape[0]
    head_count = decay_exp.shape[0]
    row_count = queries.shape[0]
    head_width = queries.shape[1] // head_count

    loads = []
    for n, (source, target) in enumerate(
        (
            (keys_hbm, key_rows),
            (values_hbm, value_rows),
            (queries_hbm, queries),
            (gates_hbm, gate_rows),
        )
    ):
        loads.append(pltpu.make_async_copy(source, target, local_sems.at[2 + n]))
        loads[n].start()
    barrier = pltpu.get_barrier_semaphore()

    def greet(step, carry):
        other = lax.rem(index + step, size)
        pl.semaphore_signal(barrier, inc=1, device_id=(other, owner), device_id_type=MESH)
        return carry

    lax.fori_loop(1, size, greet, 0)

    def rate_of(head, shape):
        exponent = jnp.full(shape, decay_exp[head].astype(F32), F32)
        return jnp.exp2(-exponent)

    def columns(head):
        return slice(head * head_width, (head + 1) * head_width)

    positions = lax.broadcasted_iota(jnp.int32, (row_count, head_width), 0).astype(F32)
    loads[0].wait()
    loads[1].wait()
    for head in range(head_count):
        rate = rate_of(head, (1, head_width))
        tail = jnp.exp(-rate * (row_count - 1.0 - positions))
        keyed = (key_rows[:, columns(head)].astype(F32) * tail).astype(BF16)
        product = lax.dot_general(
            keyed,
            value_rows[:, columns(head)],
            (((0,), (0,)), ((), ())),
            preferred_element_type=F32,
        )
        parts = size // head_count
        update[head * parts : (head + 1) * parts] = product.astype(BF16).reshape(
            parts, head_width // parts, head_width
        )
    pl.semaphore_wait(barrier, size - 1)

    def exchange(source, target, send, recv):
        def copy(step):
            other = lax.rem(index + step, size)
            return pltpu.make_async_remote_copy(
                src_ref=source.at[other],
                dst_ref=target.at[index],
                send_sem=send.at[step - 1],
                recv_sem=recv.at[step - 1],
                device_id=(other, owner),
                device_id_type=MESH,
            )

        def start(step, carry):
            copy(step).start()
            return carry

        def arrive(step, carry):
            copy(step).wait_recv()
            return carry

        def leave(step, carry):
            copy(step).wait_send()
            return carry

        return (
            lambda: lax.fori_loop(1, size, start, 0),
            lambda: lax.fori_loop(1, size, arrive, 0),
            lambda: lax.fori_loop(1, size, leave, 0),
        )

    start, arrive, leave = exchange(update, gathered, send_sems, recv_sems)
    start()
    kept = pltpu.make_async_copy(update.at[index], gathered.at[index], local_sems.at[0])
    kept.start()

    def inside(head):
        rate = rate_of(head, (1, row_count))
        row = lax.broadcasted_iota(jnp.int32, (row_count, row_count), 0)
        column = lax.broadcasted_iota(jnp.int32, (row_count, row_count), 1)
        offset = (row - column).astype(F32)
        damping = jnp.where(offset >= 0.0, jnp.exp(-rate * jnp.maximum(offset, 0.0)), 0.0)
        scores = lax.dot_general(
            queries[:, columns(head)],
            key_rows[:, columns(head)],
            (((1,), (1,)), ((), ())),
            preferred_element_type=F32,
        )
        mixing = (scores * damping).astype(BF16)
        inner[head] = jnp.dot(mixing, value_rows[:, columns(head)], preferred_element_type=F32)

    loads[2].wait()
    loads[3].wait()
    for head in range(head_count // 2):
        inside(head)
    kept.wait()
    arrive()
    mine = index // (size // head_count)
    carry_decay = jnp.exp(-rate_of(mine, (1, head_width)) * float(row_count))
    running = jnp.zeros(gathered.shape[1:], F32)
    for block in range(size):
        prior[block] = running.astype(BF16)
        if block + 1 < size:
            running = carry_decay * running + gathered[block].astype(F32)
    start2, arrive2, leave2 = exchange(prior, state, send_sems2, recv_sems2)
    start2()
    kept2 = pltpu.make_async_copy(prior.at[index], state.at[index], local_sems.at[1])
    kept2.start()
    for head in range(head_count // 2, head_count):
        inside(head)
    leave()
    kept2.wait()
    arrive2()
    for head in range(head_count):
        rate = rate_of(head, (1, head_width))
        parts = size // head_count
        held = state[head * parts : (head + 1) * parts].reshape(head_width, head_width)
        reached = jnp.dot(queries[:, columns(head)], held, preferred_element_type=F32)
        mixed = inner[head] + reached * jnp.exp(-rate * (positions + 1.0))
        mean_square = jnp.mean(mixed * mixed, axis=1, keepdims=True)
        normed = mixed * lax.rsqrt(mean_square + EPSILON)
        gate = gate_rows[:, columns(head)].astype(F32)
        value = normed * attn_gain[:, columns(head)] * (1.0 / (1.0 + jnp.exp(-gate)))
        settled[:, columns(head)] = value.astype(BF16)
    leave2()


def attention(queries, key_rows, value_rows, gate_rows, decay_exp, attn_gain):
    row_count, width = queries.shape
    head_count = decay_exp.shape[0]
    head_width = width // head_count
    size = lax.axis_size("ctx")
    shares = (size, head_count * head_width // size, head_width)
    return pl.pallas_call(
        attention_kernel,
        out_shape=jax.ShapeDtypeStruct(queries.shape, BF16),
        in_specs=[pl.BlockSpec(memory_space=pltpu.SMEM)]
        + [pl.BlockSpec(memory_space=pltpu.HBM)] * 4
        + [pl.BlockSpec(memory_space=pltpu.VMEM)],
        out_specs=pl.BlockSpec(memory_space=pltpu.VMEM),
        scratch_shapes=[
            pltpu.VMEM(queries.shape, BF16),
            pltpu.VMEM(queries.shape, BF16),
            pltpu.VMEM(queries.shape, BF16),
            pltpu.VMEM(queries.shape, BF16),
            pltpu.VMEM(shares, BF16),
            pltpu.VMEM(shares, BF16),
            pltpu.VMEM(shares, BF16),
            pltpu.VMEM(shares, BF16),
            pltpu.VMEM((head_count, row_count, head_width), F32),
            pltpu.SemaphoreType.DMA((size - 1,)),
            pltpu.SemaphoreType.DMA((size - 1,)),
            pltpu.SemaphoreType.DMA((size - 1,)),
            pltpu.SemaphoreType.DMA((size - 1,)),
            pltpu.SemaphoreType.DMA((6,)),
        ],
        compiler_params=pltpu.CompilerParams(
            collective_id=1, has_side_effects=True, vmem_limit_bytes=16000 * 1024
        ),
        name="attention",
    )(decay_exp, queries, key_rows, value_rows, gate_rows, attn_gain.reshape(1, width))


def token_norm(hidden, norm_gain):
    mean_square = jnp.mean(hidden * hidden, axis=1, keepdims=True)
    return (hidden * lax.rsqrt(mean_square + EPSILON) * norm_gain).astype(jnp.bfloat16)


def slot_table(chosen_ids, expert_count, capacity):
    owners = jnp.arange(expert_count, dtype=jnp.int32)
    chosen = jnp.where(owners[:, None] % 2 == 0, chosen_ids[None, :, 0], chosen_ids[None, :, 1])
    picked = chosen == owners[:, None]
    row_count = chosen_ids.shape[0]
    upto = jnp.arange(row_count)[:, None] <= jnp.arange(row_count)[None, :]
    slot_rank = jnp.dot(picked.astype(jnp.float32), upto.astype(jnp.float32)) - 1.0
    slot_ids = jnp.arange(capacity, dtype=jnp.float32)
    return picked[:, None, :] & (slot_rank[:, None, :] == slot_ids[None, :, None])


def place(index):
    return index // 8, (index // 2) % 4, index % 2


class Copies:
    def __init__(self, send_sems, recv_sems, owner):
        self.send_sems, self.recv_sems, self.owner = send_sems, recv_sems, owner
        self.count, self.started = 0, []

    def start(self, source, target, ctx):
        copy = pltpu.make_async_remote_copy(
            src_ref=source,
            dst_ref=target,
            send_sem=self.send_sems.at[self.count],
            recv_sem=self.recv_sems.at[self.count],
            device_id=(ctx, self.owner),
            device_id_type=MESH,
        )
        copy.start()
        self.count += 1
        self.started.append(copy)
        return copy

    def finish(self):
        for copy in self.started:
            copy.wait_send()


def experts_kernel(
    slots, w_gate, w_up, w_down, out,
    rows, w_in, w_out, pre, act, part, in1, comb1, mid, in2, comb2,
    send_sems, recv_sems, local_sems,
):
    index, owner = lax.axis_index("ctx"), lax.axis_index("exp")
    z, x, core = place(index)

    def device(zz, xx):
        return zz * 8 + xx * 2 + core

    x_right, x_left = lax.rem(x + 1, RING), lax.rem(x + 3, RING)
    z_right, z_left = lax.rem(z + 1, RING), lax.rem(z + 3, RING)
    partner = index + 1 - 2 * core
    near = {
        "x": (x, x_left, x_right, device(z, x_left), device(z, x_right), lax.rem(x + 2, RING)),
        "z": (z, z_left, z_right, device(z_left, x), device(z_right, x), lax.rem(z + 2, RING)),
    }
    barrier = pltpu.get_barrier_semaphore()
    for other in (partner, near["x"][3], near["x"][4], near["z"][3], near["z"][4]):
        pl.semaphore_signal(barrier, inc=1, device_id=(other, owner), device_id_type=MESH)
    pl.semaphore_wait(barrier, 5)
    copies = Copies(send_sems, recv_sems, owner)
    units = w_gate.shape[0]

    first, second = ("x", "z"), ("z", "x")
    pairs = [(c, h) for c in range(CHUNKS) for h in range(2)]
    gather1, relay1, gather2, relay2, own = {}, {}, {}, {}, {}

    def line(c, h, stage, sub, at):
        axis = (first if stage == 1 else second)[h]
        if stage == 1:
            return rows.at[c, h, sub, at, x] if axis == "z" else rows.at[c, h, sub, z, at]
        return rows.at[c, h, sub, at] if axis == "z" else rows.at[c, h, sub, :, at]

    both = slice(None)
    for n, (c, h) in enumerate(pairs):
        me, left, right, to_left, to_right, far = near[first[h]]
        mine = line(c, h, 1, both, me)
        gather1[c, h] = (
            copies.start(slots.at[c, h], mine, to_right),
            copies.start(slots.at[c, h], mine, to_left),
        )
        own[c, h] = pltpu.make_async_copy(slots.at[c, h], mine, local_sems.at[n])
        own[c, h].start()

    weight_copies, weight_shares = [], []
    for n, (source, target, base) in enumerate(
        ((w_gate, w_in, 0), (w_up, w_in, 2 * units), (w_down, w_out, 0))
    ):
        copy = pltpu.make_async_copy(
            source, target.at[pl.ds(base, units)], local_sems.at[len(pairs) + n]
        )
        copy.start()
        weight_copies.append(copy)
        weight_shares.append(copies.start(source, target.at[pl.ds(base + units, units)], partner))

    def pass_on1(c, h):
        me, left, right, to_left, to_right, far = near[first[h]]
        from_left, from_right = gather1[c, h]
        from_left.wait_recv()
        source = line(c, h, 1, 0, left)
        one = copies.start(source, source, to_right)
        from_right.wait_recv()
        source = line(c, h, 1, 1, right)
        relay1[c, h] = (one, copies.start(source, source, to_left))

    def start2(c, h):
        for copy in relay1[c, h]:
            copy.wait_recv()
        own[c, h].wait()
        me, left, right, to_left, to_right, far = near[second[h]]
        mine = line(c, h, 2, both, me)
        gather2[c, h] = (copies.start(mine, mine, to_right), copies.start(mine, mine, to_left))

    def pass_on2(c, h):
        me, left, right, to_left, to_right, far = near[second[h]]
        from_left, from_right = gather2[c, h]
        from_left.wait_recv()
        source = line(c, h, 2, 0, left)
        one = copies.start(source, source, to_right)
        from_right.wait_recv()
        source = line(c, h, 2, 1, right)
        relay2[c, h] = (one, copies.start(source, source, to_left))

    def multiply_in(c):
        for h in range(2):
            for copy in relay2[c, h]:
                copy.wait_recv()
        if c == 0:
            for n in range(2):
                weight_copies[n].wait()
                weight_shares[n].wait_recv()

        def tile(t, carry):
            total = None
            for h in range(2):
                for sub in range(2):
                    block = rows[c, h, sub, pl.ds(2 * t, 2)].reshape(256, WIDTH)
                    column = ((c * 2 + h) * 2 + sub) * WIDTH
                    term = lax.dot_general(
                        w_in[:, column : column + WIDTH],
                        block,
                        (((1,), (1,)), ((), ())),
                        preferred_element_type=F32,
                    )
                    total = term if total is None else total + term
            if c == 0:
                pre[t] = total
            else:
                pre[t] = pre[t] + total
            return carry

        lax.fori_loop(0, 2, tile, 0)

    for c, h in pairs:
        pass_on1(c, h)
    for h in range(2):
        start2(0, h)
    for h in range(2):
        start2(1, h)
    for h in range(2):
        start2(2, h)
    for h in range(2):
        pass_on2(0, h)
    for h in range(2):
        pass_on2(1, h)
    multiply_in(0)
    for h in range(2):
        pass_on2(2, h)
    multiply_in(1)
    multiply_in(2)

    def activate(t, carry):
        gate = pre[t, : 2 * units]
        up = pre[t, 2 * units :]
        value = gate / (1.0 + jnp.exp(-gate)) * up
        act[pl.ds(pl.multiple_of(t * 256, 256), 256), :] = value.T.astype(BF16)
        return carry

    lax.fori_loop(0, 2, activate, 0)
    weight_copies[2].wait()
    weight_shares[2].wait_recv()

    def multiply_out(c):
        def block(n, carry):
            column = pl.multiple_of((c * 4 + n) * WIDTH, WIDTH)
            value = jnp.dot(
                act[...], w_out[:, pl.ds(column, WIDTH)], preferred_element_type=F32
            )
            part[c, n // 2, n % 2] = value.astype(BF16).reshape(RING, RING, SLOTS, WIDTH)
            return carry

        lax.fori_loop(0, 4, block, 0)

    def piece(c, h, sub, at):
        return part.at[c, h, sub, at] if second[h] == "z" else part.at[c, h, sub, :, at]

    def scatter(c, h, axis, view, landing):
        me, left, right, to_left, to_right, far = near[axis]
        return (
            copies.start(view(0, far), landing.at[c, h, 0], to_left),
            copies.start(view(1, far), landing.at[c, h, 1], to_right),
            copies.start(view(0, right), landing.at[c, h, 2], to_right),
            copies.start(view(1, left), landing.at[c, h, 3], to_left),
        )

    def join(c, h, axis, view, landing, staging, sent):
        me, left, right, to_left, to_right, far = near[axis]
        joined = []
        for sub, at, to in ((0, left, to_left), (1, right, to_right)):
            sent[sub].wait_recv()
            staging[c, h, sub] = (
                landing[c, h, sub].astype(F32) + view(sub, at)[...].astype(F32)
            ).astype(BF16)
            joined.append(copies.start(staging.at[c, h, sub], landing.at[c, h, 4 + sub], to))
        return joined

    def total(c, h, axis, view, landing, sent, joined, sub):
        me = near[axis][0]
        sent[2 + sub].wait_recv()
        joined[sub].wait_recv()
        return (
            view(sub, me)[...].astype(F32)
            + landing[c, h, 2 + sub].astype(F32)
            + landing[c, h, 4 + sub].astype(F32)
        ).astype(BF16)

    sent1, joined1, sent2, joined2 = {}, {}, {}, {}

    def send_part(c):
        for h in range(2):
            sent1[c, h] = scatter(c, h, second[h], functools.partial(piece, c, h), in1)

    def join_part(c):
        for h in range(2):
            view = functools.partial(piece, c, h)
            joined1[c, h] = join(c, h, second[h], view, in1, comb1, sent1[c, h])

    def middle(c, h, sub, at):
        return mid.at[c, h, sub, at]

    def send_mid(c):
        for h in range(2):
            view = functools.partial(piece, c, h)
            for sub in range(2):
                mid[c, h, sub] = total(
                    c, h, second[h], view, in1, sent1[c, h], joined1[c, h], sub
                )
            view = functools.partial(middle, c, h)
            sent2[c, h] = scatter(c, h, first[h], view, in2)

    def join_mid(c):
        for h in range(2):
            view = functools.partial(middle, c, h)
            joined2[c, h] = join(c, h, first[h], view, in2, comb2, sent2[c, h])

    def settle_out(c):
        for h in range(2):
            view = functools.partial(middle, c, h)
            for sub in range(2):
                out[c, h, sub] = total(
                    c, h, first[h], view, in2, sent2[c, h], joined2[c, h], sub
                )

    multiply_out(0)
    send_part(0)
    multiply_out(1)
    send_part(1)
    multiply_out(2)
    send_part(2)
    join_part(0)
    join_part(1)
    send_mid(0)
    join_part(2)
    join_mid(0)
    send_mid(1)
    settle_out(0)
    join_mid(1)
    send_mid(2)
    settle_out(1)
    join_mid(2)
    settle_out(2)
    copies.finish()


def experts(slots, w_gate, w_up, w_down):
    units, width = w_gate.shape
    blocked = slots.reshape(SLOTS, CHUNKS, 2, 2, WIDTH).transpose(1, 2, 3, 0, 4)
    count = CHUNKS * 2 * (8 + 12) + 3
    whole = (CHUNKS, 2, 2, RING, RING, SLOTS, WIDTH)
    produced = pl.pallas_call(
        experts_kernel,
        out_shape=jax.ShapeDtypeStruct(blocked.shape, BF16),
        in_specs=[pl.BlockSpec(memory_space=pltpu.VMEM)] + [pl.BlockSpec(memory_space=pl.ANY)] * 3,
        out_specs=pl.BlockSpec(memory_space=pltpu.VMEM),
        scratch_shapes=[
            pltpu.VMEM(whole, BF16),
            pltpu.VMEM((4 * units, width), BF16),
            pltpu.VMEM((2 * units, width), BF16),
            pltpu.VMEM((2, 4 * units, 256), F32),
            pltpu.VMEM((RING * RING * SLOTS, 2 * units), BF16),
            pltpu.VMEM(whole, BF16),
            pltpu.VMEM((CHUNKS, 2, 6, RING, SLOTS, WIDTH), BF16),
            pltpu.VMEM((CHUNKS, 2, 2, RING, SLOTS, WIDTH), BF16),
            pltpu.VMEM((CHUNKS, 2, 2, RING, SLOTS, WIDTH), BF16),
            pltpu.VMEM((CHUNKS, 2, 6, SLOTS, WIDTH), BF16),
            pltpu.VMEM((CHUNKS, 2, 2, SLOTS, WIDTH), BF16),
            pltpu.SemaphoreType.DMA((count,)),
            pltpu.SemaphoreType.DMA((count,)),
            pltpu.SemaphoreType.DMA((2 * CHUNKS + 3,)),
        ],
        compiler_params=pltpu.CompilerParams(
            collective_id=3, has_side_effects=True, vmem_limit_bytes=64000 * 1024
        ),
        name="experts",
    )(blocked, w_gate, w_up, w_down)
    return produced.transpose(3, 0, 1, 2, 4).reshape(SLOTS, width)


def body(
    queries,
    key_rows,
    value_rows,
    gate_rows,
    decay_exp,
    attn_gain,
    out_proj,
    residual,
    norm_gain,
    routes,
    route_weights,
    w_gate,
    w_up,
    w_down,
):
    settled = attention(queries, key_rows, value_rows, gate_rows, decay_exp, attn_gain)
    span_rows = queries.shape[0]
    group_count = lax.axis_size("exp")
    group_rows = span_rows // group_count
    first_mine = lax.axis_index("exp") * group_rows
    capacity = group_rows // 8
    projected = jnp.dot(settled, out_proj, preferred_element_type=jnp.float32)
    summed = lax.psum_scatter(
        projected.astype(jnp.bfloat16), "exp", scatter_dimension=0, tiled=True
    ).astype(jnp.float32)
    hidden = summed + residual.astype(jnp.float32)
    normed = token_norm(hidden, norm_gain)
    my_routes = lax.dynamic_slice_in_dim(routes, first_mine, group_rows, 0)
    my_weights = lax.dynamic_slice_in_dim(route_weights, first_mine, group_rows, 0)
    table = slot_table(my_routes, group_count, capacity)
    outgoing = jnp.einsum(
        "ecn,nd->ecd", table.astype(jnp.bfloat16), normed, preferred_element_type=jnp.float32
    ).astype(jnp.bfloat16)
    mine = lax.all_to_all(outgoing, "exp", 0, 0, tiled=True)
    mine = mine.reshape(group_count * capacity, -1)
    produced = experts(mine, w_gate[0], w_up[0], w_down[0])
    produced = produced.reshape(group_count, capacity, -1)
    returned = lax.all_to_all(produced, "exp", 0, 0, tiled=True)
    for column in range(2):
        fetched = jnp.einsum(
            "ecn,ecd->nd",
            table[column::2].astype(jnp.bfloat16),
            returned[column::2],
            preferred_element_type=jnp.float32,
        )
        hidden = hidden + my_weights[:, column][:, None] * fetched
    return hidden.astype(jnp.bfloat16)


def solution(mesh):
    in_specs = (
        P("ctx", "exp"),
        P("ctx", "exp"),
        P("ctx", "exp"),
        P("ctx", "exp"),
        P("exp"),
        P("exp"),
        P("exp", None),
        P(("ctx", "exp"), None),
        P(),
        P("ctx", None),
        P("ctx", None),
        P("exp", "ctx", None),
        P("exp", "ctx", None),
        P("exp", "ctx", None),
    )
    out_specs = P(("ctx", "exp"), None)
    return jax.shard_map(body, mesh=mesh, in_specs=in_specs, out_specs=out_specs, check_vma=False)
```

```python
import functools

import jax
import jax.numpy as jnp
from jax import lax
from jax.experimental import pallas as pl
from jax.experimental.pallas import tpu as pltpu
from jax.sharding import PartitionSpec as P

EPSILON = 1e-06
MESH = pl.DeviceIdType.MESH
BF16 = jnp.bfloat16
F32 = jnp.float32
RING = 4
CHUNKS = 6
WIDTH = 256
SLOTS = 32


def attention_kernel(
    decay_exp, queries_hbm, keys_hbm, values_hbm, gates_hbm, attn_gain, settled,
    queries, key_rows, value_rows, gate_rows, update, gathered, prior, state, inner,
    send_sems, recv_sems, send_sems2, recv_sems2, local_sems,
):
    index, owner = lax.axis_index("ctx"), lax.axis_index("exp")
    size = gathered.shape[0]
    head_count = decay_exp.shape[0]
    row_count = queries.shape[0]
    head_width = queries.shape[1] // head_count

    loads = []
    for n, (source, target) in enumerate(
        (
            (keys_hbm, key_rows),
            (values_hbm, value_rows),
            (queries_hbm, queries),
            (gates_hbm, gate_rows),
        )
    ):
        loads.append(pltpu.make_async_copy(source, target, local_sems.at[2 + n]))
        loads[n].start()
    barrier = pltpu.get_barrier_semaphore()

    def greet(step, carry):
        other = lax.rem(index + step, size)
        pl.semaphore_signal(barrier, inc=1, device_id=(other, owner), device_id_type=MESH)
        return carry

    lax.fori_loop(1, size, greet, 0)

    def rate_of(head, shape):
        exponent = jnp.full(shape, decay_exp[head].astype(F32), F32)
        return jnp.exp2(-exponent)

    def columns(head):
        return slice(head * head_width, (head + 1) * head_width)

    positions = lax.broadcasted_iota(jnp.int32, (row_count, head_width), 0).astype(F32)
    loads[0].wait()
    loads[1].wait()
    for head in range(head_count):
        rate = rate_of(head, (1, head_width))
        tail = jnp.exp(-rate * (row_count - 1.0 - positions))
        keyed = (key_rows[:, columns(head)].astype(F32) * tail).astype(BF16)
        product = lax.dot_general(
            keyed,
            value_rows[:, columns(head)],
            (((0,), (0,)), ((), ())),
            preferred_element_type=F32,
        )
        parts = size // head_count
        update[head * parts : (head + 1) * parts] = product.astype(BF16).reshape(
            parts, head_width // parts, head_width
        )
    pl.semaphore_wait(barrier, size - 1)

    def exchange(source, target, send, recv):
        def copy(step):
            other = lax.rem(index + step, size)
            return pltpu.make_async_remote_copy(
                src_ref=source.at[other],
                dst_ref=target.at[index],
                send_sem=send.at[step - 1],
                recv_sem=recv.at[step - 1],
                device_id=(other, owner),
                device_id_type=MESH,
            )

        def start(step, carry):
            copy(step).start()
            return carry

        def arrive(step, carry):
            copy(step).wait_recv()
            return carry

        def leave(step, carry):
            copy(step).wait_send()
            return carry

        return (
            lambda: lax.fori_loop(1, size, start, 0),
            lambda: lax.fori_loop(1, size, arrive, 0),
            lambda: lax.fori_loop(1, size, leave, 0),
        )

    start, arrive, leave = exchange(update, gathered, send_sems, recv_sems)
    start()
    kept = pltpu.make_async_copy(update.at[index], gathered.at[index], local_sems.at[0])
    kept.start()

    def inside(head):
        rate = rate_of(head, (1, row_count))
        row = lax.broadcasted_iota(jnp.int32, (row_count, row_count), 0)
        column = lax.broadcasted_iota(jnp.int32, (row_count, row_count), 1)
        offset = (row - column).astype(F32)
        damping = jnp.where(offset >= 0.0, jnp.exp(-rate * jnp.maximum(offset, 0.0)), 0.0)
        scores = lax.dot_general(
            queries[:, columns(head)],
            key_rows[:, columns(head)],
            (((1,), (1,)), ((), ())),
            preferred_element_type=F32,
        )
        mixing = (scores * damping).astype(BF16)
        inner[head] = jnp.dot(mixing, value_rows[:, columns(head)], preferred_element_type=F32)

    loads[2].wait()
    loads[3].wait()
    for head in range(head_count // 2):
        inside(head)
    kept.wait()
    arrive()
    mine = index // (size // head_count)
    carry_decay = jnp.exp(-rate_of(mine, (1, head_width)) * float(row_count))
    running = jnp.zeros(gathered.shape[1:], F32)
    for block in range(size):
        prior[block] = running.astype(BF16)
        if block + 1 < size:
            running = carry_decay * running + gathered[block].astype(F32)
    start2, arrive2, leave2 = exchange(prior, state, send_sems2, recv_sems2)
    start2()
    kept2 = pltpu.make_async_copy(prior.at[index], state.at[index], local_sems.at[1])
    kept2.start()
    for head in range(head_count // 2, head_count):
        inside(head)
    leave()
    kept2.wait()
    arrive2()
    for head in range(head_count):
        rate = rate_of(head, (1, head_width))
        parts = size // head_count
        held = state[head * parts : (head + 1) * parts].reshape(head_width, head_width)
        reached = jnp.dot(queries[:, columns(head)], held, preferred_element_type=F32)
        mixed = inner[head] + reached * jnp.exp(-rate * (positions + 1.0))
        mean_square = jnp.mean(mixed * mixed, axis=1, keepdims=True)
        normed = mixed * lax.rsqrt(mean_square + EPSILON)
        gate = gate_rows[:, columns(head)].astype(F32)
        value = normed * attn_gain[:, columns(head)] * (1.0 / (1.0 + jnp.exp(-gate)))
        settled[:, columns(head)] = value.astype(BF16)
    leave2()


def attention(queries, key_rows, value_rows, gate_rows, decay_exp, attn_gain):
    row_count, width = queries.shape
    head_count = decay_exp.shape[0]
    head_width = width // head_count
    size = lax.axis_size("ctx")
    shares = (size, head_count * head_width // size, head_width)
    return pl.pallas_call(
        attention_kernel,
        out_shape=jax.ShapeDtypeStruct(queries.shape, BF16),
        in_specs=[pl.BlockSpec(memory_space=pltpu.SMEM)]
        + [pl.BlockSpec(memory_space=pltpu.HBM)] * 4
        + [pl.BlockSpec(memory_space=pltpu.VMEM)],
        out_specs=pl.BlockSpec(memory_space=pltpu.VMEM),
        scratch_shapes=[
            pltpu.VMEM(queries.shape, BF16),
            pltpu.VMEM(queries.shape, BF16),
            pltpu.VMEM(queries.shape, BF16),
            pltpu.VMEM(queries.shape, BF16),
            pltpu.VMEM(shares, BF16),
            pltpu.VMEM(shares, BF16),
            pltpu.VMEM(shares, BF16),
            pltpu.VMEM(shares, BF16),
            pltpu.VMEM((head_count, row_count, head_width), F32),
            pltpu.SemaphoreType.DMA((size - 1,)),
            pltpu.SemaphoreType.DMA((size - 1,)),
            pltpu.SemaphoreType.DMA((size - 1,)),
            pltpu.SemaphoreType.DMA((size - 1,)),
            pltpu.SemaphoreType.DMA((6,)),
        ],
        compiler_params=pltpu.CompilerParams(
            collective_id=1, has_side_effects=True, vmem_limit_bytes=64000 * 1024
        ),
        name="attention",
    )(decay_exp, queries, key_rows, value_rows, gate_rows, attn_gain.reshape(1, width))


def slot_table(chosen_ids, expert_count, capacity):
    owners = jnp.arange(expert_count, dtype=jnp.int32)
    chosen = jnp.where(owners[:, None] % 2 == 0, chosen_ids[None, :, 0], chosen_ids[None, :, 1])
    picked = chosen == owners[:, None]
    row_count = chosen_ids.shape[0]
    upto = jnp.arange(row_count)[:, None] <= jnp.arange(row_count)[None, :]
    slot_rank = jnp.dot(picked.astype(jnp.float32), upto.astype(jnp.float32)) - 1.0
    slot_ids = jnp.arange(capacity, dtype=jnp.float32)
    return picked[:, None, :] & (slot_rank[:, None, :] == slot_ids[None, :, None])


def place(index):
    return index // 8, (index // 2) % 4, index % 2


class Copies:
    def __init__(self, send_sems, recv_sems):
        self.send_sems, self.recv_sems = send_sems, recv_sems
        self.count, self.waiting = 0, []

    def start(self, source, target, device):
        copy = pltpu.make_async_remote_copy(
            src_ref=source,
            dst_ref=target,
            send_sem=self.send_sems.at[self.count],
            recv_sem=self.recv_sems.at[self.count],
            device_id=device,
            device_id_type=MESH,
        )
        copy.start()
        self.count += 1
        self.waiting.append(copy)
        return copy

    def finish(self):
        for copy in self.waiting:
            copy.wait_send()
        self.waiting = []


def layer_kernel(
    settled, out_proj, residual, norm_gain, pick, fetch, shares, w_gate, w_up, w_down, out,
    proj_w, proj, in0, comb0, hidden, squares, outbox, inbox, scale_out, scale_in, scales,
    rows, w_in, w_out, pre, act, in1, comb1, mid, in2, comb2, homebox, back,
    send_sems, recv_sems, local_sems,
):
    index, owner = lax.axis_index("ctx"), lax.axis_index("exp")
    z, x, core = place(index)
    part = rows

    def device(zz, xx):
        return (zz * 8 + xx * 2 + core, owner)

    def beside(at):
        return lax.rem(at + RING - 1, RING), lax.rem(at + 1, RING), lax.rem(at + 2, RING)

    x_left, x_right, x_far = beside(x)
    z_left, z_right, z_far = beside(z)
    y_left, y_right, y_far = beside(owner)
    partner = (index + 1 - 2 * core, owner)
    near = {
        "x": (x, x_left, x_right, device(z, x_left), device(z, x_right), x_far),
        "z": (z, z_left, z_right, device(z_left, x), device(z_right, x), z_far),
        "y": (owner, y_left, y_right, (index, y_left), (index, y_right), y_far),
    }
    column_peers = [lax.rem(owner + step, RING) for step in range(1, RING)]
    plane_peers = [
        device(lax.rem(z + dz, RING), lax.rem(x + dx, RING))
        for dz in range(RING)
        for dx in range(RING)
        if dz or dx
    ]
    barrier = pltpu.get_barrier_semaphore()
    greeted = [partner] + [(index, other) for other in column_peers] + plane_peers
    for other in greeted:
        pl.semaphore_signal(barrier, inc=1, device_id=other, device_id_type=MESH)
    copies = Copies(send_sems, recv_sems)
    local_count = [0]

    def local(source, target):
        copy = pltpu.make_async_copy(source, target, local_sems.at[local_count[0]])
        local_count[0] += 1
        copy.start()
        return copy

    units = w_gate.shape[0]
    piece_width = 4 * WIDTH
    half = 2 * WIDTH
    first, second = ("x", "z"), ("z", "x")
    both = slice(None)

    def scatter(axis, view, land):
        me, left, right, to_left, to_right, far = near[axis]
        return (
            copies.start(view(0, far), land(0), to_left),
            copies.start(view(1, far), land(1), to_right),
            copies.start(view(0, right), land(2), to_right),
            copies.start(view(1, left), land(3), to_left),
        )

    def join(axis, view, land, stage, sent):
        me, left, right, to_left, to_right, far = near[axis]
        joined = []
        for sub, at, to in ((0, left, to_left), (1, right, to_right)):
            sent[sub].wait_recv()
            stage(sub)[...] = (
                land(sub)[...].astype(F32) + view(sub, at)[...].astype(F32)
            ).astype(BF16)
            joined.append(copies.start(stage(sub), land(4 + sub), to))
        return joined

    def total(axis, view, land, sent, joined, sub):
        me = near[axis][0]
        sent[2 + sub].wait_recv()
        joined[sub].wait_recv()
        return (
            view(sub, me)[...].astype(F32)
            + land(2 + sub)[...].astype(F32)
            + land(4 + sub)[...].astype(F32)
        )

    loads = {}

    def load_proj(c):
        loads[c] = local(out_proj.at[:, pl.ds(c * piece_width, piece_width)], proj_w.at[c % 2])

    def project(c):
        loads[c].wait()
        for s in range(2):
            value = jnp.dot(
                settled[...],
                proj_w[c % 2, :, s * half : (s + 1) * half],
                preferred_element_type=F32,
            )
            proj[c, s] = value.astype(BF16).reshape(RING, -1, half)
        if c + 2 < CHUNKS:
            load_proj(c + 2)

    sent0, joined0, dispatched = {}, {}, {}

    def view0(c):
        return lambda sub, at: proj.at[c, sub, at]

    def land0(c):
        return lambda i: in0.at[c, i]

    def send_proj(c):
        sent0[c] = scatter("y", view0(c), land0(c))

    def join_proj(c):
        joined0[c] = join("y", view0(c), land0(c), lambda sub: comb0.at[c, sub], sent0[c])

    def exchange(box, landing):
        sent = [
            copies.start(box.at[other], landing.at[owner], (index, other))
            for other in column_peers
        ]
        return sent, local(box.at[owner], landing.at[owner])

    def arrive(exchanged):
        for copy in exchanged[0]:
            copy.wait_recv()
        exchanged[1].wait()

    def stacked(box, *place):
        return jnp.concatenate(
            [box[(*place[:1], e, *place[1:])].astype(F32) for e in range(RING)], axis=0
        )

    def dispatch(c):
        for s in range(2):
            columns = slice((c * 2 + s) * half, (c * 2 + s + 1) * half)
            value = total("y", view0(c), land0(c), sent0[c], joined0[c], s)
            value = value + residual[:, columns].astype(F32)
            hidden[c, s] = value
            square = value * value
            folded = square[:, :128]
            for lane in range(128, half, 128):
                folded = folded + square[:, lane : lane + 128]
            if c == 0 and s == 0:
                squares[...] = folded
            else:
                squares[...] = squares[...] + folded
            scaled = (value * norm_gain[:, columns]).astype(BF16)
            picked = jnp.dot(pick[...], scaled, preferred_element_type=F32)
            for e in range(RING):
                outbox[c, e, s] = picked[8 * e : 8 * e + 8].astype(BF16)
        dispatched[c] = exchange(outbox.at[c], inbox.at[c])

    def send_scales():
        mean_square = jnp.sum(squares[...], axis=1, keepdims=True) / (CHUNKS * piece_width)
        inverse = jnp.broadcast_to(lax.rsqrt(mean_square + EPSILON), squares.shape)
        picked = jnp.dot(
            pick[...].astype(F32),
            inverse,
            precision=lax.Precision.HIGHEST,
            preferred_element_type=F32,
        )
        for e in range(RING):
            scale_out[e] = picked[8 * e : 8 * e + 8]
        return exchange(scale_out, scale_in)

    def share_scales(exchanged):
        arrive(exchanged)
        mine = jnp.concatenate([scale_in[e] for e in range(RING)], axis=0)
        row = lax.broadcasted_iota(jnp.int32, (SLOTS, 128), 0)
        lane = lax.broadcasted_iota(jnp.int32, (SLOTS, 128), 1)
        line = jnp.sum(jnp.where(lane == x * SLOTS + row, mine, 0.0), axis=0, keepdims=True)
        scales[z, x] = jnp.broadcast_to(line, (8, 128))
        return [copies.start(scales.at[z, x], scales.at[z, x], other) for other in plane_peers]

    gather1, relay1, gather2, relay2 = {}, {}, {}, {}

    def line_of(c, h, stage, sub, at):
        axis = (first if stage == 1 else second)[h]
        if stage == 1:
            return rows.at[c, h, sub, at, x] if axis == "z" else rows.at[c, h, sub, z, at]
        return rows.at[c, h, sub, at] if axis == "z" else rows.at[c, h, sub, :, at]

    def spread(c, h, stage, started):
        me, left, right, to_left, to_right, far = near[(first if stage == 1 else second)[h]]
        mine = line_of(c, h, stage, both, me)
        started[c, h] = (copies.start(mine, mine, to_right), copies.start(mine, mine, to_left))

    def pass_on(c, h, stage, started, passed):
        me, left, right, to_left, to_right, far = near[(first if stage == 1 else second)[h]]
        from_left, from_right = started[c, h]
        from_left.wait_recv()
        source = line_of(c, h, stage, 0, left)
        one = copies.start(source, source, to_right)
        from_right.wait_recv()
        source = line_of(c, h, stage, 1, right)
        passed[c, h] = (one, copies.start(source, source, to_left))

    def gather_start(c):
        arrive(dispatched[c])
        for s in range(2):
            value = stacked(inbox, c, s).astype(BF16)
            for sub in range(2):
                rows[c, s, sub, z, x] = value[:, sub * WIDTH : (sub + 1) * WIDTH]
        for h in range(2):
            spread(c, h, 1, gather1)

    def gather_pass(c):
        for h in range(2):
            pass_on(c, h, 1, gather1, relay1)

    def gather_wide(c):
        for h in range(2):
            for copy in relay1[c, h]:
                copy.wait_recv()
            spread(c, h, 2, gather2)

    def gather_wide_pass(c):
        for h in range(2):
            pass_on(c, h, 2, gather2, relay2)

    weights = []

    def load_weights():
        for source, target, base in (
            (w_gate, w_in, 0),
            (w_up, w_in, 2 * units),
            (w_down, w_out, 0),
        ):
            kept = local(source, target.at[pl.ds(base, units)])
            sent = copies.start(source, target.at[pl.ds(base + units, units)], partner)
            weights.append((kept, sent))

    def multiply_in(c):
        for cc in (c, c + 1):
            for h in range(2):
                for copy in relay2[cc, h]:
                    copy.wait_recv()
        if c == 0:
            for n in range(2):
                weights[n][0].wait()
                weights[n][1].wait_recv()

        def tile(t, carry):
            total = None
            for cc in (c, c + 1):
                for h in range(2):
                    for sub in range(2):
                        block = rows[cc, h, sub, pl.ds(2 * t, 2)].reshape(256, WIDTH)
                        column = ((cc * 2 + h) * 2 + sub) * WIDTH
                        term = lax.dot_general(
                            w_in[:, column : column + WIDTH],
                            block,
                            (((1,), (1,)), ((), ())),
                            preferred_element_type=F32,
                        )
                        total = term if total is None else total + term
            pre[t] = total if c == 0 else pre[t] + total
            return carry

        lax.fori_loop(0, 2, tile, 0)

    def activate(t, carry):
        scale = jnp.concatenate(
            [jnp.sum(scales[2 * t + n], axis=0)[0:1] for n in range(2)], axis=1
        )
        gate = pre[t, : 2 * units] * scale
        up = pre[t, 2 * units :] * scale
        value = gate / (1.0 + jnp.exp(-gate)) * up
        act[pl.ds(pl.multiple_of(t * 256, 256), 256), :] = value.T.astype(BF16)
        return carry

    def multiply_out(c):
        def block(n, carry):
            column = pl.multiple_of((c * 4 + n) * WIDTH, WIDTH)
            value = jnp.dot(
                act[...], w_out[:, pl.ds(column, WIDTH)], preferred_element_type=F32
            )
            part[c, n // 2, n % 2] = value.astype(BF16).reshape(RING, RING, SLOTS, WIDTH)
            return carry

        lax.fori_loop(0, 4, block, 0)

    sent1, joined1, sent2, joined2, returned = {}, {}, {}, {}, {}

    def view1(c, h):
        if second[h] == "z":
            return lambda sub, at: part.at[c, h, sub, at]
        return lambda sub, at: part.at[c, h, sub, :, at]

    def view2(c, h):
        return lambda sub, at: mid.at[c, h, sub, at]

    def land1(c, h):
        return lambda i: in1.at[c, h, i]

    def land2(c, h):
        return lambda i: in2.at[c, h, i]

    def send_part(c):
        for h in range(2):
            sent1[c, h] = scatter(second[h], view1(c, h), land1(c, h))

    def join_part(c):
        for h in range(2):
            joined1[c, h] = join(
                second[h], view1(c, h), land1(c, h), lambda sub: comb1.at[c, h, sub], sent1[c, h]
            )

    def send_mid(c):
        for h in range(2):
            for sub in range(2):
                mid[c, h, sub] = total(
                    second[h], view1(c, h), land1(c, h), sent1[c, h], joined1[c, h], sub
                ).astype(BF16)
            sent2[c, h] = scatter(first[h], view2(c, h), land2(c, h))

    def join_mid(c):
        for h in range(2):
            joined2[c, h] = join(
                first[h], view2(c, h), land2(c, h), lambda sub: comb2.at[c, h, sub], sent2[c, h]
            )

    def send_home(c):
        for h in range(2):
            for sub in range(2):
                value = total(first[h], view2(c, h), land2(c, h), sent2[c, h], joined2[c, h], sub)
                for g in range(RING):
                    homebox[c, g, h, :, sub * WIDTH : (sub + 1) * WIDTH] = value[
                        8 * g : 8 * g + 8
                    ].astype(BF16)
        returned[c] = exchange(homebox.at[c], back.at[c])

    def finish(c):
        arrive(returned[c])
        for s in range(2):
            columns = slice((c * 2 + s) * half, (c * 2 + s + 1) * half)
            value = hidden[c, s]
            produced = stacked(back, c, s).astype(BF16)
            for column in range(2):
                fetched = jnp.dot(fetch[column], produced, preferred_element_type=F32)
                value = value + shares[:, column : column + 1] * fetched
            out[:, columns] = value.astype(BF16)

    load_proj(0)
    load_proj(1)
    project(0)
    pl.semaphore_wait(barrier, len(greeted))
    send_proj(0)
    scale_step = None
    for tick in range(1, CHUNKS + 6):
        if tick < CHUNKS:
            project(tick)
            send_proj(tick)
        if tick == 2:
            load_weights()
        if 0 <= tick - 4 < CHUNKS:
            gather_wide(tick - 4)
        if 0 <= tick - 3 < CHUNKS:
            gather_start(tick - 3)
        if 0 <= tick - 1 < CHUNKS:
            join_proj(tick - 1)
        if 0 <= tick - 3 < CHUNKS:
            gather_pass(tick - 3)
        if 0 <= tick - 2 < CHUNKS:
            dispatch(tick - 2)
            if tick - 2 == CHUNKS - 1:
                scale_step = send_scales()
        if 0 <= tick - 5 < CHUNKS:
            gather_wide_pass(tick - 5)
        if tick - 2 == CHUNKS:
            shared = share_scales(scale_step)
        done = tick - 6
        if 0 <= done < CHUNKS and done % 2 == 1 and done < CHUNKS - 1:
            multiply_in(done - 1)
    multiply_in(CHUNKS - 2)
    for copy in shared:
        copy.wait_recv()
    lax.fori_loop(0, 2, activate, 0)
    weights[2][0].wait()
    weights[2][1].wait_recv()
    copies.finish()
    for step in range(CHUNKS + 6):
        if step < CHUNKS:
            multiply_out(step)
            send_part(step)
        if 0 <= step - 2 < CHUNKS:
            join_part(step - 2)
        if 0 <= step - 3 < CHUNKS:
            send_mid(step - 3)
        if 0 <= step - 4 < CHUNKS:
            join_mid(step - 4)
        if 0 <= step - 5 < CHUNKS:
            send_home(step - 5)
        if 0 <= step - 6 < CHUNKS:
            finish(step - 6)
    copies.finish()


def layer_tail(settled, out_proj, residual, norm_gain, pick, fetch, shares, w_gate, w_up, w_down):
    units, width = w_gate.shape
    group_rows = residual.shape[0]
    depth = settled.shape[1]
    half = 2 * WIDTH
    count = CHUNKS * (6 + 3 + 3 + 16 + 24) + 3 + 15 + 3
    whole = (CHUNKS, 2, 2, RING, RING, SLOTS, WIDTH)
    box = (CHUNKS, RING, 2, SLOTS // RING, half)
    vmem = pl.BlockSpec(memory_space=pltpu.VMEM)
    anywhere = pl.BlockSpec(memory_space=pl.ANY)
    return pl.pallas_call(
        layer_kernel,
        out_shape=jax.ShapeDtypeStruct(residual.shape, BF16),
        in_specs=[vmem, anywhere, vmem, vmem, vmem, vmem, vmem] + [anywhere] * 3,
        out_specs=vmem,
        scratch_shapes=[
            pltpu.VMEM((2, depth, 4 * WIDTH), BF16),
            pltpu.VMEM((CHUNKS, 2, RING, group_rows, half), BF16),
            pltpu.VMEM((CHUNKS, 6, group_rows, half), BF16),
            pltpu.VMEM((CHUNKS, 2, group_rows, half), BF16),
            pltpu.VMEM((CHUNKS, 2, group_rows, half), F32),
            pltpu.VMEM((group_rows, 128), F32),
            pltpu.VMEM(box, BF16),
            pltpu.VMEM(box, BF16),
            pltpu.VMEM((RING, SLOTS // RING, 128), F32),
            pltpu.VMEM((RING, SLOTS // RING, 128), F32),
            pltpu.VMEM((RING, RING, 8, 128), F32),
            pltpu.VMEM(whole, BF16),
            pltpu.VMEM((4 * units, width), BF16),
            pltpu.VMEM((2 * units, width), BF16),
            pltpu.VMEM((2, 4 * units, 256), F32),
            pltpu.VMEM((RING * RING * SLOTS, 2 * units), BF16),
            pltpu.VMEM((CHUNKS, 2, 6, RING, SLOTS, WIDTH), BF16),
            pltpu.VMEM((CHUNKS, 2, 2, RING, SLOTS, WIDTH), BF16),
            pltpu.VMEM((CHUNKS, 2, 2, RING, SLOTS, WIDTH), BF16),
            pltpu.VMEM((CHUNKS, 2, 6, SLOTS, WIDTH), BF16),
            pltpu.VMEM((CHUNKS, 2, 2, SLOTS, WIDTH), BF16),
            pltpu.VMEM(box, BF16),
            pltpu.VMEM(box, BF16),
            pltpu.SemaphoreType.DMA((count,)),
            pltpu.SemaphoreType.DMA((count,)),
            pltpu.SemaphoreType.DMA((3 * CHUNKS + 4,)),
        ],
        compiler_params=pltpu.CompilerParams(
            collective_id=2, has_side_effects=True, vmem_limit_bytes=64000 * 1024
        ),
        name="layer_tail",
    )(
        settled, out_proj, residual, norm_gain.reshape(1, width), pick, fetch, shares,
        w_gate, w_up, w_down,
    )


def body(
    queries,
    key_rows,
    value_rows,
    gate_rows,
    decay_exp,
    attn_gain,
    out_proj,
    residual,
    norm_gain,
    routes,
    route_weights,
    w_gate,
    w_up,
    w_down,
):
    settled = attention(queries, key_rows, value_rows, gate_rows, decay_exp, attn_gain)
    span_rows = queries.shape[0]
    group_count = lax.axis_size("exp")
    group_rows = span_rows // group_count
    first_mine = lax.axis_index("exp") * group_rows
    capacity = group_rows // 8
    my_routes = lax.dynamic_slice_in_dim(routes, first_mine, group_rows, 0)
    my_weights = lax.dynamic_slice_in_dim(route_weights, first_mine, group_rows, 0)
    table = slot_table(my_routes, group_count, capacity)
    pick = table.reshape(group_count * capacity, group_rows)
    even = (jnp.arange(group_count * capacity) // capacity) % 2 == 0
    fetch = jnp.stack([pick.T & even, pick.T & ~even]).astype(BF16)
    return layer_tail(
        settled,
        out_proj,
        residual,
        norm_gain,
        pick.astype(BF16),
        fetch,
        my_weights,
        w_gate[0],
        w_up[0],
        w_down[0],
    )


def solution(mesh):
    in_specs = (
        P("ctx", "exp"),
        P("ctx", "exp"),
        P("ctx", "exp"),
        P("ctx", "exp"),
        P("exp"),
        P("exp"),
        P("exp", None),
        P(("ctx", "exp"), None),
        P(),
        P("ctx", None),
        P("ctx", None),
        P("exp", "ctx", None),
        P("exp", "ctx", None),
        P("exp", "ctx", None),
    )
    out_specs = P(("ctx", "exp"), None)
    return jax.shard_map(body, mesh=mesh, in_specs=in_specs, out_specs=out_specs, check_vma=False)
```

```python
import jax
import jax.numpy as jnp
from jax import lax
from jax.experimental import pallas as pl
from jax.experimental.pallas import tpu as pltpu
from jax.sharding import PartitionSpec as P

EPSILON = 1e-06
MESH = pl.DeviceIdType.MESH
BF16 = jnp.bfloat16
F32 = jnp.float32
RING = 4
CHUNKS = 6
WIDTH = 256
SLOTS = 32


def attend(
    meet, decay_exp, queries_hbm, keys_hbm, values_hbm, gates_hbm, attn_gain, settled,
    queries, key_rows, value_rows, gate_rows, update, gathered, prior, state, inner,
    send_sems, recv_sems, send_sems2, recv_sems2, local_sems,
):
    index, owner = lax.axis_index("ctx"), lax.axis_index("exp")
    size = gathered.shape[0]
    head_count = decay_exp.shape[0]
    row_count = queries.shape[0]
    head_width = queries.shape[1] // head_count

    loads = []
    for n, (source, target) in enumerate(
        (
            (keys_hbm, key_rows),
            (values_hbm, value_rows),
            (queries_hbm, queries),
            (gates_hbm, gate_rows),
        )
    ):
        loads.append(pltpu.make_async_copy(source, target, local_sems.at[2 + n]))
        loads[n].start()
    def rate_of(head, shape):
        exponent = jnp.full(shape, decay_exp[head].astype(F32), F32)
        return jnp.exp2(-exponent)

    def columns(head):
        return slice(head * head_width, (head + 1) * head_width)

    positions = lax.broadcasted_iota(jnp.int32, (row_count, head_width), 0).astype(F32)
    loads[0].wait()
    loads[1].wait()
    for head in range(head_count):
        rate = rate_of(head, (1, head_width))
        tail = jnp.exp(-rate * (row_count - 1.0 - positions))
        keyed = (key_rows[:, columns(head)].astype(F32) * tail).astype(BF16)
        product = lax.dot_general(
            keyed,
            value_rows[:, columns(head)],
            (((0,), (0,)), ((), ())),
            preferred_element_type=F32,
        )
        parts = size // head_count
        update[head * parts : (head + 1) * parts] = product.astype(BF16).reshape(
            parts, head_width // parts, head_width
        )
    meet()

    def exchange(source, target, send, recv):
        def copy(step):
            other = lax.rem(index + step, size)
            return pltpu.make_async_remote_copy(
                src_ref=source.at[other],
                dst_ref=target.at[index],
                send_sem=send.at[step - 1],
                recv_sem=recv.at[step - 1],
                device_id=(other, owner),
                device_id_type=MESH,
            )

        def start(step, carry):
            copy(step).start()
            return carry

        def arrive(step, carry):
            copy(step).wait_recv()
            return carry

        def leave(step, carry):
            copy(step).wait_send()
            return carry

        return (
            lambda: lax.fori_loop(1, size, start, 0),
            lambda: lax.fori_loop(1, size, arrive, 0),
            lambda: lax.fori_loop(1, size, leave, 0),
        )

    start, arrive, leave = exchange(update, gathered, send_sems, recv_sems)
    start()
    kept = pltpu.make_async_copy(update.at[index], gathered.at[index], local_sems.at[0])
    kept.start()

    def inside(head):
        rate = rate_of(head, (1, row_count))
        row = lax.broadcasted_iota(jnp.int32, (row_count, row_count), 0)
        column = lax.broadcasted_iota(jnp.int32, (row_count, row_count), 1)
        offset = (row - column).astype(F32)
        damping = jnp.where(offset >= 0.0, jnp.exp(-rate * jnp.maximum(offset, 0.0)), 0.0)
        scores = lax.dot_general(
            queries[:, columns(head)],
            key_rows[:, columns(head)],
            (((1,), (1,)), ((), ())),
            preferred_element_type=F32,
        )
        mixing = (scores * damping).astype(BF16)
        inner[head] = jnp.dot(mixing, value_rows[:, columns(head)], preferred_element_type=F32)

    loads[2].wait()
    loads[3].wait()
    for head in range(head_count // 2):
        inside(head)
    kept.wait()
    arrive()
    mine = index // (size // head_count)
    carry_decay = jnp.exp(-rate_of(mine, (1, head_width)) * float(row_count))
    running = jnp.zeros(gathered.shape[1:], F32)
    for block in range(size):
        prior[block] = running.astype(BF16)
        if block + 1 < size:
            running = carry_decay * running + gathered[block].astype(F32)
    start2, arrive2, leave2 = exchange(prior, state, send_sems2, recv_sems2)
    start2()
    kept2 = pltpu.make_async_copy(prior.at[index], state.at[index], local_sems.at[1])
    kept2.start()
    for head in range(head_count // 2, head_count):
        inside(head)
    leave()
    kept2.wait()
    arrive2()
    for head in range(head_count):
        rate = rate_of(head, (1, head_width))
        parts = size // head_count
        held = state[head * parts : (head + 1) * parts].reshape(head_width, head_width)
        reached = jnp.dot(queries[:, columns(head)], held, preferred_element_type=F32)
        mixed = inner[head] + reached * jnp.exp(-rate * (positions + 1.0))
        mean_square = jnp.mean(mixed * mixed, axis=1, keepdims=True)
        normed = mixed * lax.rsqrt(mean_square + EPSILON)
        gate = gate_rows[:, columns(head)].astype(F32)
        value = normed * attn_gain[:, columns(head)] * (1.0 / (1.0 + jnp.exp(-gate)))
        settled[:, columns(head)] = value.astype(BF16)
    leave2()


def place(index):
    return index // 8, (index // 2) % 4, index % 2


class Copies:
    def __init__(self, send_sems, recv_sems):
        self.send_sems, self.recv_sems = send_sems, recv_sems
        self.count, self.waiting = 0, []

    def start(self, source, target, device):
        copy = pltpu.make_async_remote_copy(
            src_ref=source,
            dst_ref=target,
            send_sem=self.send_sems.at[self.count],
            recv_sem=self.recv_sems.at[self.count],
            device_id=device,
            device_id_type=MESH,
        )
        copy.start()
        self.count += 1
        self.waiting.append(copy)
        return copy

    def finish(self):
        for copy in self.waiting:
            copy.wait_send()
        self.waiting = []


def layer_kernel(
    decay_exp, queries_hbm, keys_hbm, values_hbm, gates_hbm, attn_gain,
    out_proj, residual_hbm, norm_gain, routes, route_weights, w_gate, w_up, w_down, out,
    queries, key_rows, value_rows, gate_rows, update, gathered, prior, state, inner,
    state_sems, state_sems2, state_sems3, state_sems4, span_sems,
    settled, residual, pick, fetch, shares,
    proj_w, proj, in0, comb0, hidden, squares, outbox, inbox, scale_out, scale_in, scales,
    rows, w_in, w_out, pre, act, in1, comb1, mid, in2, comb2, homebox, back,
    send_sems, recv_sems, local_sems,
):
    index, owner = lax.axis_index("ctx"), lax.axis_index("exp")
    z, x, core = place(index)
    part = rows

    def device(zz, xx):
        return (zz * 8 + xx * 2 + core, owner)

    def beside(at):
        return lax.rem(at + RING - 1, RING), lax.rem(at + 1, RING), lax.rem(at + 2, RING)

    x_left, x_right, x_far = beside(x)
    z_left, z_right, z_far = beside(z)
    y_left, y_right, y_far = beside(owner)
    partner = (index + 1 - 2 * core, owner)
    near = {
        "x": (x, x_left, x_right, device(z, x_left), device(z, x_right), x_far),
        "z": (z, z_left, z_right, device(z_left, x), device(z_right, x), z_far),
        "y": (owner, y_left, y_right, (index, y_left), (index, y_right), y_far),
    }
    column_peers = [lax.rem(owner + step, RING) for step in range(1, RING)]
    plane_peers = [
        device(lax.rem(z + dz, RING), lax.rem(x + dx, RING))
        for dz in range(RING)
        for dx in range(RING)
        if dz or dx
    ]
    barrier = pltpu.get_barrier_semaphore()
    size = gathered.shape[0]

    def greet(step, carry):
        other = lax.rem(index + step, size)
        pl.semaphore_signal(barrier, inc=1, device_id=(other, owner), device_id_type=MESH)
        return carry

    lax.fori_loop(1, size, greet, 0)
    for other in column_peers:
        pl.semaphore_signal(barrier, inc=1, device_id=(index, other), device_id_type=MESH)
    copies = Copies(send_sems, recv_sems)
    local_count = [0]

    def local(source, target):
        copy = pltpu.make_async_copy(source, target, local_sems.at[local_count[0]])
        local_count[0] += 1
        copy.start()
        return copy

    units = w_gate.shape[0]
    piece_width = 4 * WIDTH
    half = 2 * WIDTH
    first, second = ("x", "z"), ("z", "x")
    both = slice(None)

    def scatter(axis, view, land):
        me, left, right, to_left, to_right, far = near[axis]
        return (
            copies.start(view(0, far), land(0), to_left),
            copies.start(view(1, far), land(1), to_right),
            copies.start(view(0, right), land(2), to_right),
            copies.start(view(1, left), land(3), to_left),
        )

    def join(axis, view, land, stage, sent):
        me, left, right, to_left, to_right, far = near[axis]
        joined = []
        for sub, at, to in ((0, left, to_left), (1, right, to_right)):
            sent[sub].wait_recv()
            stage(sub)[...] = (
                land(sub)[...].astype(F32) + view(sub, at)[...].astype(F32)
            ).astype(BF16)
            joined.append(copies.start(stage(sub), land(4 + sub), to))
        return joined

    def total(axis, view, land, sent, joined, sub):
        me = near[axis][0]
        sent[2 + sub].wait_recv()
        joined[sub].wait_recv()
        return (
            view(sub, me)[...].astype(F32)
            + land(2 + sub)[...].astype(F32)
            + land(4 + sub)[...].astype(F32)
        )

    def tables():
        group_rows = residual.shape[0]
        row_count = routes.shape[1]
        slot = lax.broadcasted_iota(jnp.int32, (SLOTS, row_count), 0)
        place_of = lax.broadcasted_iota(jnp.int32, (SLOTS, row_count), 1)
        expert = slot // 8
        chosen = jnp.where(expert % 2 == 0, routes[0:1, :], routes[1:2, :])
        picked = (chosen == expert) & (place_of // group_rows == owner)
        before = lax.broadcasted_iota(jnp.int32, (row_count, row_count), 0)
        after = lax.broadcasted_iota(jnp.int32, (row_count, row_count), 1)
        upto = jnp.where(before <= after, 1.0, 0.0).astype(BF16)
        rank = jnp.dot(
            jnp.where(picked, 1.0, 0.0).astype(BF16), upto, preferred_element_type=F32
        )
        chosen_slot = picked & (rank == (slot % 8 + 1).astype(F32))
        mine = lax.broadcasted_iota(jnp.int32, (group_rows, row_count), 1)
        mine = mine == owner * group_rows + lax.broadcasted_iota(
            jnp.int32, (group_rows, row_count), 0
        )
        mine_rows = jnp.where(mine, 1.0, 0.0).astype(BF16)

        def across(left, right):
            return lax.dot_general(
                left, right, (((1,), (1,)), ((), ())), preferred_element_type=F32
            ).astype(BF16)

        pick[...] = across(jnp.where(chosen_slot, 1.0, 0.0).astype(BF16), mine_rows)
        for column in range(2):
            table = chosen_slot & (expert % 2 == column)
            fetch[column] = across(mine_rows, jnp.where(table, 1.0, 0.0).astype(BF16))
            share = jnp.sum(
                jnp.where(mine, route_weights[column : column + 1, :], 0.0), axis=1, keepdims=True
            )
            shares[column] = jnp.broadcast_to(share, shares.shape[1:])

    loads = {}

    def load_proj(c):
        loads[c] = local(out_proj.at[:, pl.ds(c * piece_width, piece_width)], proj_w.at[c % 2])

    def project(c):
        loads[c].wait()
        for s in range(2):
            value = jnp.dot(
                settled[...],
                proj_w[c % 2, :, s * half : (s + 1) * half],
                preferred_element_type=F32,
            )
            proj[c, s] = value.astype(BF16).reshape(RING, -1, half)
        if c + 2 < CHUNKS:
            load_proj(c + 2)

    sent0, joined0, dispatched = {}, {}, {}

    def view0(c):
        return lambda sub, at: proj.at[c, sub, at]

    def land0(c):
        return lambda i: in0.at[c, i]

    def send_proj(c):
        sent0[c] = scatter("y", view0(c), land0(c))

    def join_proj(c):
        joined0[c] = join("y", view0(c), land0(c), lambda sub: comb0.at[c, sub], sent0[c])

    def exchange(box, landing):
        sent = [
            copies.start(box.at[other], landing.at[owner], (index, other))
            for other in column_peers
        ]
        return sent, local(box.at[owner], landing.at[owner])

    def arrive(exchanged):
        for copy in exchanged[0]:
            copy.wait_recv()
        exchanged[1].wait()

    def stacked(box, *place):
        return jnp.concatenate(
            [box[(*place[:1], e, *place[1:])].astype(F32) for e in range(RING)], axis=0
        )

    def dispatch(c):
        for s in range(2):
            columns = slice((c * 2 + s) * half, (c * 2 + s + 1) * half)
            value = total("y", view0(c), land0(c), sent0[c], joined0[c], s)
            value = value + residual[:, columns].astype(F32)
            hidden[c, s] = value
            square = value * value
            folded = square[:, :128]
            for lane in range(128, half, 128):
                folded = folded + square[:, lane : lane + 128]
            if c == 0 and s == 0:
                squares[...] = folded
            else:
                squares[...] = squares[...] + folded
            scaled = (value * norm_gain[:, columns]).astype(BF16)
            picked = jnp.dot(pick[...], scaled, preferred_element_type=F32)
            for e in range(RING):
                outbox[c, e, s] = picked[8 * e : 8 * e + 8].astype(BF16)
        dispatched[c] = exchange(outbox.at[c], inbox.at[c])

    def send_scales():
        mean_square = jnp.sum(squares[...], axis=1, keepdims=True) / (CHUNKS * piece_width)
        inverse = jnp.broadcast_to(lax.rsqrt(mean_square + EPSILON), squares.shape)
        picked = jnp.dot(
            pick[...].astype(F32),
            inverse,
            precision=lax.Precision.HIGHEST,
            preferred_element_type=F32,
        )
        for e in range(RING):
            scale_out[e] = picked[8 * e : 8 * e + 8]
        return exchange(scale_out, scale_in)

    def share_scales(exchanged):
        arrive(exchanged)
        mine = jnp.concatenate([scale_in[e] for e in range(RING)], axis=0)
        row = lax.broadcasted_iota(jnp.int32, (SLOTS, 128), 0)
        lane = lax.broadcasted_iota(jnp.int32, (SLOTS, 128), 1)
        line = jnp.sum(jnp.where(lane == x * SLOTS + row, mine, 0.0), axis=0, keepdims=True)
        scales[z, x] = jnp.broadcast_to(line, (8, 128))
        return [copies.start(scales.at[z, x], scales.at[z, x], other) for other in plane_peers]

    gather1, relay1, gather2, relay2 = {}, {}, {}, {}

    def line_of(c, h, stage, sub, at):
        axis = (first if stage == 1 else second)[h]
        if stage == 1:
            return rows.at[c, h, sub, at, x] if axis == "z" else rows.at[c, h, sub, z, at]
        return rows.at[c, h, sub, at] if axis == "z" else rows.at[c, h, sub, :, at]

    def spread(c, h, stage, started):
        me, left, right, to_left, to_right, far = near[(first if stage == 1 else second)[h]]
        mine = line_of(c, h, stage, both, me)
        started[c, h] = (copies.start(mine, mine, to_right), copies.start(mine, mine, to_left))

    def pass_on(c, h, stage, started, passed):
        me, left, right, to_left, to_right, far = near[(first if stage == 1 else second)[h]]
        from_left, from_right = started[c, h]
        from_left.wait_recv()
        source = line_of(c, h, stage, 0, left)
        one = copies.start(source, source, to_right)
        from_right.wait_recv()
        source = line_of(c, h, stage, 1, right)
        passed[c, h] = (one, copies.start(source, source, to_left))

    def gather_start(c):
        arrive(dispatched[c])
        for s in range(2):
            value = stacked(inbox, c, s).astype(BF16)
            for sub in range(2):
                rows[c, s, sub, z, x] = value[:, sub * WIDTH : (sub + 1) * WIDTH]
        for h in range(2):
            spread(c, h, 1, gather1)

    def gather_pass(c):
        for h in range(2):
            pass_on(c, h, 1, gather1, relay1)

    def gather_wide(c):
        for h in range(2):
            for copy in relay1[c, h]:
                copy.wait_recv()
            spread(c, h, 2, gather2)

    def gather_wide_pass(c):
        for h in range(2):
            pass_on(c, h, 2, gather2, relay2)

    weights = []

    def load_weights():
        for source, target, base in (
            (w_gate, w_in, 0),
            (w_up, w_in, 2 * units),
            (w_down, w_out, 0),
        ):
            kept = local(source, target.at[pl.ds(base, units)])
            sent = copies.start(source, target.at[pl.ds(base + units, units)], partner)
            weights.append((kept, sent))

    def multiply_in(c):
        for h in range(2):
            for copy in relay2[c, h]:
                copy.wait_recv()
        if c == 0:
            for n in range(2):
                weights[n][0].wait()
                weights[n][1].wait_recv()

        def tile(t, carry):
            total = None
            for h in range(2):
                for sub in range(2):
                    block = rows[c, h, sub, pl.ds(2 * t, 2)].reshape(256, WIDTH)
                    column = ((c * 2 + h) * 2 + sub) * WIDTH
                    term = lax.dot_general(
                        w_in[:, column : column + WIDTH],
                        block,
                        (((1,), (1,)), ((), ())),
                        preferred_element_type=F32,
                    )
                    total = term if total is None else total + term
            pre[t] = total if c == 0 else pre[t] + total
            return carry

        lax.fori_loop(0, 2, tile, 0)

    def activate(t, carry):
        scale = jnp.concatenate(
            [jnp.sum(scales[2 * t + n], axis=0)[0:1] for n in range(2)], axis=1
        )
        gate = pre[t, : 2 * units] * scale
        up = pre[t, 2 * units :] * scale
        value = gate / (1.0 + jnp.exp(-gate)) * up
        act[pl.ds(pl.multiple_of(t * 256, 256), 256), :] = value.T.astype(BF16)
        return carry

    def multiply_out(c):
        def block(n, carry):
            column = pl.multiple_of((c * 4 + n) * WIDTH, WIDTH)
            value = jnp.dot(
                act[...], w_out[:, pl.ds(column, WIDTH)], preferred_element_type=F32
            )
            part[c, n // 2, n % 2] = value.astype(BF16).reshape(RING, RING, SLOTS, WIDTH)
            return carry

        lax.fori_loop(0, 4, block, 0)

    sent1, joined1, sent2, joined2, returned = {}, {}, {}, {}, {}

    def view1(c, h):
        if second[h] == "z":
            return lambda sub, at: part.at[c, h, sub, at]
        return lambda sub, at: part.at[c, h, sub, :, at]

    def view2(c, h):
        return lambda sub, at: mid.at[c, h, sub, at]

    def land1(c, h):
        return lambda i: in1.at[c, h, i]

    def land2(c, h):
        return lambda i: in2.at[c, h, i]

    def send_part(c):
        for h in range(2):
            sent1[c, h] = scatter(second[h], view1(c, h), land1(c, h))

    def join_part(c):
        for h in range(2):
            joined1[c, h] = join(
                second[h], view1(c, h), land1(c, h), lambda sub: comb1.at[c, h, sub], sent1[c, h]
            )

    def send_mid(c):
        for h in range(2):
            for sub in range(2):
                mid[c, h, sub] = total(
                    second[h], view1(c, h), land1(c, h), sent1[c, h], joined1[c, h], sub
                ).astype(BF16)
            sent2[c, h] = scatter(first[h], view2(c, h), land2(c, h))

    def join_mid(c):
        for h in range(2):
            joined2[c, h] = join(
                first[h], view2(c, h), land2(c, h), lambda sub: comb2.at[c, h, sub], sent2[c, h]
            )

    def send_home(c):
        for h in range(2):
            for sub in range(2):
                value = total(first[h], view2(c, h), land2(c, h), sent2[c, h], joined2[c, h], sub)
                for g in range(RING):
                    homebox[c, g, h, :, sub * WIDTH : (sub + 1) * WIDTH] = value[
                        8 * g : 8 * g + 8
                    ].astype(BF16)
        returned[c] = exchange(homebox.at[c], back.at[c])

    def finish(c):
        arrive(returned[c])
        for s in range(2):
            columns = slice((c * 2 + s) * half, (c * 2 + s + 1) * half)
            value = hidden[c, s]
            produced = stacked(back, c, s).astype(BF16)
            for column in range(2):
                fetched = jnp.dot(fetch[column], produced, preferred_element_type=F32)
                value = value + shares[column, :, 0:1] * fetched
            out[:, columns] = value.astype(BF16)

    load_proj(0)
    load_proj(1)
    residual_load = local(residual_hbm, residual)
    tables()

    def meet():
        pl.semaphore_wait(barrier, size - 1 + len(column_peers))
        load_weights()

    attend(
        meet, decay_exp, queries_hbm, keys_hbm, values_hbm, gates_hbm, attn_gain, settled,
        queries, key_rows, value_rows, gate_rows, update, gathered, prior, state, inner,
        state_sems, state_sems2, state_sems3, state_sems4, span_sems,
    )
    residual_load.wait()
    for step, c in (
        (project, 0), (send_proj, 0), (project, 1), (project, 2), (send_proj, 1),
        (join_proj, 0), (join_proj, 1), (project, 3), (send_proj, 2), (project, 4),
        (dispatch, 0), (dispatch, 1), (project, 5), (join_proj, 2), (send_proj, 3),
        (gather_start, 0), (gather_start, 1), (gather_pass, 0), (dispatch, 2), (gather_pass, 1),
        (send_proj, 4), (gather_wide, 0), (join_proj, 3), (gather_start, 2), (gather_wide, 1),
        (send_proj, 5), (join_proj, 4), (dispatch, 3), (gather_pass, 2), (join_proj, 5),
        (gather_wide_pass, 0), (gather_wide, 2), (gather_start, 3), (dispatch, 4),
        (gather_wide_pass, 1), (dispatch, 5),
    ):
        step(c)
    scale_step = send_scales()
    for step, c in (
        (gather_start, 4), (gather_pass, 3), (gather_wide_pass, 2), (gather_start, 5),
        (gather_pass, 4),
    ):
        step(c)
    shared = share_scales(scale_step)
    for step, c in (
        (gather_wide, 3), (multiply_in, 0), (gather_pass, 5), (gather_wide, 4),
        (gather_wide, 5), (multiply_in, 1), (gather_wide_pass, 3), (multiply_in, 2),
        (gather_wide_pass, 4), (gather_wide_pass, 5), (multiply_in, 3), (multiply_in, 4),
        (multiply_in, 5),
    ):
        step(c)
    for copy in shared:
        copy.wait_recv()
    lax.fori_loop(0, 2, activate, 0)
    weights[2][0].wait()
    weights[2][1].wait_recv()
    copies.finish()
    for step, c in (
        (multiply_out, 0), (send_part, 0), (multiply_out, 1), (send_part, 1), (multiply_out, 2),
        (send_part, 2), (multiply_out, 3), (join_part, 0), (multiply_out, 4), (multiply_out, 5),
        (send_part, 3), (join_part, 1), (send_part, 4), (send_part, 5), (join_part, 2),
        (join_part, 3), (join_part, 4), (join_part, 5), (send_mid, 0), (send_mid, 1),
        (send_mid, 2), (send_mid, 3), (send_mid, 4), (join_mid, 0), (send_mid, 5),
        (join_mid, 1), (join_mid, 2), (join_mid, 3), (join_mid, 4), (send_home, 0),
        (join_mid, 5), (send_home, 1), (send_home, 2), (send_home, 3), (send_home, 4),
        (send_home, 5), (finish, 0), (finish, 1), (finish, 2), (finish, 3), (finish, 4),
        (finish, 5),
    ):
        step(c)
    copies.finish()


def layer(
    queries, key_rows, value_rows, gate_rows, decay_exp, attn_gain, out_proj, residual,
    norm_gain, routes, route_weights, w_gate, w_up, w_down,
):
    units, width = w_gate.shape
    group_rows = residual.shape[0]
    row_count, depth = queries.shape
    head_count = decay_exp.shape[0]
    head_width = depth // head_count
    size = lax.axis_size("ctx")
    states = pltpu.VMEM((size, head_count * head_width // size, head_width), BF16)
    state_sems = pltpu.SemaphoreType.DMA((size - 1,))
    span = pltpu.VMEM(queries.shape, BF16)
    half = 2 * WIDTH
    count = CHUNKS * (6 + 3 + 3 + 16 + 24) + 3 + 15 + 3
    whole = (CHUNKS, 2, 2, RING, RING, SLOTS, WIDTH)
    box = (CHUNKS, RING, 2, SLOTS // RING, half)
    vmem = pl.BlockSpec(memory_space=pltpu.VMEM)
    anywhere = pl.BlockSpec(memory_space=pl.ANY)
    return pl.pallas_call(
        layer_kernel,
        out_shape=jax.ShapeDtypeStruct(residual.shape, BF16),
        in_specs=[pl.BlockSpec(memory_space=pltpu.SMEM)]
        + [anywhere] * 4
        + [vmem, anywhere, anywhere, vmem, vmem, vmem]
        + [anywhere] * 3,
        out_specs=vmem,
        scratch_shapes=[span] * 4
        + [states] * 4
        + [pltpu.VMEM((head_count, row_count, head_width), F32)]
        + [state_sems] * 4
        + [
            pltpu.SemaphoreType.DMA((6,)),
            span,
            pltpu.VMEM(residual.shape, BF16),
            pltpu.VMEM((SLOTS, group_rows), BF16),
            pltpu.VMEM((2, group_rows, SLOTS), BF16),
            pltpu.VMEM((2, group_rows, 128), F32),
            pltpu.VMEM((2, depth, 4 * WIDTH), BF16),
            pltpu.VMEM((CHUNKS, 2, RING, group_rows, half), BF16),
            pltpu.VMEM((CHUNKS, 6, group_rows, half), BF16),
            pltpu.VMEM((CHUNKS, 2, group_rows, half), BF16),
            pltpu.VMEM((CHUNKS, 2, group_rows, half), F32),
            pltpu.VMEM((group_rows, 128), F32),
            pltpu.VMEM(box, BF16),
            pltpu.VMEM(box, BF16),
            pltpu.VMEM((RING, SLOTS // RING, 128), F32),
            pltpu.VMEM((RING, SLOTS // RING, 128), F32),
            pltpu.VMEM((RING, RING, 8, 128), F32),
            pltpu.VMEM(whole, BF16),
            pltpu.VMEM((4 * units, width), BF16),
            pltpu.VMEM((2 * units, width), BF16),
            pltpu.VMEM((2, 4 * units, 256), F32),
            pltpu.VMEM((RING * RING * SLOTS, 2 * units), BF16),
            pltpu.VMEM((CHUNKS, 2, 6, RING, SLOTS, WIDTH), BF16),
            pltpu.VMEM((CHUNKS, 2, 2, RING, SLOTS, WIDTH), BF16),
            pltpu.VMEM((CHUNKS, 2, 2, RING, SLOTS, WIDTH), BF16),
            pltpu.VMEM((CHUNKS, 2, 6, SLOTS, WIDTH), BF16),
            pltpu.VMEM((CHUNKS, 2, 2, SLOTS, WIDTH), BF16),
            pltpu.VMEM(box, BF16),
            pltpu.VMEM(box, BF16),
            pltpu.SemaphoreType.DMA((count,)),
            pltpu.SemaphoreType.DMA((count,)),
            pltpu.SemaphoreType.DMA((3 * CHUNKS + 5,)),
        ],
        compiler_params=pltpu.CompilerParams(
            collective_id=2, has_side_effects=True, vmem_limit_bytes=64000 * 1024
        ),
        name="layer",
    )(
        decay_exp, queries, key_rows, value_rows, gate_rows, attn_gain.reshape(1, depth),
        out_proj, residual, norm_gain.reshape(1, width), routes.T, route_weights.T,
        w_gate, w_up, w_down,
    )


def body(
    queries,
    key_rows,
    value_rows,
    gate_rows,
    decay_exp,
    attn_gain,
    out_proj,
    residual,
    norm_gain,
    routes,
    route_weights,
    w_gate,
    w_up,
    w_down,
):
    return layer(
        queries,
        key_rows,
        value_rows,
        gate_rows,
        decay_exp,
        attn_gain,
        out_proj,
        residual,
        norm_gain,
        routes,
        route_weights,
        w_gate[0],
        w_up[0],
        w_down[0],
    )


def solution(mesh):
    in_specs = (
        P("ctx", "exp"),
        P("ctx", "exp"),
        P("ctx", "exp"),
        P("ctx", "exp"),
        P("exp"),
        P("exp"),
        P("exp", None),
        P(("ctx", "exp"), None),
        P(),
        P("ctx", None),
        P("ctx", None),
        P("exp", "ctx", None),
        P("exp", "ctx", None),
        P("exp", "ctx", None),
    )
    out_specs = P(("ctx", "exp"), None)
    return jax.shard_map(body, mesh=mesh, in_specs=in_specs, out_specs=out_specs, check_vma=False)
```

```python
import jax
import jax.numpy as jnp
from jax import lax
from jax.experimental import pallas as pl
from jax.experimental.pallas import tpu as pltpu
from jax.sharding import PartitionSpec as P

EPSILON = 1e-06
MESH = pl.DeviceIdType.MESH
BF16 = jnp.bfloat16
F32 = jnp.float32
RING = 4
CHUNKS = 6
WIDTH = 256
SLOTS = 32


def attend(
    meet, decay_exp, queries_hbm, keys_hbm, values_hbm, gates_hbm, attn_gain, settled,
    queries, key_rows, value_rows, gate_rows, update, gathered, prior, state, inner, factor,
    send_sems, recv_sems, send_sems2, recv_sems2, local_sems,
):
    index, owner = lax.axis_index("ctx"), lax.axis_index("exp")
    size = gathered.shape[0]
    head_count = decay_exp.shape[0]
    row_count = queries.shape[0]
    head_width = queries.shape[1] // head_count

    loads = []
    for n, (source, target) in enumerate(
        (
            (keys_hbm, key_rows),
            (values_hbm, value_rows),
            (queries_hbm, queries),
            (gates_hbm, gate_rows),
        )
    ):
        loads.append(pltpu.make_async_copy(source, target, local_sems.at[2 + n]))
        loads[n].start()
    def rate_of(head, shape):
        exponent = jnp.full(shape, decay_exp[head].astype(F32), F32)
        return jnp.exp2(-exponent)

    def columns(head):
        return slice(head * head_width, (head + 1) * head_width)

    positions = lax.broadcasted_iota(jnp.int32, (row_count, head_width), 0).astype(F32)
    loads[0].wait()
    loads[1].wait()
    for head in range(head_count):
        rate = rate_of(head, (1, head_width))
        tail = jnp.exp(-rate * (row_count - 1.0 - positions))
        keyed = (key_rows[:, columns(head)].astype(F32) * tail).astype(BF16)
        product = lax.dot_general(
            keyed,
            value_rows[:, columns(head)],
            (((0,), (0,)), ((), ())),
            preferred_element_type=F32,
        )
        parts = size // head_count
        update[head * parts : (head + 1) * parts] = product.astype(BF16).reshape(
            parts, head_width // parts, head_width
        )
    meet()

    def exchange(source, target, send, recv):
        def copy(step):
            other = lax.rem(index + step, size)
            return pltpu.make_async_remote_copy(
                src_ref=source.at[other],
                dst_ref=target.at[index],
                send_sem=send.at[step - 1],
                recv_sem=recv.at[step - 1],
                device_id=(other, owner),
                device_id_type=MESH,
            )

        def start(step, carry):
            copy(step).start()
            return carry

        def arrive(step, carry):
            copy(step).wait_recv()
            return carry

        def leave(step, carry):
            copy(step).wait_send()
            return carry

        return (
            lambda: lax.fori_loop(1, size, start, 0),
            lambda: lax.fori_loop(1, size, arrive, 0),
            lambda: lax.fori_loop(1, size, leave, 0),
        )

    start, arrive, leave = exchange(update, gathered, send_sems, recv_sems)
    start()
    kept = pltpu.make_async_copy(update.at[index], gathered.at[index], local_sems.at[0])
    kept.start()

    def inside(head):
        rate = rate_of(head, (1, row_count))
        row = lax.broadcasted_iota(jnp.int32, (row_count, row_count), 0)
        column = lax.broadcasted_iota(jnp.int32, (row_count, row_count), 1)
        offset = (row - column).astype(F32)
        damping = jnp.where(offset >= 0.0, jnp.exp(-rate * jnp.maximum(offset, 0.0)), 0.0)
        scores = lax.dot_general(
            queries[:, columns(head)],
            key_rows[:, columns(head)],
            (((1,), (1,)), ((), ())),
            preferred_element_type=F32,
        )
        mixing = (scores * damping).astype(BF16)
        inner[head] = jnp.dot(mixing, value_rows[:, columns(head)], preferred_element_type=F32)
        gate = gate_rows[:, columns(head)].astype(F32)
        factor[head] = attn_gain[:, columns(head)] / (1.0 + jnp.exp(-gate))

    loads[2].wait()
    loads[3].wait()
    for head in range(head_count // 2):
        inside(head)
    kept.wait()
    arrive()
    mine = index // (size // head_count)
    carry_decay = jnp.exp(-rate_of(mine, (1, head_width)) * float(row_count))
    running = jnp.zeros(gathered.shape[1:], F32)
    for block in range(size):
        prior[block] = running.astype(BF16)
        if block + 1 < size:
            running = carry_decay * running + gathered[block].astype(F32)
    start2, arrive2, leave2 = exchange(prior, state, send_sems2, recv_sems2)
    start2()
    kept2 = pltpu.make_async_copy(prior.at[index], state.at[index], local_sems.at[1])
    kept2.start()
    for head in range(head_count // 2, head_count):
        inside(head)
    leave()
    kept2.wait()
    arrive2()
    for head in range(head_count):
        rate = rate_of(head, (1, head_width))
        parts = size // head_count
        held = state[head * parts : (head + 1) * parts].reshape(head_width, head_width)
        reached = jnp.dot(queries[:, columns(head)], held, preferred_element_type=F32)
        mixed = inner[head] + reached * jnp.exp(-rate * (positions + 1.0))
        mean_square = jnp.mean(mixed * mixed, axis=1, keepdims=True)
        normed = mixed * lax.rsqrt(mean_square + EPSILON)
        settled[:, columns(head)] = (normed * factor[head]).astype(BF16)
    leave2()


def place(index):
    return index // 8, (index // 2) % 4, index % 2


class Copies:
    def __init__(self, send_sems, recv_sems):
        self.send_sems, self.recv_sems = send_sems, recv_sems
        self.count, self.waiting = 0, []

    def start(self, source, target, device):
        copy = pltpu.make_async_remote_copy(
            src_ref=source,
            dst_ref=target,
            send_sem=self.send_sems.at[self.count],
            recv_sem=self.recv_sems.at[self.count],
            device_id=device,
            device_id_type=MESH,
        )
        copy.start()
        self.count += 1
        self.waiting.append(copy)
        return copy

    def finish(self):
        for copy in self.waiting:
            copy.wait_send()
        self.waiting = []


def layer_kernel(
    decay_exp, queries_hbm, keys_hbm, values_hbm, gates_hbm, attn_gain,
    out_proj, residual_hbm, norm_gain, routes, route_weights, w_gate, w_up, w_down, out,
    queries, key_rows, value_rows, gate_rows, update, gathered, prior, state, inner, factor,
    state_sems, state_sems2, state_sems3, state_sems4, span_sems,
    settled, residual, pick, fetch, shares,
    proj_w, proj, in0, comb0, hidden, squares, outbox, inbox, scale_out, scale_in, scales,
    rows, w_in, w_out, pre, act, in1, comb1, mid, in2, homebox, back,
    send_sems, recv_sems, local_sems,
):
    index, owner = lax.axis_index("ctx"), lax.axis_index("exp")
    z, x, core = place(index)
    part = rows

    def device(zz, xx):
        return (zz * 8 + xx * 2 + core, owner)

    def beside(at):
        return lax.rem(at + RING - 1, RING), lax.rem(at + 1, RING), lax.rem(at + 2, RING)

    x_left, x_right, x_far = beside(x)
    z_left, z_right, z_far = beside(z)
    y_left, y_right, y_far = beside(owner)
    partner = (index + 1 - 2 * core, owner)
    near = {
        "x": (x, x_left, x_right, device(z, x_left), device(z, x_right), x_far),
        "z": (z, z_left, z_right, device(z_left, x), device(z_right, x), z_far),
        "y": (owner, y_left, y_right, (index, y_left), (index, y_right), y_far),
    }
    column_peers = [lax.rem(owner + step, RING) for step in range(1, RING)]
    plane_peers = [
        device(lax.rem(z + dz, RING), lax.rem(x + dx, RING))
        for dz in range(RING)
        for dx in range(RING)
        if dz or dx
    ]
    barrier = pltpu.get_barrier_semaphore()
    size = gathered.shape[0]

    def greet(step, carry):
        other = lax.rem(index + step, size)
        pl.semaphore_signal(barrier, inc=1, device_id=(other, owner), device_id_type=MESH)
        return carry

    lax.fori_loop(1, size, greet, 0)
    for other in column_peers:
        pl.semaphore_signal(barrier, inc=1, device_id=(index, other), device_id_type=MESH)
    copies = Copies(send_sems, recv_sems)
    local_count = [0]

    def local(source, target):
        copy = pltpu.make_async_copy(source, target, local_sems.at[local_count[0]])
        local_count[0] += 1
        copy.start()
        return copy

    units = w_gate.shape[0]
    piece_width = 4 * WIDTH
    half = 2 * WIDTH
    first, second = ("x", "z"), ("z", "x")
    both = slice(None)

    def scatter(axis, view, land):
        me, left, right, to_left, to_right, far = near[axis]
        return (
            copies.start(view(0, far), land(0), to_left),
            copies.start(view(1, far), land(1), to_right),
            copies.start(view(0, right), land(2), to_right),
            copies.start(view(1, left), land(3), to_left),
        )

    def join(axis, view, land, stage, sent):
        me, left, right, to_left, to_right, far = near[axis]
        joined = []
        for sub, at, to in ((0, left, to_left), (1, right, to_right)):
            sent[sub].wait_recv()
            stage(sub)[...] = (
                land(sub)[...].astype(F32) + view(sub, at)[...].astype(F32)
            ).astype(BF16)
            joined.append(copies.start(stage(sub), land(4 + sub), to))
        return joined

    def scatter_direct(axis, view, land):
        me, left, right, to_left, to_right, far = near[axis]
        to_far = device(z, x_far) if axis == "x" else device(z_far, x)
        return (
            copies.start(view(0, far), land(4), to_far),
            copies.start(view(1, far), land(5), to_far),
            copies.start(view(0, right), land(2), to_right),
            copies.start(view(1, left), land(3), to_left),
            copies.start(view(0, left), land(0), to_left),
            copies.start(view(1, right), land(1), to_right),
        )

    def total_direct(axis, view, land, sent, sub):
        value = view(sub, near[axis][0])[...].astype(F32)
        for n, i in ((4 + sub, sub), (2 + sub, 2 + sub), (sub, 4 + sub)):
            sent[n].wait_recv()
            value = value + land(i)[...].astype(F32)
        return value

    def total(axis, view, land, sent, joined, sub):
        me = near[axis][0]
        sent[2 + sub].wait_recv()
        joined[sub].wait_recv()
        return (
            view(sub, me)[...].astype(F32)
            + land(2 + sub)[...].astype(F32)
            + land(4 + sub)[...].astype(F32)
        )

    def tables():
        group_rows = residual.shape[0]
        row_count = routes.shape[1]
        slot = lax.broadcasted_iota(jnp.int32, (SLOTS, row_count), 0)
        place_of = lax.broadcasted_iota(jnp.int32, (SLOTS, row_count), 1)
        expert = slot // 8
        chosen = jnp.where(expert % 2 == 0, routes[0:1, :], routes[1:2, :])
        picked = (chosen == expert) & (place_of // group_rows == owner)
        before = lax.broadcasted_iota(jnp.int32, (row_count, row_count), 0)
        after = lax.broadcasted_iota(jnp.int32, (row_count, row_count), 1)
        upto = jnp.where(before <= after, 1.0, 0.0).astype(BF16)
        rank = jnp.dot(
            jnp.where(picked, 1.0, 0.0).astype(BF16), upto, preferred_element_type=F32
        )
        chosen_slot = picked & (rank == (slot % 8 + 1).astype(F32))
        mine = lax.broadcasted_iota(jnp.int32, (group_rows, row_count), 1)
        mine = mine == owner * group_rows + lax.broadcasted_iota(
            jnp.int32, (group_rows, row_count), 0
        )
        mine_rows = jnp.where(mine, 1.0, 0.0).astype(BF16)

        def across(left, right):
            return lax.dot_general(
                left, right, (((1,), (1,)), ((), ())), preferred_element_type=F32
            ).astype(BF16)

        pick[...] = across(jnp.where(chosen_slot, 1.0, 0.0).astype(BF16), mine_rows)
        for column in range(2):
            table = chosen_slot & (expert % 2 == column)
            fetch[column] = across(mine_rows, jnp.where(table, 1.0, 0.0).astype(BF16))
            share = jnp.sum(
                jnp.where(mine, route_weights[column : column + 1, :], 0.0), axis=1, keepdims=True
            )
            shares[column] = jnp.broadcast_to(share, shares.shape[1:])

    loads = {}

    def load_proj(c):
        loads[c] = local(out_proj.at[:, pl.ds(c * piece_width, piece_width)], proj_w.at[c % 2])

    def project(c):
        loads[c].wait()
        for s in range(2):
            value = jnp.dot(
                settled[...],
                proj_w[c % 2, :, s * half : (s + 1) * half],
                preferred_element_type=F32,
            )
            proj[c, s] = value.astype(BF16).reshape(RING, -1, half)
        if c + 2 < CHUNKS:
            load_proj(c + 2)

    sent0, joined0, dispatched = {}, {}, {}

    def view0(c):
        return lambda sub, at: proj.at[c, sub, at]

    def land0(c):
        return lambda i: in0.at[c, i]

    def send_proj(c):
        sent0[c] = scatter("y", view0(c), land0(c))

    def join_proj(c):
        joined0[c] = join("y", view0(c), land0(c), lambda sub: comb0.at[c, sub], sent0[c])

    def exchange(box, landing):
        sent = [
            copies.start(box.at[other], landing.at[owner], (index, other))
            for other in column_peers
        ]
        return sent, local(box.at[owner], landing.at[owner])

    def arrive(exchanged):
        for copy in exchanged[0]:
            copy.wait_recv()
        exchanged[1].wait()

    def stacked(box, *place):
        return jnp.concatenate(
            [box[(*place[:1], e, *place[1:])].astype(F32) for e in range(RING)], axis=0
        )

    def dispatch(c):
        for s in range(2):
            columns = slice((c * 2 + s) * half, (c * 2 + s + 1) * half)
            value = total("y", view0(c), land0(c), sent0[c], joined0[c], s)
            value = value + residual[:, columns].astype(F32)
            hidden[c, s] = value
            square = value * value
            folded = square[:, :128]
            for lane in range(128, half, 128):
                folded = folded + square[:, lane : lane + 128]
            if c == 0 and s == 0:
                squares[...] = folded
            else:
                squares[...] = squares[...] + folded
            scaled = (value * norm_gain[:, columns]).astype(BF16)
            picked = jnp.dot(pick[...], scaled, preferred_element_type=F32)
            for e in range(RING):
                outbox[c, e, s] = picked[8 * e : 8 * e + 8].astype(BF16)
        dispatched[c] = exchange(outbox.at[c], inbox.at[c])

    def send_scales():
        mean_square = jnp.sum(squares[...], axis=1, keepdims=True) / (CHUNKS * piece_width)
        inverse = jnp.broadcast_to(lax.rsqrt(mean_square + EPSILON), squares.shape)
        picked = jnp.dot(
            pick[...].astype(F32),
            inverse,
            precision=lax.Precision.HIGHEST,
            preferred_element_type=F32,
        )
        for e in range(RING):
            scale_out[e] = picked[8 * e : 8 * e + 8]
        return exchange(scale_out, scale_in)

    def share_scales(exchanged):
        arrive(exchanged)
        mine = jnp.concatenate([scale_in[e] for e in range(RING)], axis=0)
        row = lax.broadcasted_iota(jnp.int32, (SLOTS, 128), 0)
        lane = lax.broadcasted_iota(jnp.int32, (SLOTS, 128), 1)
        line = jnp.sum(jnp.where(lane == x * SLOTS + row, mine, 0.0), axis=0, keepdims=True)
        scales[z, x] = jnp.broadcast_to(line, (8, 128))
        return [copies.start(scales.at[z, x], scales.at[z, x], other) for other in plane_peers]

    gather1, gather2, relay2 = {}, {}, {}

    def line_of(c, h, stage, sub, at):
        axis = (first if stage == 1 else second)[h]
        if stage == 1:
            return rows.at[c, h, sub, at, x] if axis == "z" else rows.at[c, h, sub, z, at]
        return rows.at[c, h, sub, at] if axis == "z" else rows.at[c, h, sub, :, at]

    def spread(c, h, stage, started):
        me, left, right, to_left, to_right, far = near[(first if stage == 1 else second)[h]]
        mine = line_of(c, h, stage, both, me)
        sent = []
        if stage == 1:
            to_far = device(z, x_far) if first[h] == "x" else device(z_far, x)
            sent = [copies.start(mine, mine, to_far)]
        started[c, h] = [copies.start(mine, mine, to_right), copies.start(mine, mine, to_left)]
        started[c, h] += sent

    def pass_on(c, h, stage, started, passed):
        me, left, right, to_left, to_right, far = near[(first if stage == 1 else second)[h]]
        from_left, from_right = started[c, h]
        from_left.wait_recv()
        source = line_of(c, h, stage, 0, left)
        one = copies.start(source, source, to_right)
        from_right.wait_recv()
        source = line_of(c, h, stage, 1, right)
        passed[c, h] = (one, copies.start(source, source, to_left))

    def gather_start(c):
        arrive(dispatched[c])
        for s in range(2):
            value = stacked(inbox, c, s).astype(BF16)
            for sub in range(2):
                rows[c, s, sub, z, x] = value[:, sub * WIDTH : (sub + 1) * WIDTH]
        for h in range(2):
            spread(c, h, 1, gather1)

    def gather_wide(c):
        for h in range(2):
            for copy in gather1[c, h]:
                copy.wait_recv()
            spread(c, h, 2, gather2)

    def gather_wide_pass(c):
        for h in range(2):
            pass_on(c, h, 2, gather2, relay2)

    weights = []

    def load_weights():
        for source, target, base in (
            (w_gate, w_in, 0),
            (w_up, w_in, 2 * units),
            (w_down, w_out, 0),
        ):
            kept = local(source, target.at[pl.ds(base, units)])
            sent = copies.start(source, target.at[pl.ds(base + units, units)], partner)
            weights.append((kept, sent))

    def multiply_in(c):
        for h in range(2):
            for copy in relay2[c, h]:
                copy.wait_recv()
        if c == 0:
            for n in range(2):
                weights[n][0].wait()
                weights[n][1].wait_recv()

        def tile(t, carry):
            total = None
            for h in range(2):
                for sub in range(2):
                    block = rows[c, h, sub, pl.ds(2 * t, 2)].reshape(256, WIDTH)
                    column = ((c * 2 + h) * 2 + sub) * WIDTH
                    term = lax.dot_general(
                        w_in[:, column : column + WIDTH],
                        block,
                        (((1,), (1,)), ((), ())),
                        preferred_element_type=F32,
                    )
                    total = term if total is None else total + term
            pre[t] = total if c == 0 else pre[t] + total
            return carry

        lax.fori_loop(0, 2, tile, 0)

    def activate(t, carry):
        scale = jnp.concatenate(
            [jnp.sum(scales[2 * t + n], axis=0)[0:1] for n in range(2)], axis=1
        )
        gate = pre[t, : 2 * units] * scale
        up = pre[t, 2 * units :] * scale
        value = gate / (1.0 + jnp.exp(-gate)) * up
        act[pl.ds(pl.multiple_of(t * 256, 256), 256), :] = value.T.astype(BF16)
        return carry

    def multiply_out(c):
        def block(n, carry):
            column = pl.multiple_of((c * 4 + n) * WIDTH, WIDTH)
            value = jnp.dot(
                act[...], w_out[:, pl.ds(column, WIDTH)], preferred_element_type=F32
            )
            part[c, n // 2, n % 2] = value.astype(BF16).reshape(RING, RING, SLOTS, WIDTH)
            return carry

        lax.fori_loop(0, 4, block, 0)

    sent1, joined1, sent2, returned = {}, {}, {}, {}

    def view1(c, h):
        if second[h] == "z":
            return lambda sub, at: part.at[c, h, sub, at]
        return lambda sub, at: part.at[c, h, sub, :, at]

    def view2(c, h):
        return lambda sub, at: mid.at[c, h, sub, at]

    def land1(c, h):
        return lambda i: in1.at[c, h, i]

    def land2(c, h):
        return lambda i: in2.at[c, h, i]

    def send_part(c):
        for h in range(2):
            sent1[c, h] = scatter(second[h], view1(c, h), land1(c, h))

    def join_part(c):
        for h in range(2):
            joined1[c, h] = join(
                second[h], view1(c, h), land1(c, h), lambda sub: comb1.at[c, h, sub], sent1[c, h]
            )

    def send_mid(c):
        for h in range(2):
            for sub in range(2):
                mid[c, h, sub] = total(
                    second[h], view1(c, h), land1(c, h), sent1[c, h], joined1[c, h], sub
                ).astype(BF16)
            sent2[c, h] = scatter_direct(first[h], view2(c, h), land2(c, h))

    def send_home(c):
        for h in range(2):
            for sub in range(2):
                value = total_direct(first[h], view2(c, h), land2(c, h), sent2[c, h], sub)
                for g in range(RING):
                    homebox[c, g, h, :, sub * WIDTH : (sub + 1) * WIDTH] = value[
                        8 * g : 8 * g + 8
                    ].astype(BF16)
        returned[c] = exchange(homebox.at[c], back.at[c])

    def finish(c):
        arrive(returned[c])
        for s in range(2):
            columns = slice((c * 2 + s) * half, (c * 2 + s + 1) * half)
            value = hidden[c, s]
            produced = stacked(back, c, s).astype(BF16)
            for column in range(2):
                fetched = jnp.dot(fetch[column], produced, preferred_element_type=F32)
                value = value + shares[column, :, 0:1] * fetched
            out[:, columns] = value.astype(BF16)

    load_proj(0)
    load_proj(1)
    residual_load = local(residual_hbm, residual)
    tables()

    def meet():
        pl.semaphore_wait(barrier, size - 1 + len(column_peers))
        load_weights()

    attend(
        meet, decay_exp, queries_hbm, keys_hbm, values_hbm, gates_hbm, attn_gain, settled,
        queries, key_rows, value_rows, gate_rows, update, gathered, prior, state, inner, factor,
        state_sems, state_sems2, state_sems3, state_sems4, span_sems,
    )
    residual_load.wait()
    for step, c in (
        (project, 0), (send_proj, 0), (project, 1), (project, 2), (send_proj, 1),
        (join_proj, 0), (join_proj, 1), (project, 3), (send_proj, 2), (project, 4),
        (dispatch, 0), (dispatch, 1), (project, 5), (join_proj, 2), (send_proj, 3),
        (gather_start, 0), (gather_start, 1), (dispatch, 2), (send_proj, 4), (gather_wide, 0),
        (join_proj, 3), (gather_start, 2), (gather_wide, 1), (send_proj, 5), (join_proj, 4),
        (dispatch, 3), (join_proj, 5), (gather_wide_pass, 0), (gather_wide, 2),
        (gather_start, 3), (dispatch, 4), (gather_wide_pass, 1), (dispatch, 5),
    ):
        step(c)
    scale_step = send_scales()
    for step, c in (
        (gather_start, 4), (gather_wide_pass, 2), (gather_start, 5), (gather_wide, 3),
        (multiply_in, 0),
    ):
        step(c)
    shared = share_scales(scale_step)
    for step, c in (
        (gather_wide, 4), (gather_wide, 5), (multiply_in, 1), (gather_wide_pass, 3),
        (multiply_in, 2), (gather_wide_pass, 4), (gather_wide_pass, 5), (multiply_in, 3),
        (multiply_in, 4), (multiply_in, 5),
    ):
        step(c)
    for copy in shared:
        copy.wait_recv()
    lax.fori_loop(0, 2, activate, 0)
    weights[2][0].wait()
    weights[2][1].wait_recv()
    copies.finish()
    for step, c in (
        (multiply_out, 0), (send_part, 0), (multiply_out, 1), (send_part, 1), (multiply_out, 2),
        (send_part, 2), (multiply_out, 3), (join_part, 0), (multiply_out, 4), (multiply_out, 5),
        (send_part, 3), (join_part, 1), (send_part, 4), (send_part, 5), (join_part, 2),
        (join_part, 3), (join_part, 4), (join_part, 5), (send_mid, 0), (send_mid, 1),
        (send_mid, 2), (send_mid, 3), (send_mid, 4), (send_mid, 5), (send_home, 0),
        (send_home, 1), (send_home, 2), (send_home, 3), (send_home, 4), (send_home, 5),
        (finish, 0), (finish, 1), (finish, 2), (finish, 3), (finish, 4), (finish, 5),
    ):
        step(c)
    copies.finish()


def layer(
    queries, key_rows, value_rows, gate_rows, decay_exp, attn_gain, out_proj, residual,
    norm_gain, routes, route_weights, w_gate, w_up, w_down,
):
    units, width = w_gate.shape
    group_rows = residual.shape[0]
    row_count, depth = queries.shape
    head_count = decay_exp.shape[0]
    head_width = depth // head_count
    size = lax.axis_size("ctx")
    states = pltpu.VMEM((size, head_count * head_width // size, head_width), BF16)
    state_sems = pltpu.SemaphoreType.DMA((size - 1,))
    span = pltpu.VMEM(queries.shape, BF16)
    half = 2 * WIDTH
    count = CHUNKS * (6 + 3 + 3 + 14 + 24) + 3 + 15 + 3
    whole = (CHUNKS, 2, 2, RING, RING, SLOTS, WIDTH)
    box = (CHUNKS, RING, 2, SLOTS // RING, half)
    vmem = pl.BlockSpec(memory_space=pltpu.VMEM)
    anywhere = pl.BlockSpec(memory_space=pl.ANY)
    return pl.pallas_call(
        layer_kernel,
        out_shape=jax.ShapeDtypeStruct(residual.shape, BF16),
        in_specs=[pl.BlockSpec(memory_space=pltpu.SMEM)]
        + [anywhere] * 4
        + [vmem, anywhere, anywhere, vmem, vmem, vmem]
        + [anywhere] * 3,
        out_specs=vmem,
        scratch_shapes=[span] * 4
        + [states] * 4
        + [pltpu.VMEM((head_count, row_count, head_width), F32)] * 2
        + [state_sems] * 4
        + [
            pltpu.SemaphoreType.DMA((6,)),
            span,
            pltpu.VMEM(residual.shape, BF16),
            pltpu.VMEM((SLOTS, group_rows), BF16),
            pltpu.VMEM((2, group_rows, SLOTS), BF16),
            pltpu.VMEM((2, group_rows, 128), F32),
            pltpu.VMEM((2, depth, 4 * WIDTH), BF16),
            pltpu.VMEM((CHUNKS, 2, RING, group_rows, half), BF16),
            pltpu.VMEM((CHUNKS, 6, group_rows, half), BF16),
            pltpu.VMEM((CHUNKS, 2, group_rows, half), BF16),
            pltpu.VMEM((CHUNKS, 2, group_rows, half), F32),
            pltpu.VMEM((group_rows, 128), F32),
            pltpu.VMEM(box, BF16),
            pltpu.VMEM(box, BF16),
            pltpu.VMEM((RING, SLOTS // RING, 128), F32),
            pltpu.VMEM((RING, SLOTS // RING, 128), F32),
            pltpu.VMEM((RING, RING, 8, 128), F32),
            pltpu.VMEM(whole, BF16),
            pltpu.VMEM((4 * units, width), BF16),
            pltpu.VMEM((2 * units, width), BF16),
            pltpu.VMEM((2, 4 * units, 256), F32),
            pltpu.VMEM((RING * RING * SLOTS, 2 * units), BF16),
            pltpu.VMEM((CHUNKS, 2, 6, RING, SLOTS, WIDTH), BF16),
            pltpu.VMEM((CHUNKS, 2, 2, RING, SLOTS, WIDTH), BF16),
            pltpu.VMEM((CHUNKS, 2, 2, RING, SLOTS, WIDTH), BF16),
            pltpu.VMEM((CHUNKS, 2, 6, SLOTS, WIDTH), BF16),
            pltpu.VMEM(box, BF16),
            pltpu.VMEM(box, BF16),
            pltpu.SemaphoreType.DMA((count,)),
            pltpu.SemaphoreType.DMA((count,)),
            pltpu.SemaphoreType.DMA((3 * CHUNKS + 5,)),
        ],
        compiler_params=pltpu.CompilerParams(
            collective_id=2, has_side_effects=True, vmem_limit_bytes=64000 * 1024
        ),
        name="layer",
    )(
        decay_exp, queries, key_rows, value_rows, gate_rows, attn_gain.reshape(1, depth),
        out_proj, residual, norm_gain.reshape(1, width), routes.T, route_weights.T,
        w_gate, w_up, w_down,
    )


def body(
    queries,
    key_rows,
    value_rows,
    gate_rows,
    decay_exp,
    attn_gain,
    out_proj,
    residual,
    norm_gain,
    routes,
    route_weights,
    w_gate,
    w_up,
    w_down,
):
    return layer(
        queries,
        key_rows,
        value_rows,
        gate_rows,
        decay_exp,
        attn_gain,
        out_proj,
        residual,
        norm_gain,
        routes,
        route_weights,
        w_gate[0],
        w_up[0],
        w_down[0],
    )


def solution(mesh):
    in_specs = (
        P("ctx", "exp"),
        P("ctx", "exp"),
        P("ctx", "exp"),
        P("ctx", "exp"),
        P("exp"),
        P("exp"),
        P("exp", None),
        P(("ctx", "exp"), None),
        P(),
        P("ctx", None),
        P("ctx", None),
        P("exp", "ctx", None),
        P("exp", "ctx", None),
        P("exp", "ctx", None),
    )
    out_specs = P(("ctx", "exp"), None)
    return jax.shard_map(body, mesh=mesh, in_specs=in_specs, out_specs=out_specs, check_vma=False)
```

```python
import jax
import jax.numpy as jnp
from jax import lax
from jax.experimental import pallas as pl
from jax.experimental.pallas import tpu as pltpu
from jax.sharding import PartitionSpec as P

EPSILON = 1e-06
MESH = pl.DeviceIdType.MESH
BF16 = jnp.bfloat16
F32 = jnp.float32
RING = 4
CHUNKS = 6
WIDTH = 256
SLOTS = 32
HEAD_PIECES = 3


def attend(
    meet, decay_exp, queries_hbm, keys_hbm, values_hbm, gates_hbm, attn_gain, settled,
    queries, key_rows, value_rows, gate_rows, update, gathered, prior, state, inner, factor,
    send_sems, recv_sems, send_sems2, recv_sems2, local_sems,
):
    index, owner = lax.axis_index("ctx"), lax.axis_index("exp")
    size = gathered.shape[0]
    head_count = decay_exp.shape[0]
    row_count = queries.shape[0]
    head_width = queries.shape[1] // head_count

    loads = []
    for n, (source, target) in enumerate(
        (
            (keys_hbm, key_rows),
            (values_hbm, value_rows),
            (queries_hbm, queries),
            (gates_hbm, gate_rows),
        )
    ):
        loads.append(pltpu.make_async_copy(source, target, local_sems.at[2 + n]))
        loads[n].start()
    def rate_of(head, shape):
        exponent = jnp.full(shape, decay_exp[head].astype(F32), F32)
        return jnp.exp2(-exponent)

    def columns(head):
        return slice(head * head_width, (head + 1) * head_width)

    positions = lax.broadcasted_iota(jnp.int32, (row_count, head_width), 0).astype(F32)
    loads[0].wait()
    loads[1].wait()
    for head in range(head_count):
        rate = rate_of(head, (1, head_width))
        tail = jnp.exp(-rate * (row_count - 1.0 - positions))
        keyed = (key_rows[:, columns(head)].astype(F32) * tail).astype(BF16)
        product = lax.dot_general(
            keyed,
            value_rows[:, columns(head)],
            (((0,), (0,)), ((), ())),
            preferred_element_type=F32,
        )
        parts = size // head_count
        update[head * parts : (head + 1) * parts] = product.astype(BF16).reshape(
            parts, head_width // parts, head_width
        )
    meet()

    def exchange(source, target, send, recv):
        def copy(step):
            other = lax.rem(index + step, size)
            return pltpu.make_async_remote_copy(
                src_ref=source.at[other],
                dst_ref=target.at[index],
                send_sem=send.at[step - 1],
                recv_sem=recv.at[step - 1],
                device_id=(other, owner),
                device_id_type=MESH,
            )

        def start(step, carry):
            copy(step).start()
            return carry

        def arrive(step, carry):
            copy(step).wait_recv()
            return carry

        def leave(step, carry):
            copy(step).wait_send()
            return carry

        return (
            lambda: lax.fori_loop(1, size, start, 0),
            lambda: lax.fori_loop(1, size, arrive, 0),
            lambda: lax.fori_loop(1, size, leave, 0),
        )

    start, arrive, leave = exchange(update, gathered, send_sems, recv_sems)
    start()
    kept = pltpu.make_async_copy(update.at[index], gathered.at[index], local_sems.at[0])
    kept.start()

    def inside(head):
        rate = rate_of(head, (1, row_count))
        row = lax.broadcasted_iota(jnp.int32, (row_count, row_count), 0)
        column = lax.broadcasted_iota(jnp.int32, (row_count, row_count), 1)
        offset = (row - column).astype(F32)
        damping = jnp.where(offset >= 0.0, jnp.exp(-rate * jnp.maximum(offset, 0.0)), 0.0)
        scores = lax.dot_general(
            queries[:, columns(head)],
            key_rows[:, columns(head)],
            (((1,), (1,)), ((), ())),
            preferred_element_type=F32,
        )
        mixing = (scores * damping).astype(BF16)
        inner[head] = jnp.dot(mixing, value_rows[:, columns(head)], preferred_element_type=F32)
        gate = gate_rows[:, columns(head)].astype(F32)
        factor[head] = attn_gain[:, columns(head)] / (1.0 + jnp.exp(-gate))

    loads[2].wait()
    loads[3].wait()
    for head in range(head_count // 2):
        inside(head)
    kept.wait()
    arrive()
    mine = index // (size // head_count)
    carry_decay = jnp.exp(-rate_of(mine, (1, head_width)) * float(row_count))
    running = jnp.zeros(gathered.shape[1:], F32)
    for block in range(size):
        prior[block] = running.astype(BF16)
        if block + 1 < size:
            running = carry_decay * running + gathered[block].astype(F32)
    start2, arrive2, leave2 = exchange(prior, state, send_sems2, recv_sems2)
    start2()
    kept2 = pltpu.make_async_copy(prior.at[index], state.at[index], local_sems.at[1])
    kept2.start()
    for head in range(head_count // 2, head_count):
        inside(head)
    leave()
    kept2.wait()
    arrive2()
    for head in range(head_count):
        rate = rate_of(head, (1, head_width))
        parts = size // head_count
        held = state[head * parts : (head + 1) * parts].reshape(head_width, head_width)
        reached = jnp.dot(queries[:, columns(head)], held, preferred_element_type=F32)
        mixed = inner[head] + reached * jnp.exp(-rate * (positions + 1.0))
        mean_square = jnp.mean(mixed * mixed, axis=1, keepdims=True)
        normed = mixed * lax.rsqrt(mean_square + EPSILON)
        settled[:, columns(head)] = (normed * factor[head]).astype(BF16)
    leave2()


def place(index):
    return index // 8, (index // 2) % 4, index % 2


class Copies:
    def __init__(self, send_sems, recv_sems):
        self.send_sems, self.recv_sems = send_sems, recv_sems
        self.count, self.waiting = 0, []

    def start(self, source, target, device):
        copy = pltpu.make_async_remote_copy(
            src_ref=source,
            dst_ref=target,
            send_sem=self.send_sems.at[self.count],
            recv_sem=self.recv_sems.at[self.count],
            device_id=device,
            device_id_type=MESH,
        )
        copy.start()
        self.count += 1
        self.waiting.append(copy)
        return copy

    def finish(self):
        for copy in self.waiting:
            copy.wait_send()
        self.waiting = []


def layer_kernel(
    decay_exp, queries_hbm, keys_hbm, values_hbm, gates_hbm, attn_gain,
    out_proj, residual_hbm, norm_gain, routes, route_weights, w_gate, w_up, w_down, out,
    queries, key_rows, value_rows, gate_rows, update, gathered, prior, state, inner, factor,
    state_sems, state_sems2, state_sems3, state_sems4, span_sems,
    settled, residual, pick, fetch, shares,
    proj_w, proj, in0, comb0, hidden, squares, outbox, inbox, scale_out, scale_in, scales,
    rows, w_in, w_out, pre, act, in1, comb1, mid, in2, homebox, back,
    send_sems, recv_sems, local_sems,
):
    index, owner = lax.axis_index("ctx"), lax.axis_index("exp")
    z, x, core = place(index)
    part = rows

    def device(zz, xx):
        return (zz * 8 + xx * 2 + core, owner)

    def beside(at):
        return lax.rem(at + RING - 1, RING), lax.rem(at + 1, RING), lax.rem(at + 2, RING)

    x_left, x_right, x_far = beside(x)
    z_left, z_right, z_far = beside(z)
    y_left, y_right, y_far = beside(owner)
    partner = (index + 1 - 2 * core, owner)
    near = {
        "x": (x, x_left, x_right, device(z, x_left), device(z, x_right), x_far),
        "z": (z, z_left, z_right, device(z_left, x), device(z_right, x), z_far),
        "y": (owner, y_left, y_right, (index, y_left), (index, y_right), y_far),
    }
    column_peers = [lax.rem(owner + step, RING) for step in range(1, RING)]
    plane_peers = [
        device(lax.rem(z + dz, RING), lax.rem(x + dx, RING))
        for dz in range(RING)
        for dx in range(RING)
        if dz or dx
    ]
    barrier = pltpu.get_barrier_semaphore()
    size = gathered.shape[0]

    def greet(step, carry):
        other = lax.rem(index + step, size)
        pl.semaphore_signal(barrier, inc=1, device_id=(other, owner), device_id_type=MESH)
        return carry

    lax.fori_loop(1, size, greet, 0)
    for other in column_peers:
        pl.semaphore_signal(barrier, inc=1, device_id=(index, other), device_id_type=MESH)
    copies = Copies(send_sems, recv_sems)
    local_count = [0]

    def local(source, target):
        copy = pltpu.make_async_copy(source, target, local_sems.at[local_count[0]])
        local_count[0] += 1
        copy.start()
        return copy

    units = w_gate.shape[0]
    piece_width = 4 * WIDTH
    half = 2 * WIDTH
    first, second = ("x", "z"), ("z", "x")
    both = slice(None)

    def scatter(axis, view, land):
        me, left, right, to_left, to_right, far = near[axis]
        return (
            copies.start(view(0, far), land(0), to_left),
            copies.start(view(1, far), land(1), to_right),
            copies.start(view(0, right), land(2), to_right),
            copies.start(view(1, left), land(3), to_left),
        )

    def join(axis, view, land, stage, sent):
        me, left, right, to_left, to_right, far = near[axis]
        joined = []
        for sub, at, to in ((0, left, to_left), (1, right, to_right)):
            sent[sub].wait_recv()
            stage(sub)[...] = (
                land(sub)[...].astype(F32) + view(sub, at)[...].astype(F32)
            ).astype(BF16)
            joined.append(copies.start(stage(sub), land(4 + sub), to))
        return joined

    def scatter_direct(axis, view, land):
        me, left, right, to_left, to_right, far = near[axis]
        to_far = device(z, x_far) if axis == "x" else device(z_far, x)
        return (
            copies.start(view(0, far), land(4), to_far),
            copies.start(view(1, far), land(5), to_far),
            copies.start(view(0, right), land(2), to_right),
            copies.start(view(1, left), land(3), to_left),
            copies.start(view(0, left), land(0), to_left),
            copies.start(view(1, right), land(1), to_right),
        )

    def total_direct(axis, view, land, sent, sub):
        value = view(sub, near[axis][0])[...].astype(F32)
        for n, i in ((4 + sub, sub), (2 + sub, 2 + sub), (sub, 4 + sub)):
            sent[n].wait_recv()
            value = value + land(i)[...].astype(F32)
        return value

    def total(axis, view, land, sent, joined, sub):
        me = near[axis][0]
        sent[2 + sub].wait_recv()
        joined[sub].wait_recv()
        return (
            view(sub, me)[...].astype(F32)
            + land(2 + sub)[...].astype(F32)
            + land(4 + sub)[...].astype(F32)
        )

    def tables():
        group_rows = residual.shape[0]
        row_count = routes.shape[1]
        slot = lax.broadcasted_iota(jnp.int32, (SLOTS, row_count), 0)
        place_of = lax.broadcasted_iota(jnp.int32, (SLOTS, row_count), 1)
        expert = slot // 8
        chosen = jnp.where(expert % 2 == 0, routes[0:1, :], routes[1:2, :])
        picked = (chosen == expert) & (place_of // group_rows == owner)
        before = lax.broadcasted_iota(jnp.int32, (row_count, row_count), 0)
        after = lax.broadcasted_iota(jnp.int32, (row_count, row_count), 1)
        upto = jnp.where(before <= after, 1.0, 0.0).astype(BF16)
        rank = jnp.dot(
            jnp.where(picked, 1.0, 0.0).astype(BF16), upto, preferred_element_type=F32
        )
        chosen_slot = picked & (rank == (slot % 8 + 1).astype(F32))
        mine = lax.broadcasted_iota(jnp.int32, (group_rows, row_count), 1)
        mine = mine == owner * group_rows + lax.broadcasted_iota(
            jnp.int32, (group_rows, row_count), 0
        )
        mine_rows = jnp.where(mine, 1.0, 0.0).astype(BF16)

        def across(left, right):
            return lax.dot_general(
                left, right, (((1,), (1,)), ((), ())), preferred_element_type=F32
            ).astype(BF16)

        pick[...] = across(jnp.where(chosen_slot, 1.0, 0.0).astype(BF16), mine_rows)
        for column in range(2):
            table = chosen_slot & (expert % 2 == column)
            fetch[column] = across(mine_rows, jnp.where(table, 1.0, 0.0).astype(BF16))
            share = jnp.sum(
                jnp.where(mine, route_weights[column : column + 1, :], 0.0), axis=1, keepdims=True
            )
            shares[column] = jnp.broadcast_to(share, shares.shape[1:])

    loads = {}

    def load_proj(c):
        loads[c] = local(out_proj.at[:, pl.ds(c * piece_width, piece_width)], proj_w.at[c % 2])

    def project(c):
        loads[c].wait()
        for s in range(2):
            value = jnp.dot(
                settled[...],
                proj_w[c % 2, :, s * half : (s + 1) * half],
                preferred_element_type=F32,
            )
            proj[c, s] = value.astype(BF16).reshape(RING, -1, half)
        if c + 2 < CHUNKS:
            load_proj(c + 2)

    sent0, joined0, dispatched = {}, {}, {}

    def view0(c):
        return lambda sub, at: proj.at[c, sub, at]

    def land0(c):
        return lambda i: in0.at[c, i]

    def send_proj(c):
        sent0[c] = scatter("y", view0(c), land0(c))

    def join_proj(c):
        joined0[c] = join("y", view0(c), land0(c), lambda sub: comb0.at[c, sub], sent0[c])

    def exchange(box, landing):
        sent = [
            copies.start(box.at[other], landing.at[owner], (index, other))
            for other in column_peers
        ]
        return sent, local(box.at[owner], landing.at[owner])

    def arrive(exchanged):
        for copy in exchanged[0]:
            copy.wait_recv()
        exchanged[1].wait()

    def stacked(box, *place):
        return jnp.concatenate(
            [box[(*place[:1], e, *place[1:])].astype(F32) for e in range(RING)], axis=0
        )

    def dispatch(c):
        for s in range(2):
            columns = slice((c * 2 + s) * half, (c * 2 + s + 1) * half)
            value = total("y", view0(c), land0(c), sent0[c], joined0[c], s)
            value = value + residual[:, columns].astype(F32)
            hidden[c, s] = value
            square = value * value
            folded = square[:, :128]
            for lane in range(128, half, 128):
                folded = folded + square[:, lane : lane + 128]
            if c == 0 and s == 0:
                squares[...] = folded
            else:
                squares[...] = squares[...] + folded
            scaled = (value * norm_gain[:, columns]).astype(BF16)
            picked = jnp.dot(pick[...], scaled, preferred_element_type=F32)
            for e in range(RING):
                outbox[c, e, s] = picked[8 * e : 8 * e + 8].astype(BF16)
        dispatched[c] = exchange(outbox.at[c], inbox.at[c])

    def send_scales():
        mean_square = jnp.sum(squares[...], axis=1, keepdims=True) / (CHUNKS * piece_width)
        inverse = jnp.broadcast_to(lax.rsqrt(mean_square + EPSILON), squares.shape)
        picked = jnp.dot(
            pick[...].astype(F32),
            inverse,
            precision=lax.Precision.HIGHEST,
            preferred_element_type=F32,
        )
        for e in range(RING):
            scale_out[e] = picked[8 * e : 8 * e + 8]
        return exchange(scale_out, scale_in)

    def share_scales(exchanged):
        arrive(exchanged)
        mine = jnp.concatenate([scale_in[e] for e in range(RING)], axis=0)
        row = lax.broadcasted_iota(jnp.int32, (SLOTS, 128), 0)
        lane = lax.broadcasted_iota(jnp.int32, (SLOTS, 128), 1)
        line = jnp.sum(jnp.where(lane == x * SLOTS + row, mine, 0.0), axis=0, keepdims=True)
        scales[z, x] = jnp.broadcast_to(line, (8, 128))
        return [copies.start(scales.at[z, x], scales.at[z, x], other) for other in plane_peers]

    gather1, relay1, gather2, relay2 = {}, {}, {}, {}

    def line_of(c, h, stage, sub, at):
        axis = (first if stage == 1 else second)[h]
        if stage == 1:
            return rows.at[c, h, sub, at, x] if axis == "z" else rows.at[c, h, sub, z, at]
        return rows.at[c, h, sub, at] if axis == "z" else rows.at[c, h, sub, :, at]

    def spread(c, h, stage, started):
        me, left, right, to_left, to_right, far = near[(first if stage == 1 else second)[h]]
        mine = line_of(c, h, stage, both, me)
        sent = []
        if stage == 1 and c < HEAD_PIECES:
            to_far = device(z, x_far) if first[h] == "x" else device(z_far, x)
            sent = [copies.start(mine, mine, to_far)]
        started[c, h] = [copies.start(mine, mine, to_right), copies.start(mine, mine, to_left)]
        started[c, h] += sent

    def pass_on(c, h, stage, started, passed):
        me, left, right, to_left, to_right, far = near[(first if stage == 1 else second)[h]]
        from_left, from_right = started[c, h]
        from_left.wait_recv()
        source = line_of(c, h, stage, 0, left)
        one = copies.start(source, source, to_right)
        from_right.wait_recv()
        source = line_of(c, h, stage, 1, right)
        passed[c, h] = (one, copies.start(source, source, to_left))

    def gather_start(c):
        arrive(dispatched[c])
        for s in range(2):
            value = stacked(inbox, c, s).astype(BF16)
            for sub in range(2):
                rows[c, s, sub, z, x] = value[:, sub * WIDTH : (sub + 1) * WIDTH]
        for h in range(2):
            spread(c, h, 1, gather1)

    def gather_pass(c):
        if c < HEAD_PIECES:
            return
        for h in range(2):
            pass_on(c, h, 1, gather1, relay1)

    def gather_wide(c):
        for h in range(2):
            for copy in gather1[c, h] if c < HEAD_PIECES else relay1[c, h]:
                copy.wait_recv()
            spread(c, h, 2, gather2)

    def gather_wide_pass(c):
        for h in range(2):
            pass_on(c, h, 2, gather2, relay2)

    weights = []

    def load_weights():
        for source, target, base in (
            (w_gate, w_in, 0),
            (w_up, w_in, 2 * units),
            (w_down, w_out, 0),
        ):
            kept = local(source, target.at[pl.ds(base, units)])
            sent = copies.start(source, target.at[pl.ds(base + units, units)], partner)
            weights.append((kept, sent))

    def multiply_in(c):
        for h in range(2):
            for copy in relay2[c, h]:
                copy.wait_recv()
        if c == 0:
            for n in range(2):
                weights[n][0].wait()
                weights[n][1].wait_recv()

        def tile(t, carry):
            total = None
            for h in range(2):
                for sub in range(2):
                    block = rows[c, h, sub, pl.ds(2 * t, 2)].reshape(256, WIDTH)
                    column = ((c * 2 + h) * 2 + sub) * WIDTH
                    term = lax.dot_general(
                        w_in[:, column : column + WIDTH],
                        block,
                        (((1,), (1,)), ((), ())),
                        preferred_element_type=F32,
                    )
                    total = term if total is None else total + term
            pre[t] = total if c == 0 else pre[t] + total
            return carry

        lax.fori_loop(0, 2, tile, 0)

    def activate(t, carry):
        scale = jnp.concatenate(
            [jnp.sum(scales[2 * t + n], axis=0)[0:1] for n in range(2)], axis=1
        )
        gate = pre[t, : 2 * units] * scale
        up = pre[t, 2 * units :] * scale
        value = gate / (1.0 + jnp.exp(-gate)) * up
        act[pl.ds(pl.multiple_of(t * 256, 256), 256), :] = value.T.astype(BF16)
        return carry

    def multiply_out(c):
        def block(n, carry):
            column = pl.multiple_of((c * 4 + n) * WIDTH, WIDTH)
            value = jnp.dot(
                act[...], w_out[:, pl.ds(column, WIDTH)], preferred_element_type=F32
            )
            part[c, n // 2, n % 2] = value.astype(BF16).reshape(RING, RING, SLOTS, WIDTH)
            return carry

        lax.fori_loop(0, 4, block, 0)

    sent1, joined1, sent2, returned = {}, {}, {}, {}

    def view1(c, h):
        if second[h] == "z":
            return lambda sub, at: part.at[c, h, sub, at]
        return lambda sub, at: part.at[c, h, sub, :, at]

    def view2(c, h):
        return lambda sub, at: mid.at[c, h, sub, at]

    def land1(c, h):
        return lambda i: in1.at[c, h, i]

    def land2(c, h):
        return lambda i: in2.at[c, h, i]

    def send_part(c):
        for h in range(2):
            sent1[c, h] = scatter(second[h], view1(c, h), land1(c, h))

    def join_part(c):
        for h in range(2):
            joined1[c, h] = join(
                second[h], view1(c, h), land1(c, h), lambda sub: comb1.at[c, h, sub], sent1[c, h]
            )

    def send_mid(c):
        for h in range(2):
            for sub in range(2):
                mid[c, h, sub] = total(
                    second[h], view1(c, h), land1(c, h), sent1[c, h], joined1[c, h], sub
                ).astype(BF16)
            sent2[c, h] = scatter_direct(first[h], view2(c, h), land2(c, h))

    def send_home(c):
        for h in range(2):
            for sub in range(2):
                value = total_direct(first[h], view2(c, h), land2(c, h), sent2[c, h], sub)
                for g in range(RING):
                    homebox[c, g, h, :, sub * WIDTH : (sub + 1) * WIDTH] = value[
                        8 * g : 8 * g + 8
                    ].astype(BF16)
        returned[c] = exchange(homebox.at[c], back.at[c])

    def finish(c):
        arrive(returned[c])
        for s in range(2):
            columns = slice((c * 2 + s) * half, (c * 2 + s + 1) * half)
            value = hidden[c, s]
            produced = stacked(back, c, s).astype(BF16)
            for column in range(2):
                fetched = jnp.dot(fetch[column], produced, preferred_element_type=F32)
                value = value + shares[column, :, 0:1] * fetched
            out[:, columns] = value.astype(BF16)

    load_proj(0)
    load_proj(1)
    residual_load = local(residual_hbm, residual)
    tables()

    def meet():
        pl.semaphore_wait(barrier, size - 1 + len(column_peers))
        load_weights()

    attend(
        meet, decay_exp, queries_hbm, keys_hbm, values_hbm, gates_hbm, attn_gain, settled,
        queries, key_rows, value_rows, gate_rows, update, gathered, prior, state, inner, factor,
        state_sems, state_sems2, state_sems3, state_sems4, span_sems,
    )
    residual_load.wait()
    for step, c in (
        (project, 0), (send_proj, 0), (project, 1), (project, 2), (send_proj, 1),
        (join_proj, 0), (join_proj, 1), (project, 3), (send_proj, 2), (project, 4),
        (dispatch, 0), (dispatch, 1), (project, 5), (join_proj, 2), (send_proj, 3),
        (gather_start, 0), (gather_start, 1), (gather_pass, 0), (dispatch, 2), (gather_pass, 1),
        (send_proj, 4), (gather_wide, 0), (join_proj, 3), (gather_start, 2), (gather_wide, 1),
        (send_proj, 5), (join_proj, 4), (dispatch, 3), (gather_pass, 2), (join_proj, 5),
        (gather_wide_pass, 0), (gather_wide, 2), (gather_start, 3), (dispatch, 4),
        (gather_wide_pass, 1), (dispatch, 5),
    ):
        step(c)
    scale_step = send_scales()
    for step, c in (
        (gather_start, 4), (gather_pass, 3), (gather_wide_pass, 2), (gather_start, 5),
        (gather_pass, 4),
    ):
        step(c)
    shared = share_scales(scale_step)
    for step, c in (
        (gather_wide, 3), (multiply_in, 0), (gather_pass, 5), (gather_wide, 4),
        (gather_wide, 5), (multiply_in, 1), (gather_wide_pass, 3), (multiply_in, 2),
        (gather_wide_pass, 4), (gather_wide_pass, 5), (multiply_in, 3), (multiply_in, 4),
        (multiply_in, 5),
    ):
        step(c)
    for copy in shared:
        copy.wait_recv()
    lax.fori_loop(0, 2, activate, 0)
    weights[2][0].wait()
    weights[2][1].wait_recv()
    copies.finish()
    for step, c in (
        (multiply_out, 0), (send_part, 0), (multiply_out, 1), (send_part, 1), (multiply_out, 2),
        (send_part, 2), (multiply_out, 3), (join_part, 0), (multiply_out, 4), (multiply_out, 5),
        (send_part, 3), (join_part, 1), (send_part, 4), (send_part, 5), (join_part, 2),
        (join_part, 3), (join_part, 4), (join_part, 5), (send_mid, 0), (send_mid, 1),
        (send_mid, 2), (send_mid, 3), (send_mid, 4), (send_mid, 5), (send_home, 0),
        (send_home, 1), (send_home, 2), (send_home, 3), (send_home, 4), (send_home, 5),
        (finish, 0), (finish, 1), (finish, 2), (finish, 3), (finish, 4), (finish, 5),
    ):
        step(c)
    copies.finish()


def layer(
    queries, key_rows, value_rows, gate_rows, decay_exp, attn_gain, out_proj, residual,
    norm_gain, routes, route_weights, w_gate, w_up, w_down,
):
    units, width = w_gate.shape
    group_rows = residual.shape[0]
    row_count, depth = queries.shape
    head_count = decay_exp.shape[0]
    head_width = depth // head_count
    size = lax.axis_size("ctx")
    states = pltpu.VMEM((size, head_count * head_width // size, head_width), BF16)
    state_sems = pltpu.SemaphoreType.DMA((size - 1,))
    span = pltpu.VMEM(queries.shape, BF16)
    half = 2 * WIDTH
    count = CHUNKS * (6 + 3 + 3 + 16 + 24) + 3 + 15 + 3
    whole = (CHUNKS, 2, 2, RING, RING, SLOTS, WIDTH)
    box = (CHUNKS, RING, 2, SLOTS // RING, half)
    vmem = pl.BlockSpec(memory_space=pltpu.VMEM)
    anywhere = pl.BlockSpec(memory_space=pl.ANY)
    return pl.pallas_call(
        layer_kernel,
        out_shape=jax.ShapeDtypeStruct(residual.shape, BF16),
        in_specs=[pl.BlockSpec(memory_space=pltpu.SMEM)]
        + [anywhere] * 4
        + [vmem, anywhere, anywhere, vmem, vmem, vmem]
        + [anywhere] * 3,
        out_specs=vmem,
        scratch_shapes=[span] * 4
        + [states] * 4
        + [pltpu.VMEM((head_count, row_count, head_width), F32)] * 2
        + [state_sems] * 4
        + [
            pltpu.SemaphoreType.DMA((6,)),
            span,
            pltpu.VMEM(residual.shape, BF16),
            pltpu.VMEM((SLOTS, group_rows), BF16),
            pltpu.VMEM((2, group_rows, SLOTS), BF16),
            pltpu.VMEM((2, group_rows, 128), F32),
            pltpu.VMEM((2, depth, 4 * WIDTH), BF16),
            pltpu.VMEM((CHUNKS, 2, RING, group_rows, half), BF16),
            pltpu.VMEM((CHUNKS, 6, group_rows, half), BF16),
            pltpu.VMEM((CHUNKS, 2, group_rows, half), BF16),
            pltpu.VMEM((CHUNKS, 2, group_rows, half), F32),
            pltpu.VMEM((group_rows, 128), F32),
            pltpu.VMEM(box, BF16),
            pltpu.VMEM(box, BF16),
            pltpu.VMEM((RING, SLOTS // RING, 128), F32),
            pltpu.VMEM((RING, SLOTS // RING, 128), F32),
            pltpu.VMEM((RING, RING, 8, 128), F32),
            pltpu.VMEM(whole, BF16),
            pltpu.VMEM((4 * units, width), BF16),
            pltpu.VMEM((2 * units, width), BF16),
            pltpu.VMEM((2, 4 * units, 256), F32),
            pltpu.VMEM((RING * RING * SLOTS, 2 * units), BF16),
            pltpu.VMEM((CHUNKS, 2, 6, RING, SLOTS, WIDTH), BF16),
            pltpu.VMEM((CHUNKS, 2, 2, RING, SLOTS, WIDTH), BF16),
            pltpu.VMEM((CHUNKS, 2, 2, RING, SLOTS, WIDTH), BF16),
            pltpu.VMEM((CHUNKS, 2, 6, SLOTS, WIDTH), BF16),
            pltpu.VMEM(box, BF16),
            pltpu.VMEM(box, BF16),
            pltpu.SemaphoreType.DMA((count,)),
            pltpu.SemaphoreType.DMA((count,)),
            pltpu.SemaphoreType.DMA((3 * CHUNKS + 5,)),
        ],
        compiler_params=pltpu.CompilerParams(
            collective_id=2, has_side_effects=True, vmem_limit_bytes=64000 * 1024
        ),
        name="layer",
    )(
        decay_exp, queries, key_rows, value_rows, gate_rows, attn_gain.reshape(1, depth),
        out_proj, residual, norm_gain.reshape(1, width), routes.T, route_weights.T,
        w_gate, w_up, w_down,
    )


def body(
    queries,
    key_rows,
    value_rows,
    gate_rows,
    decay_exp,
    attn_gain,
    out_proj,
    residual,
    norm_gain,
    routes,
    route_weights,
    w_gate,
    w_up,
    w_down,
):
    return layer(
        queries,
        key_rows,
        value_rows,
        gate_rows,
        decay_exp,
        attn_gain,
        out_proj,
        residual,
        norm_gain,
        routes,
        route_weights,
        w_gate[0],
        w_up[0],
        w_down[0],
    )


def solution(mesh):
    in_specs = (
        P("ctx", "exp"),
        P("ctx", "exp"),
        P("ctx", "exp"),
        P("ctx", "exp"),
        P("exp"),
        P("exp"),
        P("exp", None),
        P(("ctx", "exp"), None),
        P(),
        P("ctx", None),
        P("ctx", None),
        P("exp", "ctx", None),
        P("exp", "ctx", None),
        P("exp", "ctx", None),
    )
    out_specs = P(("ctx", "exp"), None)
    return jax.shard_map(body, mesh=mesh, in_specs=in_specs, out_specs=out_specs, check_vma=False)
```

```python
import jax
import jax.numpy as jnp
from jax import lax
from jax.experimental import pallas as pl
from jax.experimental.pallas import tpu as pltpu
from jax.sharding import PartitionSpec as P

EPSILON = 1e-06
MESH = pl.DeviceIdType.MESH
BF16 = jnp.bfloat16
F32 = jnp.float32
RING = 4
CHUNKS = 6
WIDTH = 256
SLOTS = 32
HEAD_PIECES = 3


def attend(
    meet, decay_exp, queries_hbm, keys_hbm, values_hbm, gates_hbm, attn_gain, settled,
    queries, key_rows, value_rows, gate_rows, update, gathered, prior, state, inner, factor,
    send_sems, recv_sems, send_sems2, recv_sems2, local_sems,
):
    index, owner = lax.axis_index("ctx"), lax.axis_index("exp")
    size = gathered.shape[0]
    head_count = decay_exp.shape[0]
    row_count = queries.shape[0]
    head_width = queries.shape[1] // head_count

    loads = []
    for n, (source, target) in enumerate(
        (
            (keys_hbm, key_rows),
            (values_hbm, value_rows),
            (queries_hbm, queries),
            (gates_hbm, gate_rows),
        )
    ):
        loads.append(pltpu.make_async_copy(source, target, local_sems.at[2 + n]))
        loads[n].start()
    def rate_of(head, shape):
        exponent = jnp.full(shape, decay_exp[head].astype(F32), F32)
        return jnp.exp2(-exponent)

    def columns(head):
        return slice(head * head_width, (head + 1) * head_width)

    positions = lax.broadcasted_iota(jnp.int32, (row_count, head_width), 0).astype(F32)
    loads[0].wait()
    loads[1].wait()
    for head in range(head_count):
        rate = rate_of(head, (1, head_width))
        tail = jnp.exp(-rate * (row_count - 1.0 - positions))
        keyed = (key_rows[:, columns(head)].astype(F32) * tail).astype(BF16)
        product = lax.dot_general(
            keyed,
            value_rows[:, columns(head)],
            (((0,), (0,)), ((), ())),
            preferred_element_type=F32,
        )
        parts = size // head_count
        update[head * parts : (head + 1) * parts] = product.astype(BF16).reshape(
            parts, head_width // parts, head_width
        )
    meet()

    def exchange(source, target, send, recv):
        def copy(step):
            other = lax.rem(index + step, size)
            return pltpu.make_async_remote_copy(
                src_ref=source.at[other],
                dst_ref=target.at[index],
                send_sem=send.at[step - 1],
                recv_sem=recv.at[step - 1],
                device_id=(other, owner),
                device_id_type=MESH,
            )

        def start(step, carry):
            copy(step).start()
            return carry

        def arrive(step, carry):
            copy(step).wait_recv()
            return carry

        def leave(step, carry):
            copy(step).wait_send()
            return carry

        return (
            lambda: lax.fori_loop(1, size, start, 0),
            lambda: lax.fori_loop(1, size, arrive, 0),
            lambda: lax.fori_loop(1, size, leave, 0),
        )

    start, arrive, leave = exchange(update, gathered, send_sems, recv_sems)
    start()
    kept = pltpu.make_async_copy(update.at[index], gathered.at[index], local_sems.at[0])
    kept.start()

    def inside(head):
        rate = rate_of(head, (1, row_count))
        row = lax.broadcasted_iota(jnp.int32, (row_count, row_count), 0)
        column = lax.broadcasted_iota(jnp.int32, (row_count, row_count), 1)
        offset = (row - column).astype(F32)
        damping = jnp.where(offset >= 0.0, jnp.exp(-rate * jnp.maximum(offset, 0.0)), 0.0)
        scores = lax.dot_general(
            queries[:, columns(head)],
            key_rows[:, columns(head)],
            (((1,), (1,)), ((), ())),
            preferred_element_type=F32,
        )
        mixing = (scores * damping).astype(BF16)
        inner[head] = jnp.dot(mixing, value_rows[:, columns(head)], preferred_element_type=F32)
        gate = gate_rows[:, columns(head)].astype(F32)
        factor[head] = attn_gain[:, columns(head)] / (1.0 + jnp.exp(-gate))

    loads[2].wait()
    loads[3].wait()
    for head in range(head_count // 2):
        inside(head)
    kept.wait()
    arrive()
    mine = index // (size // head_count)
    carry_decay = jnp.exp(-rate_of(mine, (1, head_width)) * float(row_count))
    running = jnp.zeros(gathered.shape[1:], F32)
    for block in range(size):
        prior[block] = running.astype(BF16)
        if block + 1 < size:
            running = carry_decay * running + gathered[block].astype(F32)
    start2, arrive2, leave2 = exchange(prior, state, send_sems2, recv_sems2)
    start2()
    kept2 = pltpu.make_async_copy(prior.at[index], state.at[index], local_sems.at[1])
    kept2.start()
    for head in range(head_count // 2, head_count):
        inside(head)
    leave()
    kept2.wait()
    arrive2()
    for head in range(head_count):
        rate = rate_of(head, (1, head_width))
        parts = size // head_count
        held = state[head * parts : (head + 1) * parts].reshape(head_width, head_width)
        reached = jnp.dot(queries[:, columns(head)], held, preferred_element_type=F32)
        mixed = inner[head] + reached * jnp.exp(-rate * (positions + 1.0))
        mean_square = jnp.mean(mixed * mixed, axis=1, keepdims=True)
        normed = mixed * lax.rsqrt(mean_square + EPSILON)
        settled[:, columns(head)] = (normed * factor[head]).astype(BF16)
    leave2()


def place(index):
    return index // 8, (index // 2) % 4, index % 2


class Copies:
    def __init__(self, send_sems, recv_sems):
        self.send_sems, self.recv_sems = send_sems, recv_sems
        self.count, self.waiting = 0, []

    def start(self, source, target, device):
        copy = pltpu.make_async_remote_copy(
            src_ref=source,
            dst_ref=target,
            send_sem=self.send_sems.at[self.count],
            recv_sem=self.recv_sems.at[self.count],
            device_id=device,
            device_id_type=MESH,
        )
        copy.start()
        self.count += 1
        self.waiting.append(copy)
        return copy

    def finish(self):
        for copy in self.waiting:
            copy.wait_send()
        self.waiting = []


def layer_kernel(
    decay_exp, queries_hbm, keys_hbm, values_hbm, gates_hbm, attn_gain,
    out_proj, residual_hbm, norm_gain, routes, route_weights, w_gate, w_up, w_down, out,
    queries, key_rows, value_rows, gate_rows, update, gathered, prior, state, inner, factor,
    state_sems, state_sems2, state_sems3, state_sems4, span_sems,
    settled, residual, pick, fetch, shares,
    proj_w, proj, in0, comb0, hidden, squares, outbox, inbox, scale_out, scale_in, scales,
    rows, w_in, w_out, pre, act, in1, comb1, mid, in2, homebox, back,
    send_sems, recv_sems, local_sems,
):
    index, owner = lax.axis_index("ctx"), lax.axis_index("exp")
    z, x, core = place(index)
    part = rows

    def device(zz, xx):
        return (zz * 8 + xx * 2 + core, owner)

    def beside(at):
        return lax.rem(at + RING - 1, RING), lax.rem(at + 1, RING), lax.rem(at + 2, RING)

    x_left, x_right, x_far = beside(x)
    z_left, z_right, z_far = beside(z)
    y_left, y_right, y_far = beside(owner)
    partner = (index + 1 - 2 * core, owner)
    near = {
        "x": (x, x_left, x_right, device(z, x_left), device(z, x_right), x_far),
        "z": (z, z_left, z_right, device(z_left, x), device(z_right, x), z_far),
        "y": (owner, y_left, y_right, (index, y_left), (index, y_right), y_far),
    }
    column_peers = [lax.rem(owner + step, RING) for step in range(1, RING)]
    plane_peers = [
        device(lax.rem(z + dz, RING), lax.rem(x + dx, RING))
        for dz in range(RING)
        for dx in range(RING)
        if dz or dx
    ]
    barrier = pltpu.get_barrier_semaphore()
    size = gathered.shape[0]

    def greet(step, carry):
        other = lax.rem(index + step, size)
        pl.semaphore_signal(barrier, inc=1, device_id=(other, owner), device_id_type=MESH)
        return carry

    lax.fori_loop(1, size, greet, 0)
    for other in column_peers:
        pl.semaphore_signal(barrier, inc=1, device_id=(index, other), device_id_type=MESH)
    copies = Copies(send_sems, recv_sems)
    local_count = [0]

    def local(source, target):
        copy = pltpu.make_async_copy(source, target, local_sems.at[local_count[0]])
        local_count[0] += 1
        copy.start()
        return copy

    units = w_gate.shape[0]
    piece_width = 4 * WIDTH
    half = 2 * WIDTH
    first, second = ("x", "z"), ("z", "x")
    both = slice(None)

    def scatter(axis, view, land):
        me, left, right, to_left, to_right, far = near[axis]
        return (
            copies.start(view(0, far), land(0), to_left),
            copies.start(view(1, far), land(1), to_right),
            copies.start(view(0, right), land(2), to_right),
            copies.start(view(1, left), land(3), to_left),
        )

    def join(axis, view, land, stage, sent):
        me, left, right, to_left, to_right, far = near[axis]
        joined = []
        for sub, at, to in ((0, left, to_left), (1, right, to_right)):
            sent[sub].wait_recv()
            stage(sub)[...] = (
                land(sub)[...].astype(F32) + view(sub, at)[...].astype(F32)
            ).astype(BF16)
            joined.append(copies.start(stage(sub), land(4 + sub), to))
        return joined

    def scatter_direct(axis, view, land):
        me, left, right, to_left, to_right, far = near[axis]
        to_far = device(z, x_far) if axis == "x" else device(z_far, x)
        return (
            copies.start(view(0, far), land(4), to_far),
            copies.start(view(1, far), land(5), to_far),
            copies.start(view(0, right), land(2), to_right),
            copies.start(view(1, left), land(3), to_left),
            copies.start(view(0, left), land(0), to_left),
            copies.start(view(1, right), land(1), to_right),
        )

    def total_direct(axis, view, land, sent, sub):
        value = view(sub, near[axis][0])[...].astype(F32)
        for n, i in ((4 + sub, sub), (2 + sub, 2 + sub), (sub, 4 + sub)):
            sent[n].wait_recv()
            value = value + land(i)[...].astype(F32)
        return value

    def total(axis, view, land, sent, joined, sub):
        me = near[axis][0]
        sent[2 + sub].wait_recv()
        joined[sub].wait_recv()
        return (
            view(sub, me)[...].astype(F32)
            + land(2 + sub)[...].astype(F32)
            + land(4 + sub)[...].astype(F32)
        )

    def tables():
        group_rows = residual.shape[0]
        row_count = routes.shape[1]
        slot = lax.broadcasted_iota(jnp.int32, (SLOTS, row_count), 0)
        place_of = lax.broadcasted_iota(jnp.int32, (SLOTS, row_count), 1)
        expert = slot // 8
        chosen = jnp.where(expert % 2 == 0, routes[0:1, :], routes[1:2, :])
        picked = (chosen == expert) & (place_of // group_rows == owner)
        before = lax.broadcasted_iota(jnp.int32, (row_count, row_count), 0)
        after = lax.broadcasted_iota(jnp.int32, (row_count, row_count), 1)
        upto = jnp.where(before <= after, 1.0, 0.0).astype(BF16)
        rank = jnp.dot(
            jnp.where(picked, 1.0, 0.0).astype(BF16), upto, preferred_element_type=F32
        )
        chosen_slot = picked & (rank == (slot % 8 + 1).astype(F32))
        mine = lax.broadcasted_iota(jnp.int32, (group_rows, row_count), 1)
        mine = mine == owner * group_rows + lax.broadcasted_iota(
            jnp.int32, (group_rows, row_count), 0
        )
        mine_rows = jnp.where(mine, 1.0, 0.0).astype(BF16)

        def across(left, right):
            return lax.dot_general(
                left, right, (((1,), (1,)), ((), ())), preferred_element_type=F32
            ).astype(BF16)

        pick[...] = across(jnp.where(chosen_slot, 1.0, 0.0).astype(BF16), mine_rows)
        for column in range(2):
            table = chosen_slot & (expert % 2 == column)
            fetch[column] = across(mine_rows, jnp.where(table, 1.0, 0.0).astype(BF16))
            share = jnp.sum(
                jnp.where(mine, route_weights[column : column + 1, :], 0.0), axis=1, keepdims=True
            )
            shares[column] = jnp.broadcast_to(share, shares.shape[1:])

    loads = {}

    def load_proj(c):
        loads[c] = local(out_proj.at[:, pl.ds(c * piece_width, piece_width)], proj_w.at[c % 2])

    def project(c):
        loads[c].wait()
        for s in range(2):
            value = jnp.dot(
                settled[...],
                proj_w[c % 2, :, s * half : (s + 1) * half],
                preferred_element_type=F32,
            )
            proj[c, s] = value.astype(BF16).reshape(RING, -1, half)
        if c + 2 < CHUNKS:
            load_proj(c + 2)

    sent0, joined0, dispatched = {}, {}, {}

    def view0(c):
        return lambda sub, at: proj.at[c, sub, at]

    def land0(c):
        return lambda i: in0.at[c, i]

    def send_proj(c):
        sent0[c] = scatter("y", view0(c), land0(c))

    def join_proj(c):
        joined0[c] = join("y", view0(c), land0(c), lambda sub: comb0.at[c, sub], sent0[c])

    def exchange(box, landing):
        sent = [
            copies.start(box.at[other], landing.at[owner], (index, other))
            for other in column_peers
        ]
        return sent, local(box.at[owner], landing.at[owner])

    def arrive(exchanged):
        for copy in exchanged[0]:
            copy.wait_recv()
        exchanged[1].wait()

    def stacked(box, *place):
        return jnp.concatenate(
            [box[(*place[:1], e, *place[1:])].astype(F32) for e in range(RING)], axis=0
        )

    def dispatch(c):
        for s in range(2):
            columns = slice((c * 2 + s) * half, (c * 2 + s + 1) * half)
            value = total("y", view0(c), land0(c), sent0[c], joined0[c], s)
            value = value + residual[:, columns].astype(F32)
            hidden[c, s] = value
            square = value * value
            folded = square[:, :128]
            for lane in range(128, half, 128):
                folded = folded + square[:, lane : lane + 128]
            if c == 0 and s == 0:
                squares[...] = folded
            else:
                squares[...] = squares[...] + folded
            scaled = (value * norm_gain[:, columns]).astype(BF16)
            picked = jnp.dot(pick[...], scaled, preferred_element_type=F32)
            for e in range(RING):
                outbox[c, e, s] = picked[8 * e : 8 * e + 8].astype(BF16)
        dispatched[c] = exchange(outbox.at[c], inbox.at[c])

    def send_scales():
        mean_square = jnp.sum(squares[...], axis=1, keepdims=True) / (CHUNKS * piece_width)
        inverse = jnp.broadcast_to(lax.rsqrt(mean_square + EPSILON), squares.shape)
        picked = jnp.dot(
            pick[...].astype(F32),
            inverse,
            precision=lax.Precision.HIGHEST,
            preferred_element_type=F32,
        )
        for e in range(RING):
            scale_out[e] = picked[8 * e : 8 * e + 8]
        return exchange(scale_out, scale_in)

    def share_scales(exchanged):
        arrive(exchanged)
        mine = jnp.concatenate([scale_in[e] for e in range(RING)], axis=0)
        row = lax.broadcasted_iota(jnp.int32, (SLOTS, 128), 0)
        lane = lax.broadcasted_iota(jnp.int32, (SLOTS, 128), 1)
        line = jnp.sum(jnp.where(lane == x * SLOTS + row, mine, 0.0), axis=0, keepdims=True)
        scales[z, x] = jnp.broadcast_to(line, (8, 128))
        return [copies.start(scales.at[z, x], scales.at[z, x], other) for other in plane_peers]

    gather1, relay1, gather2, relay2 = {}, {}, {}, {}

    def line_of(c, h, stage, sub, at):
        axis = (first if stage == 1 else second)[h]
        if stage == 1:
            return rows.at[c, h, sub, at, x] if axis == "z" else rows.at[c, h, sub, z, at]
        return rows.at[c, h, sub, at] if axis == "z" else rows.at[c, h, sub, :, at]

    def spread(c, h, stage, started):
        me, left, right, to_left, to_right, far = near[(first if stage == 1 else second)[h]]
        mine = line_of(c, h, stage, both, me)
        sent = []
        if stage == 1 and c < HEAD_PIECES:
            to_far = device(z, x_far) if first[h] == "x" else device(z_far, x)
            sent = [copies.start(mine, mine, to_far)]
        started[c, h] = [copies.start(mine, mine, to_right), copies.start(mine, mine, to_left)]
        started[c, h] += sent

    def pass_on(c, h, stage, started, passed):
        me, left, right, to_left, to_right, far = near[(first if stage == 1 else second)[h]]
        from_left, from_right = started[c, h]
        from_left.wait_recv()
        source = line_of(c, h, stage, 0, left)
        one = copies.start(source, source, to_right)
        from_right.wait_recv()
        source = line_of(c, h, stage, 1, right)
        passed[c, h] = (one, copies.start(source, source, to_left))

    def gather_start(c):
        arrive(dispatched[c])
        for s in range(2):
            value = stacked(inbox, c, s).astype(BF16)
            for sub in range(2):
                rows[c, s, sub, z, x] = value[:, sub * WIDTH : (sub + 1) * WIDTH]
        for h in range(2):
            spread(c, h, 1, gather1)

    def gather_pass(c):
        if c < HEAD_PIECES:
            return
        for h in range(2):
            pass_on(c, h, 1, gather1, relay1)

    def gather_wide(c):
        for h in range(2):
            for copy in gather1[c, h] if c < HEAD_PIECES else relay1[c, h]:
                copy.wait_recv()
            spread(c, h, 2, gather2)

    def gather_wide_pass(c):
        for h in range(2):
            pass_on(c, h, 2, gather2, relay2)

    weights = []

    def load_weights():
        for source, target, base in (
            (w_gate, w_in, 0),
            (w_up, w_in, 2 * units),
            (w_down, w_out, 0),
        ):
            kept = local(source, target.at[pl.ds(base, units)])
            sent = copies.start(source, target.at[pl.ds(base + units, units)], partner)
            weights.append((kept, sent))

    def multiply_in(c):
        for h in range(2):
            for copy in relay2[c, h]:
                copy.wait_recv()
        if c == 0:
            for n in range(2):
                weights[n][0].wait()
                weights[n][1].wait_recv()

        def tile(t, carry):
            total = None
            for h in range(2):
                for sub in range(2):
                    block = rows[c, h, sub, pl.ds(2 * t, 2)].reshape(256, WIDTH)
                    column = ((c * 2 + h) * 2 + sub) * WIDTH
                    term = lax.dot_general(
                        w_in[:, column : column + WIDTH],
                        block,
                        (((1,), (1,)), ((), ())),
                        preferred_element_type=F32,
                    )
                    total = term if total is None else total + term
            pre[t] = total if c == 0 else pre[t] + total
            return carry

        lax.fori_loop(0, 2, tile, 0)

    def activate(t, carry):
        scale = jnp.concatenate(
            [jnp.sum(scales[2 * t + n], axis=0)[0:1] for n in range(2)], axis=1
        )
        gate = pre[t, : 2 * units] * scale
        up = pre[t, 2 * units :] * scale
        value = gate / (1.0 + jnp.exp(-gate)) * up
        act[pl.ds(pl.multiple_of(t * 256, 256), 256), :] = value.T.astype(BF16)
        return carry

    def multiply_out(c):
        def block(n, carry):
            column = pl.multiple_of((c * 4 + n) * WIDTH, WIDTH)
            value = jnp.dot(
                act[...], w_out[:, pl.ds(column, WIDTH)], preferred_element_type=F32
            )
            part[c, n // 2, n % 2] = value.astype(BF16).reshape(RING, RING, SLOTS, WIDTH)
            return carry

        for h in range(2):
            lax.fori_loop(2 * h, 2 * h + 2, block, 0)
            sent1[c, h] = scatter(second[h], view1(c, h), land1(c, h))

    sent1, joined1, sent2, returned = {}, {}, {}, {}

    def view1(c, h):
        if second[h] == "z":
            return lambda sub, at: part.at[c, h, sub, at]
        return lambda sub, at: part.at[c, h, sub, :, at]

    def view2(c, h):
        return lambda sub, at: mid.at[c, h, sub, at]

    def land1(c, h):
        return lambda i: in1.at[c, h, i]

    def land2(c, h):
        return lambda i: in2.at[c, h, i]

    def join_part(c):
        for h in range(2):
            joined1[c, h] = join(
                second[h], view1(c, h), land1(c, h), lambda sub: comb1.at[c, h, sub], sent1[c, h]
            )

    def send_mid(c):
        for h in range(2):
            for sub in range(2):
                mid[c, h, sub] = total(
                    second[h], view1(c, h), land1(c, h), sent1[c, h], joined1[c, h], sub
                ).astype(BF16)
            sent2[c, h] = scatter_direct(first[h], view2(c, h), land2(c, h))

    def send_home(c):
        for h in range(2):
            for sub in range(2):
                value = total_direct(first[h], view2(c, h), land2(c, h), sent2[c, h], sub)
                for g in range(RING):
                    homebox[c, g, h, :, sub * WIDTH : (sub + 1) * WIDTH] = value[
                        8 * g : 8 * g + 8
                    ].astype(BF16)
        returned[c] = exchange(homebox.at[c], back.at[c])

    def finish(c):
        arrive(returned[c])
        for s in range(2):
            columns = slice((c * 2 + s) * half, (c * 2 + s + 1) * half)
            value = hidden[c, s]
            produced = stacked(back, c, s).astype(BF16)
            for column in range(2):
                fetched = jnp.dot(fetch[column], produced, preferred_element_type=F32)
                value = value + shares[column, :, 0:1] * fetched
            out[:, columns] = value.astype(BF16)

    load_proj(0)
    load_proj(1)
    residual_load = local(residual_hbm, residual)
    tables()

    def meet():
        pl.semaphore_wait(barrier, size - 1 + len(column_peers))
        load_weights()

    attend(
        meet, decay_exp, queries_hbm, keys_hbm, values_hbm, gates_hbm, attn_gain, settled,
        queries, key_rows, value_rows, gate_rows, update, gathered, prior, state, inner, factor,
        state_sems, state_sems2, state_sems3, state_sems4, span_sems,
    )
    residual_load.wait()
    for step, c in (
        (project, 0), (send_proj, 0), (project, 1), (project, 2), (send_proj, 1),
        (join_proj, 0), (join_proj, 1), (project, 3), (send_proj, 2), (project, 4),
        (dispatch, 0), (dispatch, 1), (project, 5), (join_proj, 2), (send_proj, 3),
        (gather_start, 0), (gather_start, 1), (gather_pass, 0), (dispatch, 2), (gather_pass, 1),
        (send_proj, 4), (gather_wide, 0), (join_proj, 3), (gather_start, 2), (gather_wide, 1),
        (send_proj, 5), (join_proj, 4), (dispatch, 3), (gather_pass, 2), (join_proj, 5),
        (gather_wide_pass, 0), (gather_wide, 2), (gather_start, 3), (dispatch, 4),
        (gather_wide_pass, 1), (dispatch, 5),
    ):
        step(c)
    scale_step = send_scales()
    for step, c in (
        (gather_start, 4), (gather_pass, 3), (gather_wide_pass, 2), (gather_start, 5),
        (gather_pass, 4),
    ):
        step(c)
    shared = share_scales(scale_step)
    for step, c in (
        (gather_wide, 3), (multiply_in, 0), (gather_pass, 5), (gather_wide, 4),
        (gather_wide, 5), (multiply_in, 1), (gather_wide_pass, 3), (multiply_in, 2),
        (gather_wide_pass, 4), (gather_wide_pass, 5), (multiply_in, 3), (multiply_in, 4),
        (multiply_in, 5),
    ):
        step(c)
    for copy in shared:
        copy.wait_recv()
    lax.fori_loop(0, 2, activate, 0)
    weights[2][0].wait()
    weights[2][1].wait_recv()
    copies.finish()
    for step, c in (
        (multiply_out, 0), (multiply_out, 1), (multiply_out, 2),
        (multiply_out, 3), (join_part, 0), (multiply_out, 4), (multiply_out, 5),
        (join_part, 1), (join_part, 2),
        (join_part, 3), (join_part, 4), (join_part, 5), (send_mid, 0), (send_mid, 1),
        (send_mid, 2), (send_mid, 3), (send_mid, 4), (send_mid, 5), (send_home, 0),
        (send_home, 1), (send_home, 2), (send_home, 3), (send_home, 4), (send_home, 5),
        (finish, 0), (finish, 1), (finish, 2), (finish, 3), (finish, 4), (finish, 5),
    ):
        step(c)
    copies.finish()


def layer(
    queries, key_rows, value_rows, gate_rows, decay_exp, attn_gain, out_proj, residual,
    norm_gain, routes, route_weights, w_gate, w_up, w_down,
):
    units, width = w_gate.shape
    group_rows = residual.shape[0]
    row_count, depth = queries.shape
    head_count = decay_exp.shape[0]
    head_width = depth // head_count
    size = lax.axis_size("ctx")
    states = pltpu.VMEM((size, head_count * head_width // size, head_width), BF16)
    state_sems = pltpu.SemaphoreType.DMA((size - 1,))
    span = pltpu.VMEM(queries.shape, BF16)
    half = 2 * WIDTH
    count = CHUNKS * (6 + 3 + 3 + 16 + 24) + 3 + 15 + 3
    whole = (CHUNKS, 2, 2, RING, RING, SLOTS, WIDTH)
    box = (CHUNKS, RING, 2, SLOTS // RING, half)
    vmem = pl.BlockSpec(memory_space=pltpu.VMEM)
    anywhere = pl.BlockSpec(memory_space=pl.ANY)
    return pl.pallas_call(
        layer_kernel,
        out_shape=jax.ShapeDtypeStruct(residual.shape, BF16),
        in_specs=[pl.BlockSpec(memory_space=pltpu.SMEM)]
        + [anywhere] * 4
        + [vmem, anywhere, anywhere, vmem, vmem, vmem]
        + [anywhere] * 3,
        out_specs=vmem,
        scratch_shapes=[span] * 4
        + [states] * 4
        + [pltpu.VMEM((head_count, row_count, head_width), F32)] * 2
        + [state_sems] * 4
        + [
            pltpu.SemaphoreType.DMA((6,)),
            span,
            pltpu.VMEM(residual.shape, BF16),
            pltpu.VMEM((SLOTS, group_rows), BF16),
            pltpu.VMEM((2, group_rows, SLOTS), BF16),
            pltpu.VMEM((2, group_rows, 128), F32),
            pltpu.VMEM((2, depth, 4 * WIDTH), BF16),
            pltpu.VMEM((CHUNKS, 2, RING, group_rows, half), BF16),
            pltpu.VMEM((CHUNKS, 6, group_rows, half), BF16),
            pltpu.VMEM((CHUNKS, 2, group_rows, half), BF16),
            pltpu.VMEM((CHUNKS, 2, group_rows, half), F32),
            pltpu.VMEM((group_rows, 128), F32),
            pltpu.VMEM(box, BF16),
            pltpu.VMEM(box, BF16),
            pltpu.VMEM((RING, SLOTS // RING, 128), F32),
            pltpu.VMEM((RING, SLOTS // RING, 128), F32),
            pltpu.VMEM((RING, RING, 8, 128), F32),
            pltpu.VMEM(whole, BF16),
            pltpu.VMEM((4 * units, width), BF16),
            pltpu.VMEM((2 * units, width), BF16),
            pltpu.VMEM((2, 4 * units, 256), F32),
            pltpu.VMEM((RING * RING * SLOTS, 2 * units), BF16),
            pltpu.VMEM((CHUNKS, 2, 6, RING, SLOTS, WIDTH), BF16),
            pltpu.VMEM((CHUNKS, 2, 2, RING, SLOTS, WIDTH), BF16),
            pltpu.VMEM((CHUNKS, 2, 2, RING, SLOTS, WIDTH), BF16),
            pltpu.VMEM((CHUNKS, 2, 6, SLOTS, WIDTH), BF16),
            pltpu.VMEM(box, BF16),
            pltpu.VMEM(box, BF16),
            pltpu.SemaphoreType.DMA((count,)),
            pltpu.SemaphoreType.DMA((count,)),
            pltpu.SemaphoreType.DMA((3 * CHUNKS + 5,)),
        ],
        compiler_params=pltpu.CompilerParams(
            collective_id=2, has_side_effects=True, vmem_limit_bytes=64000 * 1024
        ),
        name="layer",
    )(
        decay_exp, queries, key_rows, value_rows, gate_rows, attn_gain.reshape(1, depth),
        out_proj, residual, norm_gain.reshape(1, width), routes.T, route_weights.T,
        w_gate, w_up, w_down,
    )


def body(
    queries,
    key_rows,
    value_rows,
    gate_rows,
    decay_exp,
    attn_gain,
    out_proj,
    residual,
    norm_gain,
    routes,
    route_weights,
    w_gate,
    w_up,
    w_down,
):
    return layer(
        queries,
        key_rows,
        value_rows,
        gate_rows,
        decay_exp,
        attn_gain,
        out_proj,
        residual,
        norm_gain,
        routes,
        route_weights,
        w_gate[0],
        w_up[0],
        w_down[0],
    )


def solution(mesh):
    in_specs = (
        P("ctx", "exp"),
        P("ctx", "exp"),
        P("ctx", "exp"),
        P("ctx", "exp"),
        P("exp"),
        P("exp"),
        P("exp", None),
        P(("ctx", "exp"), None),
        P(),
        P("ctx", None),
        P("ctx", None),
        P("exp", "ctx", None),
        P("exp", "ctx", None),
        P("exp", "ctx", None),
    )
    out_specs = P(("ctx", "exp"), None)
    return jax.shard_map(body, mesh=mesh, in_specs=in_specs, out_specs=out_specs, check_vma=False)
```
